32 devices in a mesh: groups: 2 (over y), dom: 4 (over z), sub: 2 (over x), field: 2 (over core).
Axes of the slice: x: 2, y: 2, z: 4, core: 2. Of those that a mesh axis runs over, the one named last changes fastest.
Arguments:
- background: float32 [3, 65536], P(None, ('groups', 'dom', 'sub')), parts along dimension 1, may hold values from -6 to 6
- obs_weight: float32 [65536], P(('groups', 'dom', 'sub')), parts along dimension 0, may hold values from 0.02 to 0.2
- connect: int32 [10, 32768], P(None, ('groups', 'dom', 'sub', 'field')), parts along dimension 1, may hold values from 0 to 5631, as said below
- live_blocks: int32 [32], P(('groups', 'dom', 'sub', 'field')), parts along dimension 0, may hold values from 2 to 8, as said below
- elem_scale: float32 [32768], P(('groups', 'dom', 'sub', 'field')), parts along dimension 0, may hold values from 0.5 to 2
- reg_weight: float32 [32768], P(('groups', 'dom', 'sub', 'field')), parts along dimension 0, may hold values from 0.2 to 2
- iterate: float32 [32768], P(('groups', 'dom', 'sub', 'field')), parts along dimension 0, may hold values from -6 to 6
- residual: float32 [32768], P(('groups', 'dom', 'sub', 'field')), parts along dimension 0, may hold values from -30 to 30
- direction: float32 [32768], P(('groups', 'dom', 'sub', 'field')), parts along dimension 0, may hold values from -30 to 30
- send_nodes: int32 [16, 3, 2, 256], P(('groups', 'dom', 'sub')), parts along dimension 0, may hold values from 0 to 4095, as said below
- send_count: int32 [16, 3, 2], P(('groups', 'dom', 'sub')), parts along dimension 0, may hold values from 0 to 256, as said below
- ref_stiff: float32 [30, 30], replicated, may hold values from -1.05 to 4.05, as said below
Outputs:
- iterate_next: float32 [32768], P(('groups', 'dom', 'sub', 'field')), parts along dimension 0
- residual_next: float32 [32768], P(('groups', 'dom', 'sub', 'field')), parts along dimension 0
- direction_next: float32 [32768], P(('groups', 'dom', 'sub', 'field')), parts along dimension 0
The draws below stay inside these ranges and needn't reach their ends.
There are 2 independent parts, one for each index of `groups`. The reference program is written for one: setup_inputs(seed, part) draws one part's arguments, and reference() takes and returns one part's arrays. A program takes and returns all parts, laid end to end along the dimension named above; an argument that names none is the same for every part. Nothing has to cross between parts.
Inputs may be any that keep to these rules, and one draw needn't show every extreme that they name: `send_nodes`: for every link the first send_count slots hold distinct owned nodes; later slots are padding. `send_count`: links go only to partitions of dom index d - 1, d or d + 1 and never to the sender itself or past the ends of dom; some link is full with 256 slots. `connect`: entries from 4096 on name ghost slots that are live slots of their owner's link. `live_blocks`: live blocks fill a device's slots from its first one; some device has 8. `ref_stiff`: Symmetric.
All inputs are finite; a program needn't handle non-finite values.
Results may differ from the reference program's by a relative error of at most 0.00005.
Values sent between devices are 32-bit elements; how exact they have to be, the bound alone decides.
No kernel may reach another device: no remote copies, remote signals or barrier semaphores. Data moves between devices by JAX's collectives and lax.ppermute only.
A program may use at most 64 MiB of HBM per device.

```python
import math
import jax
import jax.numpy as jnp
from jax import lax

NLOC = 4096
MAXB = 8
BLK = 128
LINK = 256
PARTITIONS = 8
CORES = 16
NODES = 32768
ELEMS = 16384
N_DOM = 4
N_SUB = 2
N_FIELD = 2


def interface_layout(key):
    salted = jax.random.fold_in(key, 17)
    linked_key, amount_key, chosen_key, start_key, stride_key = jax.random.split(salted, 5)
    partition = jnp.arange(PARTITIONS, dtype=jnp.int32)
    dom_index = partition // N_SUB
    sub_index = partition % N_SUB
    offset = jnp.arange(3, dtype=jnp.int32)
    target_sub = jnp.arange(N_SUB, dtype=jnp.int32)
    target_dom = dom_index[:, None, None] + offset[None, :, None] - 1
    itself = (offset[None, :, None] == 1) & (target_sub[None, None, :] == sub_index[:, None, None])
    exists = (target_dom >= 0) & (target_dom < N_DOM) & jnp.logical_not(itself)
    linked = jax.random.randint(linked_key, (PARTITIONS, 3, N_SUB), 0, 4) > 0
    amount = jax.random.randint(amount_key, (PARTITIONS, 3, N_SUB), LINK // 4, LINK + 1)
    counts = jnp.where(exists & linked, amount, 0)
    chosen = jax.random.randint(chosen_key, (), 0, PARTITIONS)
    counts = counts.at[chosen, 1, (chosen % N_SUB + 1) % N_SUB].set(LINK)
    starts = jax.random.randint(start_key, (PARTITIONS, 3, N_SUB, 1), 0, NLOC)
    strides = jax.random.randint(stride_key, (PARTITIONS, 3, N_SUB, 1), 1, NLOC // LINK + 1)
    sent_nodes = (starts + jnp.arange(LINK, dtype=jnp.int32)[None, None, None, :] * strides) % NLOC
    return (sent_nodes.astype(jnp.int32), counts.astype(jnp.int32))


def draw_send_nodes(key, part):
    sent_nodes, counts = interface_layout(key)
    return sent_nodes


def draw_send_count(key, part):
    sent_nodes, counts = interface_layout(key)
    return counts


def draw_connect(key, part):
    sent_nodes, counts = interface_layout(key)
    salted = jax.random.fold_in(key, 29)
    local_key, offset_key, source_key, position_key, choose_key = jax.random.split(salted, 5)
    layout_shape = (10, ELEMS)
    element = jnp.arange(ELEMS, dtype=jnp.int32)
    partition = element // (N_FIELD * MAXB * BLK)
    dom_index = partition // N_SUB
    sub_index = jnp.broadcast_to((partition % N_SUB)[None, :], layout_shape)
    local_pick = jax.random.randint(local_key, layout_shape, 0, NLOC)
    offset = jax.random.randint(offset_key, layout_shape, 0, 3)
    source_sub = jax.random.randint(source_key, layout_shape, 0, N_SUB)
    position = jax.random.randint(position_key, layout_shape, 0, LINK)
    wanted = jax.random.randint(choose_key, layout_shape, 0, 4) == 0
    raw_dom = dom_index[None, :] + offset - 1
    inside = (raw_dom >= 0) & (raw_dom < N_DOM)
    owner_part = jnp.clip(raw_dom, 0, N_DOM - 1) * N_SUB + source_sub
    usable = wanted & inside & (position < counts[owner_part, 2 - offset, sub_index])
    ghost_pick = NLOC + (offset * N_SUB + source_sub) * LINK + position
    return jnp.where(usable, ghost_pick, local_pick).astype(jnp.int32)


def draw_live_blocks(key, part):
    salted = jax.random.fold_in(key, 41)
    amount_key, chosen_key = jax.random.split(salted)
    counts = jax.random.randint(amount_key, (CORES,), MAXB // 4, MAXB // 2 + 1)
    chosen = jax.random.randint(chosen_key, (), 0, CORES)
    return counts.at[chosen].set(MAXB).astype(jnp.int32)


def rising_field(key, salt):
    salted = jax.random.fold_in(key, salt)
    scale_key, value_key = jax.random.split(salted)
    position = jnp.arange(ELEMS, dtype=jnp.float32) / ELEMS
    spread = jnp.exp(jax.random.uniform(scale_key, (ELEMS,), jnp.float32, 0.0, jnp.log(10.0)))
    scales = (1.0 + 2.0 * position) * spread / 4.0
    baseline = jnp.clip(jax.random.normal(value_key, (ELEMS,), jnp.float32), -4.0, 4.0)
    return (baseline * scales).astype(jnp.float32)


def draw_residual(key, part):
    return rising_field(key, 61)


def draw_direction(key, part):
    return rising_field(key, 67)


def draw_ref_stiff(key, part):
    salted = jax.random.fold_in(key, 53)
    diagonal_key, coupling_key = jax.random.split(salted)
    diagonal = jax.random.uniform(diagonal_key, (30,), jnp.float32, 1.5, 3.0)
    coupling = jnp.clip(jax.random.normal(coupling_key, (30, 30), jnp.float32), -3.0, 3.0)
    symmetric = 0.35 * (coupling + coupling.T) / 2.0
    identity = jnp.eye(30, dtype=jnp.float32)
    return (symmetric * (1.0 - identity) + identity * diagonal[None, :]).astype(jnp.float32)


def shard_levels(own_key, extent, cuts, smallest, high):
    def one(axis_at, shards_of):
        draws = jax.random.uniform(jax.random.fold_in(jax.random.fold_in(own_key, 6), axis_at), (shards_of,), jnp.float32, smallest / len(cuts), high / len(cuts))
        return jnp.repeat(jnp.exp(draws), extent[axis_at] // shards_of).reshape((-1,) + (1,) * (len(extent) - axis_at - 1))

    level = one(*cuts[0])
    for cut in cuts[1:]:
        level = level * one(*cut)
    return level


def bell_draw(own_key, extent, deviation, reach, pieces=(), kind=jnp.bfloat16):
    gain = shard_levels(own_key, extent, pieces, -0.22, 0.18) if pieces else 1.0
    drawn = jax.random.normal(own_key, extent, jnp.float32) * deviation * gain
    return jnp.minimum(jnp.maximum(drawn, -reach), reach).astype(kind)


def setup_inputs(seed: int = 0, part: int = 0) -> dict:
    key_list = jax.random.split(jax.random.key(seed), 13)
    own_keys = jax.random.split(jax.random.fold_in(key_list[12], part), 13)
    background = bell_draw(own_keys[0], (3, NODES), 1.0, 6.0, ((1, 8),), jnp.float32)
    obs_weight = jnp.clip(jnp.exp(math.log(0.2) - 2.3025851 * jax.random.uniform(own_keys[1], (NODES,), jnp.float32) ** shard_levels(own_keys[1], (NODES,), ((0, 8),), -0.2, 0.2)), 0.02, 0.2)
    connect = draw_connect(jax.random.fold_in(jax.random.fold_in(key_list[12], part), 71), part)
    live_blocks = draw_live_blocks(jax.random.fold_in(jax.random.fold_in(key_list[12], part), 71), part)
    elem_scale = jnp.clip(jnp.exp(math.log(2.0) - 1.3862944 * jax.random.uniform(own_keys[4], (ELEMS,), jnp.float32) ** shard_levels(own_keys[4], (ELEMS,), ((0, 16),), -0.2, 0.2)), 0.5, 2.0)
    reg_weight = jnp.clip(jnp.exp(math.log(2.0) - 2.3025851 * jax.random.uniform(own_keys[5], (ELEMS,), jnp.float32) ** shard_levels(own_keys[5], (ELEMS,), ((0, 16),), -0.2, 0.2)), 0.2, 2.0)
    iterate = bell_draw(own_keys[6], (ELEMS,), 1.0, 6.0, ((0, 16),), jnp.float32)
    residual = draw_residual(jax.random.fold_in(jax.random.fold_in(key_list[12], part), 71), part)
    direction = draw_direction(jax.random.fold_in(jax.random.fold_in(key_list[12], part), 71), part)
    send_nodes = draw_send_nodes(jax.random.fold_in(jax.random.fold_in(key_list[12], part), 71), part)
    send_count = draw_send_count(jax.random.fold_in(jax.random.fold_in(key_list[12], part), 71), part)
    ref_stiff = draw_ref_stiff(jax.random.fold_in(key_list[12], 71), part)
    return dict(background=background, obs_weight=obs_weight, connect=connect, live_blocks=live_blocks, elem_scale=elem_scale, reg_weight=reg_weight, iterate=iterate, residual=residual, direction=direction, send_nodes=send_nodes, send_count=send_count, ref_stiff=ref_stiff)


def global_nodes(connect, send_nodes, send_count):
    element_count = connect.shape[1]
    element = jnp.arange(element_count, dtype=jnp.int32)
    partition = element // (N_FIELD * MAXB * BLK)
    dom_index = partition // N_SUB
    sub_index = jnp.broadcast_to((partition % N_SUB)[None, :], connect.shape)
    ghosted = jnp.maximum(connect - NLOC, 0)
    offset = ghosted // (N_SUB * LINK)
    source_sub = (ghosted // LINK) % N_SUB
    position = ghosted % LINK
    raw_dom = dom_index[None, :] + offset - 1
    inside = (raw_dom >= 0) & (raw_dom < N_DOM)
    owner_part = (jnp.clip(raw_dom, 0, N_DOM - 1) * N_SUB + source_sub).astype(jnp.int32)
    slot_node = send_nodes[owner_part, 2 - offset, sub_index, position]
    remote = owner_part * NLOC + slot_node
    remote_ok = inside & (position < send_count[owner_part, 2 - offset, sub_index])
    local_ok = connect < NLOC
    node_map = jnp.where(local_ok, partition[None, :] * NLOC + connect, remote).astype(jnp.int32)
    valid_mask = (local_ok | remote_ok).astype(jnp.float32)
    return node_map, valid_mask


def reference(background, obs_weight, connect, live_blocks, elem_scale, reg_weight, iterate, residual, direction, send_nodes, send_count, ref_stiff):
    element_count = connect.shape[1]
    element = jnp.arange(element_count, dtype=jnp.int32)
    device = element // (MAXB * BLK)
    within = element % (MAXB * BLK)
    live_mask = (within < BLK * live_blocks[device]).astype(jnp.float32)
    search = live_mask * direction
    remain = live_mask * residual
    guess = live_mask * iterate
    node_map, valid_mask = global_nodes(connect, send_nodes, send_count)
    element_state = (background[:, node_map] * valid_mask[None]).reshape(30, element_count)
    coupled = (live_mask * elem_scale)[None, :] * jnp.dot(ref_stiff, element_state, precision=lax.Precision.HIGHEST)
    terms = (search[None, :] * coupled).reshape(3, 10, element_count) * valid_mask[None]
    assembled = jnp.zeros(background.shape, jnp.float32).at[:, node_map.reshape(-1)].add(terms.reshape(3, -1))
    weighted = obs_weight[None, :] * assembled
    pulled = weighted[:, node_map] * valid_mask[None]
    hess_search = jnp.sum(coupled.reshape(3, 10, element_count) * pulled, axis=(0, 1)) + reg_weight * search
    squared_before = jnp.sum(remain * remain)
    curvature_sum = jnp.sum(search * hess_search)
    step_length = squared_before / curvature_sum
    iterate_next = guess + step_length * search
    residual_next = remain - step_length * hess_search
    squared_after = jnp.sum(residual_next * residual_next)
    direction_next = residual_next + (squared_after / squared_before) * search
    return iterate_next, residual_next, direction_next
```

```python
import functools

import jax
import jax.numpy as jnp
from jax import lax
from jax.experimental import pallas as pl
from jax.experimental.pallas import tpu as pltpu
from jax.sharding import PartitionSpec as P

BLK = 128
LANES = 128
SUBS = 8
PARTS = 3

VMEM = pl.BlockSpec(memory_space=pltpu.VMEM)
SMEM = pl.BlockSpec(memory_space=pltpu.SMEM)


def up_to(count, step):
    return -(-count // step) * step


def lookup(table, rows, index, unroll):
    high = [i // LANES for i in index]
    low = [i % LANES for i in index]
    zero = jnp.zeros(index[0].shape, jnp.float32)

    def step(row, found):
        lines = [
            jnp.broadcast_to(table[c, pl.ds(row, 1), :], zero.shape) for c in range(3)
        ]
        out = []
        for i in range(len(index)):
            here = high[i] == row
            for c in range(3):
                value = jnp.take_along_axis(
                    lines[c], low[i], axis=1, mode="promise_in_bounds"
                )
                out.append(jnp.where(here, value, found[3 * i + c]))
        return tuple(out)

    found = lax.fori_loop(0, rows, step, (zero,) * (3 * len(index)), unroll=unroll)
    return [found[3 * i : 3 * i + 3] for i in range(len(index))]


def split_parts(value):
    pieces = []
    for _ in range(PARTS - 1):
        piece = value.astype(jnp.bfloat16).astype(jnp.float32)
        pieces.append(piece)
        value = value - piece
    pieces.append(value.astype(jnp.bfloat16).astype(jnp.float32))
    return pieces


def one_hot_pair(lines, index, rows, width):
    high = index // width
    low = index % width
    row = lax.broadcasted_iota(jnp.int32, (rows, LANES), 0)
    here = row == jnp.broadcast_to(high, (rows, LANES))
    left = jnp.concatenate(
        [jnp.where(here, jnp.broadcast_to(x, (rows, LANES)), 0.0) for x in lines], axis=0
    ).astype(jnp.bfloat16)
    spot = lax.broadcasted_iota(jnp.int32, (width, LANES), 0)
    right = jnp.where(
        spot == jnp.broadcast_to(low, (width, LANES)), 1.0, 0.0
    ).astype(jnp.bfloat16)
    return left, right


def contract(left, right):
    return lax.dot_general(
        left, right, (((1,), (1,)), ((), ())), preferred_element_type=jnp.float32
    )


def link_rows(sub_count, halves):
    return [
        (o, t, h, (o * sub_count + t) * halves + h)
        for o in range(3)
        for t in range(sub_count)
        for h in range(halves)
    ]


def load_links(nodes, index, sub_count, halves):
    for o, t, h, row in link_rows(sub_count, halves):
        index[row : row + 1, :] = nodes[0, o, t : t + 1, h * LANES : (h + 1) * LANES]
    used = 3 * sub_count * halves
    if index.shape[0] > used:
        index[used:, :] = jnp.zeros((index.shape[0] - used, LANES), jnp.int32)


def open_lanes(counts, o, t, h):
    lane = lax.broadcasted_iota(jnp.int32, (1, LANES), 1) + h * LANES
    return lane < counts[0, o, t]


def send_links(table, table_rows, counts, index, values, out, dom_count, sub_count, halves):
    tiles = index.shape[0] // SUBS
    found = lookup(
        table, table_rows, [index[i * SUBS : (i + 1) * SUBS, :] for i in range(tiles)], 4
    )
    for i in range(tiles):
        for c in range(3):
            values[c, i * SUBS : (i + 1) * SUBS, :] = found[i][c]

    def clear(p, carry):
        out[p] = jnp.zeros(out.shape[1:], jnp.float32)
        return carry

    lax.fori_loop(0, out.shape[0], clear, 0)
    dom = lax.axis_index("dom")
    for o in range(3):
        place = dom + o - 1

        @pl.when((place >= 0) & (place < dom_count))
        def _():
            for t in range(sub_count):
                for h in range(halves):
                    row = (o * sub_count + t) * halves + h
                    here = open_lanes(counts, o, t, h)
                    for c in range(3):
                        line = values[c, row : row + 1, :]
                        out[place * sub_count + t, c * halves + h : c * halves + h + 1, :] = (
                            jnp.where(here, line, 0.0)
                        )


def fill_ghosts(table, first, arrived, dom_count, sub_count, halves):
    dom = lax.axis_index("dom")
    for o in range(3):
        place = dom + o - 1
        inside = (place >= 0) & (place < dom_count)
        safe = jnp.clip(place, 0, dom_count - 1)
        for t in range(sub_count):
            chunk = arrived[safe * sub_count + t]
            chunk = jnp.where(inside, chunk, 0.0)
            for c in range(3):
                row = first + (o * sub_count + t) * halves
                table[c, row : row + halves, :] = chunk[c * halves : (c + 1) * halves, :]


def start_kernel(dims, counts, nodes, background, out, index, values, table):
    dom_count, sub_count, halves = dims
    rows = background.shape[1] // LANES
    for c in range(3):
        for r in range(rows):
            table[c, r : r + 1, :] = background[c : c + 1, r * LANES : (r + 1) * LANES]
    load_links(nodes, index, sub_count, halves)
    send_links(table, rows, counts, index, values, out, dom_count, sub_count, halves)


def forward_kernel(
    dims,
    live,
    stiff,
    background,
    arrived,
    connect,
    scale,
    direction,
    coupled,
    owned,
    outbound,
    table,
    index,
    state,
    pieces,
    left,
    right,
    total,
):
    dom_count, sub_count, halves = dims
    width = halves * LANES
    rows = background.shape[1] // LANES
    owned_high = background.shape[1] // width
    ghost_rows = 3 * sub_count * halves
    for c in range(3):
        for r in range(rows):
            table[c, r : r + 1, :] = background[c : c + 1, r * LANES : (r + 1) * LANES]
    fill_ghosts(table, rows, arrived, dom_count, sub_count, halves)
    for k in range(10):
        for b in range(SUBS):
            index[k, b : b + 1, :] = connect[k : k + 1, b * LANES : (b + 1) * LANES]
    found = lookup(table, rows + ghost_rows, [index[k] for k in range(10)], 2)
    for c in range(3):
        for k in range(10):
            state[c * 10 + k] = found[k][c]
    element = (
        lax.broadcasted_iota(jnp.int32, (SUBS, LANES), 0) * LANES
        + lax.broadcasted_iota(jnp.int32, (SUBS, LANES), 1)
    )
    mask = (element < BLK * live[0]).astype(jnp.float32)
    search = mask * direction[...]
    factor = mask * scale[...]
    for c in range(3):
        sums = [None] * 10
        for j in range(30):
            value = state[j]
            for k in range(10):
                term = stiff[c * 10 + k, j] * value
                sums[k] = term if j == 0 else sums[k] + term
        for k in range(10):
            result = factor * sums[k]
            coupled[c * 10 + k] = result
            for part, piece in enumerate(split_parts(search * result)):
                pieces[part * 3 + c, k] = piece

    high_rows = left.shape[0] // (3 * PARTS)

    def scatter(k, carry):
        for b in range(SUBS):
            lines = [pieces[q, k, b : b + 1, :] for q in range(3 * PARTS)]
            a, m = one_hot_pair(lines, index[k, b : b + 1, :], high_rows, width)
            left[:, b * LANES : (b + 1) * LANES] = a
            right[:, b * LANES : (b + 1) * LANES] = m
        total[...] += contract(left[...], right[...])
        return carry

    total[...] = jnp.zeros_like(total)
    lax.fori_loop(0, 10, scatter, 0)

    def summed(c, low, count):
        value = None
        for part in reversed(range(PARTS)):
            base = (part * 3 + c) * high_rows
            piece = total[base + low : base + low + count, :]
            value = piece if value is None else value + piece
        return value

    def clear(p, carry):
        outbound[p] = jnp.zeros(outbound.shape[1:], jnp.float32)
        return carry

    lax.fori_loop(0, outbound.shape[0], clear, 0)
    dom = lax.axis_index("dom")
    fields = outbound.shape[0] // (dom_count * sub_count)
    ghost = [None] * 3
    for c in range(3):
        owned[c] = summed(c, 0, owned_high)
        ghost[c] = summed(c, owned_high, 3 * sub_count)
    for o in range(3):
        place = dom + o - 1

        @pl.when((place >= 0) & (place < dom_count))
        def _():
            for t in range(sub_count):
                for c in range(3):
                    for h in range(halves):
                        line = ghost[c][
                            o * sub_count + t : o * sub_count + t + 1,
                            h * LANES : (h + 1) * LANES,
                        ]
                        spot = c * halves + h
                        for f in range(fields):
                            outbound[
                                (place * sub_count + t) * fields + f, spot : spot + 1, :
                            ] = line


def owner_kernel(
    dims,
    counts,
    nodes,
    mine,
    other,
    arrived,
    obs,
    weighted,
    out,
    index,
    values,
    left,
    right,
):
    dom_count, sub_count, halves = dims
    width = halves * LANES
    fields = arrived.shape[0] // (dom_count * sub_count)
    owned_high = mine.shape[1]
    load_links(nodes, index, sub_count, halves)
    dom = lax.axis_index("dom")
    for o in range(3):
        place = dom + o - 1
        inside = (place >= 0) & (place < dom_count)
        safe = jnp.clip(place, 0, dom_count - 1)
        for t in range(sub_count):
            chunk = arrived[(safe * sub_count + t) * fields]
            for f in range(1, fields):
                chunk = chunk + arrived[(safe * sub_count + t) * fields + f]
            chunk = jnp.where(inside, chunk, 0.0)
            split = split_parts(chunk)
            for h in range(halves):
                row = (o * sub_count + t) * halves + h
                here = open_lanes(counts, o, t, h)
                lines = [
                    jnp.where(here, split[part][c * halves + h : c * halves + h + 1, :], 0.0)
                    for part in range(PARTS)
                    for c in range(3)
                ]
                a, m = one_hot_pair(lines, index[row : row + 1, :], owned_high, width)
                left[:, row * LANES : (row + 1) * LANES] = a
                right[:, row * LANES : (row + 1) * LANES] = m
    total = contract(left[...], right[...])
    for c in range(3):
        value = mine[c] + other[c]
        landed = None
        for part in reversed(range(PARTS)):
            base = (part * 3 + c) * owned_high
            piece = total[base : base + owned_high, :]
            landed = piece if landed is None else landed + piece
        value = value + landed
        for h in range(halves):
            weight = obs[pl.ds(h, owned_high, stride=halves), :]
            weighted[c, pl.ds(h, owned_high, stride=halves), :] = (
                weight * value[:, h * LANES : (h + 1) * LANES]
            )
    rows = owned_high * halves
    send_links(weighted, rows, counts, index, values, out, dom_count, sub_count, halves)


def adjoint_kernel(
    dims,
    live,
    weighted,
    arrived,
    connect,
    coupled,
    direction,
    residual,
    reg,
    hess,
    sums,
    table,
    index,
):
    dom_count, sub_count, halves = dims
    rows = weighted.shape[1]
    table[:, 0:rows, :] = weighted[...]
    fill_ghosts(table, rows, arrived, dom_count, sub_count, halves)
    for k in range(10):
        for b in range(SUBS):
            index[k, b : b + 1, :] = connect[k : k + 1, b * LANES : (b + 1) * LANES]
    found = lookup(
        table, rows + 3 * sub_count * halves, [index[k] for k in range(10)], 2
    )
    element = (
        lax.broadcasted_iota(jnp.int32, (SUBS, LANES), 0) * LANES
        + lax.broadcasted_iota(jnp.int32, (SUBS, LANES), 1)
    )
    mask = (element < BLK * live[0]).astype(jnp.float32)
    search = mask * direction[...]
    remain = mask * residual[...]
    image = None
    for c in range(3):
        for k in range(10):
            term = coupled[c * 10 + k] * found[k][c]
            image = term if image is None else image + term
    image = image + reg[...] * search
    hess[...] = image
    for i, product in enumerate(
        (remain * remain, search * image, remain * image, image * image)
    ):
        line = jnp.sum(product, axis=0, keepdims=True)
        sums[:, i * LANES : (i + 1) * LANES] = jnp.broadcast_to(
            line, (sums.shape[0], LANES)
        )


def update_kernel(
    live, sums, hess, iterate, residual, direction, iterate_out, residual_out, direction_out
):
    totals = []
    for i in range(4):
        line = jnp.sum(sums[:, i * LANES : (i + 1) * LANES], axis=0, keepdims=True)
        line = jnp.sum(line, axis=1, keepdims=True)
        totals.append(jnp.broadcast_to(line, (SUBS, LANES)))
    squared_before, curvature_sum, cross_term, image_square = totals
    element = (
        lax.broadcasted_iota(jnp.int32, (SUBS, LANES), 0) * LANES
        + lax.broadcasted_iota(jnp.int32, (SUBS, LANES), 1)
    )
    mask = (element < BLK * live[0]).astype(jnp.float32)
    search = mask * direction[...]
    step_length = squared_before / curvature_sum
    squared_after = (
        squared_before
        - 2.0 * step_length * cross_term
        + step_length * step_length * image_square
    )
    residual_next = mask * residual[...] - step_length * hess[...]
    iterate_out[...] = mask * iterate[...] + step_length * search
    residual_out[...] = residual_next
    direction_out[...] = residual_next + squared_after / squared_before * search


def on_device(
    background,
    obs_weight,
    connect,
    live_blocks,
    elem_scale,
    reg_weight,
    iterate,
    residual,
    direction,
    send_nodes,
    send_count,
    ref_stiff,
):
    f32, i32, bf16 = jnp.float32, jnp.int32, jnp.bfloat16
    shape = jax.ShapeDtypeStruct
    dom_count = lax.axis_size("dom")
    sub_count = lax.axis_size("sub")
    field_count = lax.axis_size("field")
    owned_nodes = background.shape[1]
    link_slots = send_nodes.shape[3]
    halves = link_slots // LANES
    width = link_slots
    owned_high = owned_nodes // width
    owned_rows = owned_nodes // LANES
    ghost_rows = 3 * sub_count * halves
    table_rows = owned_rows + ghost_rows
    partitions = dom_count * sub_count
    devices = partitions * field_count
    chunk = up_to(3 * halves, SUBS)
    link_tiles = up_to(ghost_rows, SUBS)
    high_rows = up_to(owned_high + 3 * sub_count, SUBS)
    dims = (dom_count, sub_count, halves)
    tiled = lambda x: x.reshape(-1, LANES)
    scale, reg, guess, remain, search = map(
        tiled, (elem_scale, reg_weight, iterate, residual, direction)
    )
    obs = tiled(obs_weight)
    links = ("dom", "sub")
    cores = ("dom", "sub", "field")

    outbound = pl.pallas_call(
        functools.partial(start_kernel, dims),
        out_shape=shape((partitions, chunk, LANES), f32),
        in_specs=[SMEM, VMEM, VMEM],
        out_specs=VMEM,
        scratch_shapes=[
            pltpu.VMEM((link_tiles, LANES), i32),
            pltpu.VMEM((3, link_tiles, LANES), f32),
            pltpu.VMEM((3, owned_rows, LANES), f32),
        ],
    )(send_count, send_nodes, background)
    arrived = lax.all_to_all(outbound, links, 0, 0, tiled=True)

    coupled, owned, outbound = pl.pallas_call(
        functools.partial(forward_kernel, dims),
        out_shape=(
            shape((30, SUBS, LANES), f32),
            shape((3, owned_high, width), f32),
            shape((devices, chunk, LANES), f32),
        ),
        in_specs=[SMEM, SMEM] + [VMEM] * 5,
        out_specs=(VMEM,) * 3,
        scratch_shapes=[
            pltpu.VMEM((3, table_rows, LANES), f32),
            pltpu.VMEM((10, SUBS, LANES), i32),
            pltpu.VMEM((30, SUBS, LANES), f32),
            pltpu.VMEM((3 * PARTS, 10, SUBS, LANES), f32),
            pltpu.VMEM((3 * PARTS * high_rows, SUBS * LANES), bf16),
            pltpu.VMEM((width, SUBS * LANES), bf16),
            pltpu.VMEM((3 * PARTS * high_rows, width), f32),
        ],
    )(live_blocks, ref_stiff, background, arrived, connect, scale, search)
    swapped = lax.ppermute(
        owned, "field", [(i, (i + 1) % field_count) for i in range(field_count)]
    )
    arrived = lax.all_to_all(outbound, cores, 0, 0, tiled=True)

    weighted, outbound = pl.pallas_call(
        functools.partial(owner_kernel, dims),
        out_shape=(
            shape((3, owned_rows, LANES), f32),
            shape((partitions, chunk, LANES), f32),
        ),
        in_specs=[SMEM] + [VMEM] * 5,
        out_specs=(VMEM,) * 2,
        scratch_shapes=[
            pltpu.VMEM((link_tiles, LANES), i32),
            pltpu.VMEM((3, link_tiles, LANES), f32),
            pltpu.VMEM((3 * PARTS * owned_high, ghost_rows * LANES), bf16),
            pltpu.VMEM((width, ghost_rows * LANES), bf16),
        ],
    )(send_count, send_nodes, owned, swapped, arrived, obs)
    arrived = lax.all_to_all(outbound, links, 0, 0, tiled=True)

    hess, sums = pl.pallas_call(
        functools.partial(adjoint_kernel, dims),
        out_shape=(shape((SUBS, LANES), f32), shape((devices, 4 * LANES), f32)),
        in_specs=[SMEM] + [VMEM] * 7,
        out_specs=(VMEM,) * 2,
        scratch_shapes=[
            pltpu.VMEM((3, table_rows, LANES), f32),
            pltpu.VMEM((10, SUBS, LANES), i32),
        ],
    )(live_blocks, weighted, arrived, connect, coupled, search, remain, reg)
    sums = lax.all_to_all(sums, cores, 0, 0, tiled=True)

    results = pl.pallas_call(
        update_kernel,
        out_shape=(shape((SUBS, LANES), f32),) * 3,
        in_specs=[SMEM] + [VMEM] * 5,
        out_specs=(VMEM,) * 3,
    )(live_blocks, sums, hess, guess, remain, search)
    return tuple(x.reshape(-1) for x in results)


def solution(mesh):
    placed = (
        P(None, ("groups", "dom", "sub")),
        P(("groups", "dom", "sub")),
        P(None, ("groups", "dom", "sub", "field")),
        P(("groups", "dom", "sub", "field")),
        P(("groups", "dom", "sub", "field")),
        P(("groups", "dom", "sub", "field")),
        P(("groups", "dom", "sub", "field")),
        P(("groups", "dom", "sub", "field")),
        P(("groups", "dom", "sub", "field")),
        P(("groups", "dom", "sub"), None, None, None),
        P(("groups", "dom", "sub"), None, None),
        P(),
    )
    return jax.shard_map(
        on_device,
        mesh=mesh,
        in_specs=placed,
        out_specs=(
            P(("groups", "dom", "sub", "field")),
            P(("groups", "dom", "sub", "field")),
            P(("groups", "dom", "sub", "field")),
        ),
        check_vma=False,
    )
```

```python
import functools

import jax
import jax.numpy as jnp
from jax import lax
from jax.experimental import pallas as pl
from jax.experimental.pallas import tpu as pltpu
from jax.sharding import PartitionSpec as P

BLK = 128
LANES = 128
SUBS = 8
PARTS = 3
GROUP = 1
UNROLL = 10
SUMS = 4
LANE_BITS = 7

VMEM = pl.BlockSpec(memory_space=pltpu.VMEM)
SMEM = pl.BlockSpec(memory_space=pltpu.SMEM)
PARAMS = pltpu.CompilerParams(vmem_limit_bytes=16 * 2**20)


def up_to(count, step):
    return -(-count // step) * step


def lookup(table, rows, index, store):
    def pair(first, count):
        entries = [index[first + i] for i in range(count)]
        high = [lax.shift_right_logical(x, LANE_BITS) for x in entries]
        low = [x & (LANES - 1) for x in entries]
        found = [[None] * 3 for _ in entries]
        for row in range(rows):
            lines = [
                jnp.broadcast_to(table[c, row : row + 1, :], (SUBS, LANES))
                for c in range(3)
            ]
            for i in range(count):
                here = high[i] == row
                for c in range(3):
                    value = jnp.take_along_axis(
                        lines[c], low[i], axis=1, mode="promise_in_bounds"
                    )
                    found[i][c] = jnp.where(
                        here, value, 0.0 if row == 0 else found[i][c]
                    )
        for i in range(count):
            for c in range(3):
                store(first + i, c, found[i][c])

    def step(p, carry):
        pair(p * GROUP, GROUP)
        return carry

    tiles = index.shape[0]
    lax.fori_loop(0, tiles // GROUP, step, 0)
    if tiles % GROUP:
        pair(tiles // GROUP * GROUP, tiles % GROUP)


def split_parts(value):
    pieces = []
    for _ in range(PARTS - 1):
        piece = value.astype(jnp.bfloat16).astype(jnp.float32)
        pieces.append(piece)
        value = value - piece
    pieces.append(value.astype(jnp.bfloat16).astype(jnp.float32))
    return pieces


def spread(line, rows):
    return jnp.broadcast_to(line, (rows, LANES)).astype(jnp.bfloat16)


def row_numbers(rows):
    row = lax.broadcasted_iota(jnp.int32, (rows, LANES), 0)
    return row.astype(jnp.float32).astype(jnp.bfloat16)


def one_hot_pair(lines, index, owned_high, ghost_high, width):
    none = jnp.zeros((), jnp.bfloat16)
    unit = jnp.ones((), jnp.bfloat16)
    high = index // width
    low = (index & (width - 1)).astype(jnp.float32)
    here = row_numbers(owned_high) == spread(high.astype(jnp.float32), owned_high)
    blocks = [jnp.where(here, spread(x, owned_high), none) for x in lines]
    if ghost_high:
        row = lax.broadcasted_iota(jnp.int32, (ghost_high, LANES), 0) + owned_high
        here = row == jnp.broadcast_to(high, row.shape)
        rest = [jnp.where(here, jnp.broadcast_to(x, row.shape), 0.0) for x in lines]
        spare = up_to(len(lines) * ghost_high, 16) - len(lines) * ghost_high
        if spare:
            rest.append(jnp.zeros((spare, LANES), jnp.float32))
        blocks.append(jnp.concatenate(rest, axis=0).astype(jnp.bfloat16))
    left = jnp.concatenate(blocks, axis=0)
    right = jnp.where(row_numbers(width) == spread(low, width), unit, none)
    return left, right


def contract(left, right):
    return lax.dot_general(
        left, right, (((1,), (1,)), ((), ())), preferred_element_type=jnp.float32
    )


def link_rows(sub_count, halves):
    return [
        (o, t, h, (o * sub_count + t) * halves + h)
        for o in range(3)
        for t in range(sub_count)
        for h in range(halves)
    ]


def load_links(nodes, index, sub_count, halves):
    for o, t, h, row in link_rows(sub_count, halves):
        index[row // SUBS, row % SUBS : row % SUBS + 1, :] = nodes[
            0, o, t : t + 1, h * LANES : (h + 1) * LANES
        ]
    for row in range(3 * sub_count * halves, index.shape[0] * SUBS):
        index[row // SUBS, row % SUBS : row % SUBS + 1, :] = jnp.zeros((1, LANES), jnp.int32)


def open_lanes(counts, o, t, h):
    lane = lax.broadcasted_iota(jnp.int32, (1, LANES), 1) + h * LANES
    return lane < counts[0, t, o]


def send_links(table, table_rows, counts, index, values, out, dom_count, sub_count, halves):
    def store(tile, c, value):
        values[c, tile] = value

    lookup(table, table_rows, index, store)

    def clear(p, carry):
        out[p] = jnp.zeros(out.shape[1:], jnp.float32)
        return carry

    lax.fori_loop(0, out.shape[0], clear, 0)
    dom = lax.axis_index("dom")
    for o in range(3):
        place = dom + o - 1

        @pl.when((place >= 0) & (place < dom_count))
        def _():
            for t in range(sub_count):
                for h in range(halves):
                    row = (o * sub_count + t) * halves + h
                    here = open_lanes(counts, o, t, h)
                    for c in range(3):
                        line = values[c, row // SUBS, row % SUBS : row % SUBS + 1, :]
                        out[place * sub_count + t, c * halves + h : c * halves + h + 1, :] = (
                            jnp.where(here, line, 0.0)
                        )


def fill_ghosts(table, first, arrived, dom_count, sub_count, halves):
    dom = lax.axis_index("dom")
    for o in range(3):
        place = dom + o - 1
        inside = (place >= 0) & (place < dom_count)
        safe = jnp.clip(place, 0, dom_count - 1)
        for t in range(sub_count):
            chunk = arrived[safe * sub_count + t]
            chunk = jnp.where(inside, chunk, 0.0)
            for c in range(3):
                row = first + (o * sub_count + t) * halves
                table[c, row : row + halves, :] = chunk[c * halves : (c + 1) * halves, :]


def start_kernel(dims, counts, nodes, background, out, index, values, table):
    dom_count, sub_count, halves = dims
    rows = background.shape[1] // LANES
    for c in range(3):
        for r in range(rows):
            table[c, r : r + 1, :] = background[c : c + 1, r * LANES : (r + 1) * LANES]
    load_links(nodes, index, sub_count, halves)
    send_links(table, rows, counts, index, values, out, dom_count, sub_count, halves)


def forward_kernel(
    dims,
    live,
    stiff,
    background,
    arrived,
    connect,
    scale,
    direction,
    residual,
    iterate,
    reg,
    coupled,
    vectors,
    owned,
    outbound,
    table,
    index,
    state,
    pieces,
    total,
):
    dom_count, sub_count, halves = dims
    width = halves * LANES
    rows = background.shape[1] // LANES
    owned_high = background.shape[1] // width
    ghost_rows = 3 * sub_count * halves
    for c in range(3):
        for r in range(rows):
            table[c, r : r + 1, :] = background[c : c + 1, r * LANES : (r + 1) * LANES]
    fill_ghosts(table, rows, arrived, dom_count, sub_count, halves)
    for k in range(10):
        for b in range(SUBS):
            index[k, b : b + 1, :] = connect[k : k + 1, b * LANES : (b + 1) * LANES]

    def keep(k, c, value):
        state[c * 10 + k] = value

    lookup(table, rows + ghost_rows, index, keep)
    element = (
        lax.broadcasted_iota(jnp.int32, (SUBS, LANES), 0) * LANES
        + lax.broadcasted_iota(jnp.int32, (SUBS, LANES), 1)
    )
    mask = (element < BLK * live[0]).astype(jnp.float32)
    search = mask * direction[...]
    factor = mask * scale[...]
    vectors[0] = search
    vectors[1] = mask * residual[...]
    vectors[2] = mask * iterate[...]
    vectors[3] = reg[...] * search
    for c in range(3):
        sums = [None] * 10
        for j in range(30):
            value = state[j]
            for k in range(10):
                term = stiff[c * 10 + k, j] * value
                sums[k] = term if j == 0 else sums[k] + term
        for k in range(10):
            result = factor * sums[k]
            coupled[c * 10 + k] = result
            for part, piece in enumerate(split_parts(search * result)):
                pieces[part * 3 + c, k] = piece

    lines_count = 3 * PARTS
    ghost_high = up_to(3 * sub_count, SUBS)
    total[...] = jnp.zeros_like(total)

    def scatter(k, carry):
        pairs = [
            one_hot_pair(
                [pieces[q, k, b : b + 1, :] for q in range(lines_count)],
                index[k, b : b + 1, :],
                owned_high,
                ghost_high,
                width,
            )
            for b in range(SUBS)
        ]
        total[...] += contract(*[jnp.concatenate(x, axis=1) for x in zip(*pairs)])
        return carry

    lax.fori_loop(0, 10, scatter, 0, unroll=UNROLL)

    def summed(first, step, count):
        value = None
        for part in reversed(range(PARTS)):
            base = first + part * 3 * step
            piece = total[base : base + count, :]
            value = piece if value is None else value + piece
        return value

    def clear(p, carry):
        outbound[p] = jnp.zeros(outbound.shape[1:], jnp.float32)
        return carry

    lax.fori_loop(0, outbound.shape[0], clear, 0)
    dom = lax.axis_index("dom")
    fields = outbound.shape[0] // (dom_count * sub_count)
    ghost = [None] * 3
    for c in range(3):
        owned[c] = summed(c * owned_high, owned_high, owned_high)
        ghost[c] = summed(
            lines_count * owned_high + c * ghost_high, ghost_high, 3 * sub_count
        )
    for o in range(3):
        place = dom + o - 1

        @pl.when((place >= 0) & (place < dom_count))
        def _():
            for t in range(sub_count):
                for c in range(3):
                    for h in range(halves):
                        line = ghost[c][
                            o * sub_count + t : o * sub_count + t + 1,
                            h * LANES : (h + 1) * LANES,
                        ]
                        spot = c * halves + h
                        for f in range(fields):
                            outbound[
                                (place * sub_count + t) * fields + f, spot : spot + 1, :
                            ] = line


def owner_kernel(
    dims,
    counts,
    nodes,
    mine,
    other,
    arrived,
    obs,
    weighted,
    out,
    index,
    values,
):
    dom_count, sub_count, halves = dims
    width = halves * LANES
    fields = arrived.shape[0] // (dom_count * sub_count)
    owned_high = mine.shape[1]
    load_links(nodes, index, sub_count, halves)
    dom = lax.axis_index("dom")
    pairs = []
    for o in range(3):
        place = dom + o - 1
        inside = (place >= 0) & (place < dom_count)
        safe = jnp.clip(place, 0, dom_count - 1)
        for t in range(sub_count):
            chunk = arrived[(safe * sub_count + t) * fields]
            for f in range(1, fields):
                chunk = chunk + arrived[(safe * sub_count + t) * fields + f]
            chunk = jnp.where(inside, chunk, 0.0)
            split = split_parts(chunk)
            for h in range(halves):
                row = (o * sub_count + t) * halves + h
                here = open_lanes(counts, o, t, h)
                lines = [
                    jnp.where(here, split[part][c * halves + h : c * halves + h + 1, :], 0.0)
                    for part in range(PARTS)
                    for c in range(3)
                ]
                a, m = one_hot_pair(lines, index[row // SUBS, row % SUBS : row % SUBS + 1, :], owned_high, 0, width)
                pairs.append((a, m))
    total = contract(*[jnp.concatenate(x, axis=1) for x in zip(*pairs)])
    for c in range(3):
        value = mine[c] + other[c]
        landed = None
        for part in reversed(range(PARTS)):
            base = (part * 3 + c) * owned_high
            piece = total[base : base + owned_high, :]
            landed = piece if landed is None else landed + piece
        value = value + landed
        for h in range(halves):
            weight = obs[pl.ds(h, owned_high, stride=halves), :]
            weighted[c, pl.ds(h, owned_high, stride=halves), :] = (
                weight * value[:, h * LANES : (h + 1) * LANES]
            )
    rows = owned_high * halves
    send_links(weighted, rows, counts, index, values, out, dom_count, sub_count, halves)


def adjoint_kernel(
    dims, weighted, arrived, connect, coupled, vectors, hess, sums, table, index, pulled
):
    dom_count, sub_count, halves = dims
    rows = weighted.shape[1]
    table[:, 0:rows, :] = weighted[...]
    fill_ghosts(table, rows, arrived, dom_count, sub_count, halves)
    for k in range(10):
        for b in range(SUBS):
            index[k, b : b + 1, :] = connect[k : k + 1, b * LANES : (b + 1) * LANES]

    def keep(k, c, value):
        pulled[k, c] = value

    lookup(table, rows + 3 * sub_count * halves, index, keep)
    search, remain = vectors[0], vectors[1]
    image = None
    for c in range(3):
        for k in range(10):
            term = coupled[c * 10 + k] * pulled[k, c]
            image = term if image is None else image + term
    image = image + vectors[3]
    hess[...] = image
    for i, product in enumerate(
        (remain * remain, search * image, remain * image, image * image)
    ):
        line = jnp.sum(product, axis=0, keepdims=True)
        for p in range(sums.shape[0]):
            sums[p, i : i + 1, :] = line


def update_kernel(sums, hess, vectors, iterate_out, residual_out, direction_out):
    totals = []
    for i in range(4):
        line = sums[0, i : i + 1, :]
        for p in range(1, sums.shape[0]):
            line = line + sums[p, i : i + 1, :]
        line = jnp.sum(line, axis=1, keepdims=True)
        totals.append(jnp.broadcast_to(line, (SUBS, LANES)))
    squared_before, curvature_sum, cross_term, image_square = totals
    search, remain, guess = vectors[0], vectors[1], vectors[2]
    step_length = squared_before / curvature_sum
    squared_after = (
        squared_before
        - 2.0 * step_length * cross_term
        + step_length * step_length * image_square
    )
    residual_next = remain - step_length * hess[...]
    iterate_out[...] = guess + step_length * search
    residual_out[...] = residual_next
    direction_out[...] = residual_next + squared_after / squared_before * search


def on_device(
    background,
    obs_weight,
    connect,
    live_blocks,
    elem_scale,
    reg_weight,
    iterate,
    residual,
    direction,
    send_nodes,
    send_count,
    ref_stiff,
):
    f32, i32 = jnp.float32, jnp.int32
    shape = jax.ShapeDtypeStruct
    dom_count = lax.axis_size("dom")
    sub_count = lax.axis_size("sub")
    field_count = lax.axis_size("field")
    owned_nodes = background.shape[1]
    link_slots = send_nodes.shape[3]
    halves = link_slots // LANES
    width = link_slots
    owned_high = owned_nodes // width
    owned_rows = owned_nodes // LANES
    ghost_rows = 3 * sub_count * halves
    table_rows = owned_rows + ghost_rows
    partitions = dom_count * sub_count
    devices = partitions * field_count
    chunk = up_to(3 * halves, SUBS)
    link_tiles = up_to(ghost_rows, SUBS) // SUBS
    left_rows = 3 * PARTS * owned_high + up_to(3 * PARTS * up_to(3 * sub_count, SUBS), 16)
    dims = (dom_count, sub_count, halves)
    tiled = lambda x: x.reshape(-1, LANES)
    scale, reg, guess, remain, search = map(
        tiled, (elem_scale, reg_weight, iterate, residual, direction)
    )
    obs = tiled(obs_weight)
    counts = jnp.swapaxes(send_count, 1, 2)
    links = ("dom", "sub")
    cores = ("dom", "sub", "field")

    outbound = pl.pallas_call(
        functools.partial(start_kernel, dims),
        out_shape=shape((partitions, chunk, LANES), f32),
        in_specs=[SMEM, VMEM, VMEM],
        out_specs=VMEM,
        scratch_shapes=[
            pltpu.VMEM((link_tiles, SUBS, LANES), i32),
            pltpu.VMEM((3, link_tiles, SUBS, LANES), f32),
            pltpu.VMEM((3, owned_rows, LANES), f32),
        ],
    )(counts, send_nodes, background)
    arrived = lax.all_to_all(outbound, links, 0, 0, tiled=True)

    coupled, vectors, owned, outbound = pl.pallas_call(
        functools.partial(forward_kernel, dims),
        compiler_params=PARAMS,
        out_shape=(
            shape((30, SUBS, LANES), f32),
            shape((4, SUBS, LANES), f32),
            shape((3, owned_high, width), f32),
            shape((devices, chunk, LANES), f32),
        ),
        in_specs=[SMEM, SMEM] + [VMEM] * 8,
        out_specs=(VMEM,) * 4,
        scratch_shapes=[
            pltpu.VMEM((3, table_rows, LANES), f32),
            pltpu.VMEM((10, SUBS, LANES), i32),
            pltpu.VMEM((30, SUBS, LANES), f32),
            pltpu.VMEM((3 * PARTS, 10, SUBS, LANES), f32),
            pltpu.VMEM((left_rows, width), f32),
        ],
    )(
        live_blocks,
        ref_stiff,
        background,
        arrived,
        connect,
        scale,
        search,
        remain,
        guess,
        reg,
    )
    swapped = lax.ppermute(
        owned, "field", [(i, (i + 1) % field_count) for i in range(field_count)]
    )
    arrived = lax.all_to_all(outbound, cores, 0, 0, tiled=True)

    weighted, outbound = pl.pallas_call(
        functools.partial(owner_kernel, dims),
        compiler_params=PARAMS,
        out_shape=(
            shape((3, owned_rows, LANES), f32),
            shape((partitions, chunk, LANES), f32),
        ),
        in_specs=[SMEM] + [VMEM] * 5,
        out_specs=(VMEM,) * 2,
        scratch_shapes=[
            pltpu.VMEM((link_tiles, SUBS, LANES), i32),
            pltpu.VMEM((3, link_tiles, SUBS, LANES), f32),
        ],
    )(counts, send_nodes, owned, swapped, arrived, obs)
    arrived = lax.all_to_all(outbound, links, 0, 0, tiled=True)

    hess, sums = pl.pallas_call(
        functools.partial(adjoint_kernel, dims),
        compiler_params=PARAMS,
        out_shape=(shape((SUBS, LANES), f32), shape((devices, SUMS, LANES), f32)),
        in_specs=[VMEM] * 5,
        out_specs=(VMEM,) * 2,
        scratch_shapes=[
            pltpu.VMEM((3, table_rows, LANES), f32),
            pltpu.VMEM((10, SUBS, LANES), i32),
            pltpu.VMEM((10, 3, SUBS, LANES), f32),
        ],
    )(weighted, arrived, connect, coupled, vectors)
    sums = lax.all_to_all(sums, cores, 0, 0, tiled=True)

    results = pl.pallas_call(
        update_kernel,
        compiler_params=PARAMS,
        out_shape=(shape((SUBS, LANES), f32),) * 3,
        in_specs=[VMEM] * 3,
        out_specs=(VMEM,) * 3,
    )(sums, hess, vectors)
    return tuple(x.reshape(-1) for x in results)


def solution(mesh):
    placed = (
        P(None, ("groups", "dom", "sub")),
        P(("groups", "dom", "sub")),
        P(None, ("groups", "dom", "sub", "field")),
        P(("groups", "dom", "sub", "field")),
        P(("groups", "dom", "sub", "field")),
        P(("groups", "dom", "sub", "field")),
        P(("groups", "dom", "sub", "field")),
        P(("groups", "dom", "sub", "field")),
        P(("groups", "dom", "sub", "field")),
        P(("groups", "dom", "sub"), None, None, None),
        P(("groups", "dom", "sub"), None, None),
        P(),
    )
    return jax.shard_map(
        on_device,
        mesh=mesh,
        in_specs=placed,
        out_specs=(
            P(("groups", "dom", "sub", "field")),
            P(("groups", "dom", "sub", "field")),
            P(("groups", "dom", "sub", "field")),
        ),
        check_vma=False,
    )
```

```python
import functools

import jax
import jax.numpy as jnp
from jax import lax
from jax.experimental import pallas as pl
from jax.experimental.pallas import tpu as pltpu
from jax.sharding import PartitionSpec as P

BLK = 128
LANES = 128
SUBS = 8
PARTS = 3
UNROLL = 10
SUMS = 4
LANE_BITS = 7

VMEM = pl.BlockSpec(memory_space=pltpu.VMEM)
SMEM = pl.BlockSpec(memory_space=pltpu.SMEM)
PARAMS = pltpu.CompilerParams(vmem_limit_bytes=16 * 2**20)


def up_to(count, step):
    return -(-count // step) * step


def lookup(table, rows, index, store, begin=None, first=0, comps=3):
    def one(tile):
        entry = index[tile]
        high = lax.shift_right_logical(entry, LANE_BITS)
        low = entry & (LANES - 1)
        found = [0.0 if begin is None else begin(tile, c) for c in range(comps)]
        for row in range(rows):
            here = high == first + row
            for c in range(comps):
                line = jnp.broadcast_to(table[c, row : row + 1, :], (SUBS, LANES))
                value = jnp.take_along_axis(
                    line, low, axis=1, mode="promise_in_bounds"
                )
                found[c] = jnp.where(here, value, found[c])
        for c in range(comps):
            store(tile, c, found[c])

    def step(tile, carry):
        one(tile)
        return carry

    if index.shape[0] == 1:
        one(0)
    else:
        lax.fori_loop(0, index.shape[0], step, 0, unroll=min(2 if rows > 16 else 5, index.shape[0]))


def split_parts(value):
    pieces = []
    for _ in range(PARTS - 1):
        piece = value.astype(jnp.bfloat16).astype(jnp.float32)
        pieces.append(piece)
        value = value - piece
    pieces.append(value.astype(jnp.bfloat16).astype(jnp.float32))
    return pieces


def spread(line, rows):
    return jnp.broadcast_to(line, (rows, LANES)).astype(jnp.bfloat16)


def row_numbers(rows):
    row = lax.broadcasted_iota(jnp.int32, (rows, LANES), 0)
    return row.astype(jnp.float32).astype(jnp.bfloat16)


def one_hot_pair(lines, index, owned_high, ghost_high, width):
    none = jnp.zeros((), jnp.bfloat16)
    unit = jnp.ones((), jnp.bfloat16)
    high = index // width
    low = (index & (width - 1)).astype(jnp.float32)
    here = row_numbers(owned_high) == spread(high.astype(jnp.float32), owned_high)
    blocks = [jnp.where(here, spread(x, owned_high), none) for x in lines]
    if ghost_high:
        row = lax.broadcasted_iota(jnp.int32, (ghost_high, LANES), 0) + owned_high
        here = row == jnp.broadcast_to(high, row.shape)
        rest = [jnp.where(here, jnp.broadcast_to(x, row.shape), 0.0) for x in lines]
        spare = up_to(len(lines) * ghost_high, 16) - len(lines) * ghost_high
        if spare:
            rest.append(jnp.zeros((spare, LANES), jnp.float32))
        blocks.append(jnp.concatenate(rest, axis=0).astype(jnp.bfloat16))
    left = jnp.concatenate(blocks, axis=0)
    right = jnp.where(row_numbers(width) == spread(low, width), unit, none)
    return left, right


def contract(left, right):
    return lax.dot_general(
        left, right, (((1,), (1,)), ((), ())), preferred_element_type=jnp.float32
    )


def link_rows(sub_count, halves):
    return [
        (o, t, h, (o * sub_count + t) * halves + h)
        for o in range(3)
        for t in range(sub_count)
        for h in range(halves)
    ]


def load_links(nodes, index, sub_count, halves):
    for o, t, h, row in link_rows(sub_count, halves):
        index[row // SUBS, row % SUBS : row % SUBS + 1, :] = nodes[
            0, o, t : t + 1, h * LANES : (h + 1) * LANES
        ]
    for row in range(3 * sub_count * halves, index.shape[0] * SUBS):
        index[row // SUBS, row % SUBS : row % SUBS + 1, :] = jnp.zeros((1, LANES), jnp.int32)


def open_lanes(counts, o, t, h):
    lane = lax.broadcasted_iota(jnp.int32, (1, LANES), 1) + h * LANES
    return lane < counts[0, t, o]


def send_links(table, table_rows, counts, index, values, out, dom_count, sub_count, halves):
    def store(tile, c, value):
        values[c, tile] = value

    lookup(table, table_rows, index, store)

    def clear(p, carry):
        out[p] = jnp.zeros(out.shape[1:], jnp.float32)
        return carry

    lax.fori_loop(0, out.shape[0], clear, 0)
    dom = lax.axis_index("dom")
    for o in range(3):
        place = dom + o - 1

        @pl.when((place >= 0) & (place < dom_count))
        def _():
            for t in range(sub_count):
                for h in range(halves):
                    row = (o * sub_count + t) * halves + h
                    here = open_lanes(counts, o, t, h)
                    for c in range(3):
                        line = values[c, row // SUBS, row % SUBS : row % SUBS + 1, :]
                        out[place * sub_count + t, c * halves + h : c * halves + h + 1, :] = (
                            jnp.where(here, line, 0.0)
                        )


def fill_ghosts(table, first, arrived, dom_count, sub_count, halves):
    dom = lax.axis_index("dom")
    for o in range(3):
        place = dom + o - 1
        inside = (place >= 0) & (place < dom_count)
        safe = jnp.clip(place, 0, dom_count - 1)
        for t in range(sub_count):
            chunk = arrived[safe * sub_count + t]
            chunk = jnp.where(inside, chunk, 0.0)
            for c in range(3):
                row = first + (o * sub_count + t) * halves
                table[c, row : row + halves, :] = chunk[c * halves : (c + 1) * halves, :]


def start_kernel(dims, counts, nodes, background, out, index, values, table):
    dom_count, sub_count, halves = dims
    rows = background.shape[1] // LANES
    for c in range(3):
        for r in range(rows):
            table[c, r : r + 1, :] = background[c : c + 1, r * LANES : (r + 1) * LANES]
    load_links(nodes, index, sub_count, halves)
    send_links(table, rows, counts, index, values, out, dom_count, sub_count, halves)


def load_index(connect, index):
    for k in range(10):
        for b in range(SUBS):
            index[k, b : b + 1, :] = connect[k : k + 1, b * LANES : (b + 1) * LANES]


def couple(live, stiff, scale, others, state, coupled, vectors, pieces):
    element_vectors(live, scale, others, vectors)
    forward_terms(stiff, state, coupled, vectors, pieces)


def element_vectors(live, scale, others, vectors):
    direction, residual, iterate, reg = others
    element = (
        lax.broadcasted_iota(jnp.int32, (SUBS, LANES), 0) * LANES
        + lax.broadcasted_iota(jnp.int32, (SUBS, LANES), 1)
    )
    mask = (element < BLK * live[0]).astype(jnp.float32)
    search = mask * direction[...]
    vectors[0] = search
    vectors[1] = mask * residual[...]
    vectors[2] = mask * iterate[...]
    vectors[3] = reg[...] * search
    vectors[4] = mask * scale[...]


def forward_terms(stiff, state, coupled, vectors, pieces):
    search, factor = vectors[0], vectors[4]
    for c in range(3):
        sums = [None] * 10
        for j in range(30):
            value = state[j]
            for k in range(10):
                term = stiff[c * 10 + k, j] * value
                sums[k] = term if j == 0 else sums[k] + term
        for k in range(10):
            result = factor * sums[k]
            coupled[c * 10 + k] = result
            for part, piece in enumerate(split_parts(search * result)):
                pieces[part * 3 + c, k] = piece


def assemble(pieces, index, total, owned_high, ghost_high, width):
    total[...] = jnp.zeros_like(total)

    def scatter(k, carry):
        pairs = [
            one_hot_pair(
                [pieces[q, k, b : b + 1, :] for q in range(3 * PARTS)],
                index[k, b : b + 1, :],
                owned_high,
                ghost_high,
                width,
            )
            for b in range(SUBS)
        ]
        total[...] += contract(*[jnp.concatenate(x, axis=1) for x in zip(*pairs)])
        return carry

    lax.fori_loop(0, 10, scatter, 0, unroll=UNROLL)


def summed(total, first, step, count):
    value = None
    for part in reversed(range(PARTS)):
        base = first + part * 3 * step
        piece = total[base : base + count, :]
        value = piece if value is None else value + piece
    return value


def forward_kernel(
    dims,
    live,
    stiff,
    background,
    arrived,
    connect,
    scale,
    direction,
    residual,
    iterate,
    reg,
    coupled,
    vectors,
    owned,
    outbound,
    table,
    index,
    state,
    pieces,
    total,
):
    dom_count, sub_count, halves = dims
    width = halves * LANES
    rows = background.shape[1] // LANES
    owned_high = background.shape[1] // width
    ghost_rows = 3 * sub_count * halves
    for c in range(3):
        for r in range(rows):
            table[c, r : r + 1, :] = background[c : c + 1, r * LANES : (r + 1) * LANES]
    fill_ghosts(table, rows, arrived, dom_count, sub_count, halves)
    load_index(connect, index)

    def keep(k, c, value):
        state[c * 10 + k] = value

    lookup(table, rows + ghost_rows, index, keep)
    couple(
        live,
        stiff,
        scale,
        (direction, residual, iterate, reg),
        state,
        coupled,
        vectors,
        pieces,
    )
    ghost_high = up_to(3 * sub_count, SUBS)
    assemble(pieces, index, total, owned_high, ghost_high, width)

    def clear(p, carry):
        outbound[p] = jnp.zeros(outbound.shape[1:], jnp.float32)
        return carry

    lax.fori_loop(0, outbound.shape[0], clear, 0)
    dom = lax.axis_index("dom")
    fields = outbound.shape[0] // (dom_count * sub_count)
    ghost = [None] * 3
    for c in range(3):
        owned[c] = summed(total, c * owned_high, owned_high, owned_high)
        ghost[c] = summed(
            total, 3 * PARTS * owned_high + c * ghost_high, ghost_high, 3 * sub_count
        )
    for o in range(3):
        place = dom + o - 1

        @pl.when((place >= 0) & (place < dom_count))
        def _():
            for t in range(sub_count):
                for c in range(3):
                    for h in range(halves):
                        line = ghost[c][
                            o * sub_count + t : o * sub_count + t + 1,
                            h * LANES : (h + 1) * LANES,
                        ]
                        spot = c * halves + h
                        for f in range(fields):
                            outbound[
                                (place * sub_count + t) * fields + f, spot : spot + 1, :
                            ] = line


def owner_kernel(
    dims,
    counts,
    nodes,
    mine,
    other,
    arrived,
    obs,
    weighted,
    out,
    index,
    values,
):
    dom_count, sub_count, halves = dims
    width = halves * LANES
    fields = arrived.shape[0] // (dom_count * sub_count)
    owned_high = mine.shape[1]
    load_links(nodes, index, sub_count, halves)
    dom = lax.axis_index("dom")
    pairs = []
    for o in range(3):
        place = dom + o - 1
        inside = (place >= 0) & (place < dom_count)
        safe = jnp.clip(place, 0, dom_count - 1)
        for t in range(sub_count):
            chunk = arrived[(safe * sub_count + t) * fields]
            for f in range(1, fields):
                chunk = chunk + arrived[(safe * sub_count + t) * fields + f]
            chunk = jnp.where(inside, chunk, 0.0)
            split = split_parts(chunk)
            for h in range(halves):
                row = (o * sub_count + t) * halves + h
                here = open_lanes(counts, o, t, h)
                lines = [
                    jnp.where(here, split[part][c * halves + h : c * halves + h + 1, :], 0.0)
                    for part in range(PARTS)
                    for c in range(3)
                ]
                a, m = one_hot_pair(lines, index[row // SUBS, row % SUBS : row % SUBS + 1, :], owned_high, 0, width)
                pairs.append((a, m))
    total = contract(*[jnp.concatenate(x, axis=1) for x in zip(*pairs)])
    for c in range(3):
        value = mine[c] + other[c]
        landed = None
        for part in reversed(range(PARTS)):
            base = (part * 3 + c) * owned_high
            piece = total[base : base + owned_high, :]
            landed = piece if landed is None else landed + piece
        value = value + landed
        for h in range(halves):
            weight = obs[pl.ds(h, owned_high, stride=halves), :]
            weighted[c, pl.ds(h, owned_high, stride=halves), :] = (
                weight * value[:, h * LANES : (h + 1) * LANES]
            )
    rows = owned_high * halves
    send_links(weighted, rows, counts, index, values, out, dom_count, sub_count, halves)


def adjoint_kernel(
    dims, weighted, arrived, connect, coupled, vectors, hess, sums, table, index, pulled
):
    dom_count, sub_count, halves = dims
    rows = weighted.shape[1]
    table[:, 0:rows, :] = weighted[...]
    fill_ghosts(table, rows, arrived, dom_count, sub_count, halves)
    load_index(connect, index)

    def keep(k, c, value):
        pulled[k, c] = value

    lookup(table, rows + 3 * sub_count * halves, index, keep)
    search, remain = vectors[0], vectors[1]
    image = None
    for c in range(3):
        for k in range(10):
            term = coupled[c * 10 + k] * pulled[k, c]
            image = term if image is None else image + term
    image = image + vectors[3]
    hess[...] = image
    for i, product in enumerate(
        (remain * remain, search * image, remain * image, image * image)
    ):
        line = jnp.sum(product, axis=0, keepdims=True)
        for p in range(sums.shape[0]):
            sums[p, i : i + 1, :] = line


def update_kernel(sums, hess, vectors, iterate_out, residual_out, direction_out):
    totals = []
    for i in range(4):
        line = sums[0, i : i + 1, :]
        for p in range(1, sums.shape[0]):
            line = line + sums[p, i : i + 1, :]
        line = jnp.sum(line, axis=1, keepdims=True)
        totals.append(jnp.broadcast_to(line, (SUBS, LANES)))
    squared_before, curvature_sum, cross_term, image_square = totals
    search, remain, guess = vectors[0], vectors[1], vectors[2]
    step_length = squared_before / curvature_sum
    squared_after = (
        squared_before
        - 2.0 * step_length * cross_term
        + step_length * step_length * image_square
    )
    residual_next = remain - step_length * hess[...]
    iterate_out[...] = guess + step_length * search
    residual_out[...] = residual_next
    direction_out[...] = residual_next + squared_after / squared_before * search


def own_table(source, table):
    for c in range(3):
        for r in range(source.shape[1] // LANES):
            table[c, r : r + 1, :] = source[c : c + 1, r * LANES : (r + 1) * LANES]


def pair_start_kernel(counts, nodes, background, obs, pack, index, spots, table):
    sub = lax.axis_index("sub")
    step = jnp.where(lax.axis_index("field") == 0, 2, 0)
    own_table(background, table)
    table[3] = obs[...]
    row = lax.broadcasted_iota(jnp.int32, (SUBS, LANES), 0)
    slot = lax.broadcasted_iota(jnp.int32, (SUBS, LANES), 1) + row % 2 * LANES

    def line(o, k, h):
        zero = nodes[0, o, 0:1, h * LANES : (h + 1) * LANES]
        one = nodes[0, o, 1:2, h * LANES : (h + 1) * LANES]
        return jnp.where((sub ^ k) == 0, zero, one)

    def gate(links):
        limit = jnp.zeros((SUBS, LANES), jnp.int32)
        for i, (o, k) in enumerate(links):
            limit = jnp.where(row // 2 == i, counts[0, sub ^ k, o], limit)
        return slot < limit

    value_links = ((step, 0), (step, 1), (1, 1))
    weight_links = ((0, 1), (1, 1), (2, 1))
    for tile, links in ((index, value_links), (spots, weight_links)):
        tile[0] = jnp.zeros((SUBS, LANES), jnp.int32)
        for i, (o, k) in enumerate(links):
            for h in range(2):
                tile[0, 2 * i + h : 2 * i + h + 1, :] = line(o, k, h)
    value_gate = gate(value_links)

    def keep(tile, c, value):
        pack[c] = jnp.where(value_gate, value, 0.0)

    lookup(table, table.shape[1], index, keep)

    def keep_weight(tile, c, value):
        pack[5] = value

    lookup(table.at[3:4], table.shape[1], spots, keep_weight, comps=1)
    pack[3] = jnp.full((SUBS, LANES), -1.0, jnp.float32)
    pack[4] = jnp.full((SUBS, LANES), -1.0, jnp.float32)
    lane = lax.broadcasted_iota(jnp.int32, (1, LANES), 1)
    for o in range(3):
        for k in range(2):
            for h in range(2):
                at = (o * 2 + k) * 2 + h
                here = lane + h * LANES < counts[0, sub ^ k, o]
                pack[3 + at // SUBS, at % SUBS : at % SUBS + 1, :] = jnp.where(
                    here, line(o, k, h), -1
                ).astype(jnp.float32)


def pair_vector_kernel(
    live, pack, scale, direction, residual, iterate, reg, near, vectors
):
    element_vectors(live, scale, (direction, residual, iterate, reg), vectors)
    near[...] = pack[...]


def pair_join_kernel(near, sibling, out):
    row = lax.broadcasted_iota(jnp.int32, (SUBS, LANES), 0)
    for c in range(3):
        out[c] = jnp.where(row < 2, near[c], sibling[c])


def pair_ghosts(dom_count, mine, other, middle, table):
    dom = lax.axis_index("dom")
    first = lax.axis_index("field") == 0
    for c in range(3):
        below = jnp.where(first, mine[c], other[c])
        above = jnp.where(first, other[c], mine[c])
        below = jnp.where(dom > 0, below, 0.0)
        above = jnp.where(dom < dom_count - 1, above, 0.0)
        table[c, 0:4, :] = below[0:4, :]
        table[c, 4:6, :] = jnp.zeros((2, LANES), jnp.float32)
        table[c, 6:8, :] = middle[c, 4:6, :]
        table[c, 8:12, :] = above[0:4, :]


def pair_own_kernel(link_slots, background, connect, index, partial, table):
    sub = lax.axis_index("sub")
    own_table(background, table)
    load_index(connect, index)
    owned_nodes = background.shape[1]
    for k in range(10):
        entry = index[k]
        index[k] = jnp.where(entry >= owned_nodes, entry ^ (sub * link_slots), entry)

    def keep(k, c, value):
        partial[c * 10 + k] = value

    lookup(table, table.shape[1], index, keep)


def pair_forward_kernel(
    dom_count,
    stiff,
    partial,
    index,
    mine,
    other,
    middle,
    vectors,
    coupled,
    kept,
    sent,
    ghosts,
    state,
    pieces,
    total,
):
    owned_high = kept.shape[1] // 2 - SUBS // 2
    pair_ghosts(dom_count, mine, other, middle, ghosts)

    def begin(k, c):
        return partial[c * 10 + k]

    def keep(k, c, value):
        state[c * 10 + k] = value

    lookup(ghosts, 12, index, keep, begin, 2 * owned_high)
    forward_terms(stiff, state, coupled, vectors, pieces)
    width = 2 * LANES
    assemble(pieces, index, total, owned_high, SUBS, width)
    first = lax.axis_index("field") == 0
    base = 2 * owned_high
    for c in range(3):
        own = summed(total, c * owned_high, owned_high, owned_high)
        ghost = summed(total, 3 * PARTS * owned_high + c * SUBS, SUBS, SUBS)
        for h in range(2):
            half = own[:, h * LANES : (h + 1) * LANES]
            kept[c, h * owned_high : (h + 1) * owned_high, :] = half
            sent[c, h * owned_high : (h + 1) * owned_high, :] = half
            lines = ghost[:, h * LANES : (h + 1) * LANES]
            for k in range(2):
                below, above = lines[k : k + 1, :], lines[4 + k : 5 + k, :]
                at = base + 2 * k + h
                kept[c, at : at + 1, :] = jnp.where(first, above, below)
                sent[c, at : at + 1, :] = jnp.where(first, below, above)
            for out in (kept, sent):
                out[c, base + 4 + h : base + 5 + h, :] = lines[3:4, :]
                out[c, base + 6 + h : base + 7 + h, :] = jnp.zeros((1, LANES), jnp.float32)


def node_tile(links, tile):
    values = tile.astype(jnp.int32)
    return jnp.maximum(values, 0), values >= 0


def pair_sum_kernel(kept, came, pack, own, part, index, table):
    rows = own.shape[1]
    half = rows // 2
    for c in range(3):
        both = kept[c] + came[c]
        own[c] = both[:rows]
        for h in range(2):
            table[c, pl.ds(h, half, stride=2), :] = both[h * half : (h + 1) * half]
        part[3 + c] = both[rows:]
    index[0] = jnp.zeros((SUBS, LANES), jnp.int32)
    for o in range(3):
        for h in range(2):
            at = (o * 2 + 1) * 2 + h
            line = pack[3 + at // SUBS, at % SUBS : at % SUBS + 1, :].astype(jnp.int32)
            index[0, 2 * o + h : 2 * o + h + 1, :] = jnp.maximum(line, 0)

    def keep(tile, c, value):
        part[c] = value

    lookup(table, rows, index, keep)


def landing(nodes, lines, owned_high, width):
    pairs = []
    for (o, k), source in lines:
        for h in range(2):
            at = (o * 2 + k) * 2 + h
            entry = nodes[at // SUBS, at % SUBS : at % SUBS + 1, :].astype(jnp.int32)
            values = [source(c, h) for c in range(3)]
            split = [split_parts(v) for v in values]
            pairs.append(
                one_hot_pair(
                    [split[c][part] for part in range(PARTS) for c in range(3)],
                    entry,
                    owned_high,
                    0,
                    width,
                )
            )
    return contract(*[jnp.concatenate(x, axis=1) for x in zip(*pairs)])


def pair_owner_kernel(
    dom_count,
    own,
    part,
    mine,
    other,
    came,
    pack,
    sibling,
    obs,
    weighted,
    out,
    total,
    index,
    table,
):
    rows = own.shape[1]
    owned_high = rows // 2
    width = 2 * LANES
    dom = lax.axis_index("dom")
    first = lax.axis_index("field") == 0

    def pick(here, there, inside):
        def line(k):
            def get(c, h):
                at = 2 * k + h
                a, b = here(c)[at : at + 1, :], there(c)[at : at + 1, :]
                return jnp.where(inside, jnp.where(first, a, b), 0.0)

            return get

        return line

    mine_at, other_at = (lambda c: mine[c]), (lambda c: other[c])
    his_mine, his_other = (lambda c: came[6 + c]), (lambda c: came[9 + c])
    low, high = dom > 0, dom < dom_count - 1
    below = pick(mine_at, other_at, low)
    above = pick(other_at, mine_at, high)
    his_below = pick(his_mine, his_other, low)
    his_above = pick(his_other, his_mine, high)
    own_lines = (
        ((0, 0), below(0)),
        ((0, 1), his_below(1)),
        ((1, 1), lambda c, h: came[3 + c, 4 + h : 5 + h, :]),
        ((2, 0), above(0)),
        ((2, 1), his_above(1)),
    )
    his_lines = (
        ((0, 0), his_below(0)),
        ((0, 1), below(1)),
        ((1, 1), lambda c, h: part[3 + c, 4 + h : 5 + h, :]),
        ((2, 0), his_above(0)),
        ((2, 1), above(1)),
    )
    total[0] = landing(pack.at[3:5], own_lines, owned_high, width)
    total[1] = landing(sibling.at[3:5], his_lines, owned_high, width)
    for c in range(3):
        landed = summed(total.at[0], c * owned_high, owned_high, owned_high)
        his = summed(total.at[1], c * owned_high, owned_high, owned_high)
        for h in range(2):
            at = pl.ds(h, owned_high, stride=2)
            value = own[c, h * owned_high : (h + 1) * owned_high, :]
            value = obs[at, :] * (value + landed[:, h * LANES : (h + 1) * LANES])
            weighted[c, at, :] = value
            table[c, at, :] = value
            table[c, pl.ds(rows + h, owned_high, stride=2), :] = his[
                :, h * LANES : (h + 1) * LANES
            ]

    def node(tiles, o, k, h):
        at = (o * 2 + k) * 2 + h
        return tiles[3 + at // SUBS, at % SUBS : at % SUBS + 1, :].astype(jnp.int32)

    index[0] = jnp.full((SUBS, LANES), -1, jnp.int32)
    index[1] = jnp.zeros((SUBS, LANES), jnp.int32)
    shift = rows * LANES
    for h in range(2):
        line = jnp.where(first, node(pack, 2, 0, h), node(pack, 0, 0, h))
        index[0, h : h + 1, :] = line
        for at, line in (
            (2, jnp.where(first, node(sibling, 2, 1, h), node(sibling, 0, 1, h))),
            (4, node(sibling, 1, 1, h)),
        ):
            index[0, at + h : at + h + 1, :] = jnp.where(line < 0, line, line + shift)
    is_open = index[0] >= 0
    index[0] = jnp.maximum(index[0], 0)
    row = lax.broadcasted_iota(jnp.int32, (SUBS, LANES), 0)

    def lined_up(tile):
        lines = []
        for h in range(2):
            lines.append(jnp.where(first, tile[4 + h : 5 + h, :], tile[h : h + 1, :]))
        lines += [tile[2:3, :], tile[3:4, :]]
        blank = jnp.zeros((2, LANES), jnp.float32)
        return jnp.concatenate([blank] + lines + [blank], axis=0)

    weight = lined_up(sibling[5])

    def keep(tile, c, value):
        value = jnp.where(row < 2, value, weight * (lined_up(came[c]) + value))
        out[c] = jnp.where(is_open, value, 0.0)

    lookup(table, 2 * rows, index.at[0:1], keep)


def pair_near_kernel(weighted, index, coupled, near, pulled):
    def keep(k, c, value):
        pulled[c * 10 + k] = value

    lookup(weighted, weighted.shape[1], index, keep)
    image = None
    for i in range(30):
        term = coupled[i] * pulled[i]
        image = term if image is None else image + term
    near[...] = image


def write_sums(search, remain, image, sums):
    for i, product in enumerate(
        (remain * remain, search * image, remain * image, image * image)
    ):
        line = jnp.sum(product, axis=0, keepdims=True)
        for p in range(sums.shape[0]):
            sums[p, i : i + 1, :] = line


def pair_adjoint_kernel(
    dom_count,
    rows,
    near,
    mine,
    other,
    middle,
    index,
    coupled,
    vectors,
    hess,
    sums,
    ghosts,
    pulled,
):
    pair_ghosts(dom_count, mine, other, middle, ghosts)

    def keep(k, c, value):
        pulled[c * 10 + k] = value

    lookup(ghosts, 12, index, keep, first=rows)
    image = near[...]
    for i in range(30):
        image = image + coupled[i] * pulled[i]
    image = image + vectors[3]
    hess[...] = image
    write_sums(vectors[0], vectors[1], image, sums)


def pair_step(background, obs, connect, live_blocks, scale, others, nodes, counts, stiff):
    f32, i32 = jnp.float32, jnp.int32
    shape = jax.ShapeDtypeStruct
    dom_count = lax.axis_size("dom")
    owned_nodes = background.shape[1]
    link_slots = nodes.shape[3]
    rows = owned_nodes // LANES
    owned_high = owned_nodes // link_slots
    tile = (SUBS, LANES)
    swap = [(0, 1), (1, 0)]
    last = dom_count - 1
    ring = [(2 * d, 2 * d + 2) for d in range(last)]
    ring += [(2 * d + 3, 2 * d + 1) for d in range(last)]
    ring += [(2 * last, 2 * last + 1), (1, 0)]
    left_rows = 3 * PARTS * owned_high + up_to(3 * PARTS * SUBS, 16)

    def across(x):
        return lax.ppermute(x, "field", swap)

    def beside(x):
        return lax.ppermute(x, "sub", swap)

    def along(x):
        return lax.ppermute(x, ("dom", "field"), ring)

    def call(kernel, outs, scratch, smem, args, params=PARAMS):
        return pl.pallas_call(
            kernel,
            compiler_params=params,
            out_shape=outs,
            in_specs=[SMEM] * smem + [VMEM] * (len(args) - smem),
            out_specs=jax.tree.map(lambda x: VMEM, outs),
            scratch_shapes=scratch,
            cost_estimate=pl.CostEstimate(
                flops=2**20, bytes_accessed=2**16, transcendentals=0
            ),
        )(*args)

    pack = call(
        pair_start_kernel,
        shape((6,) + tile, f32),
        [
            pltpu.VMEM((1,) + tile, i32),
            pltpu.VMEM((1,) + tile, i32),
            pltpu.VMEM((4, rows, LANES), f32),
        ],
        1,
        (counts, nodes, background, obs),
        None,
    )
    sibling = beside(pack)
    pack, vectors = call(
        pair_vector_kernel,
        (shape((6,) + tile, f32), shape((5,) + tile, f32)),
        [],
        1,
        (live_blocks, pack, scale) + others,
    )
    mine = along(
        call(pair_join_kernel, shape((3,) + tile, f32), [], 0, (pack, sibling))
    )
    index, partial = call(
        functools.partial(pair_own_kernel, link_slots),
        (shape((10,) + tile, i32), shape((30,) + tile, f32)),
        [pltpu.VMEM((3, rows, LANES), f32)],
        0,
        (background, connect),
    )
    mine, partial = lax.optimization_barrier((mine, partial))
    other = across(mine)
    coupled, kept, sent = call(
        functools.partial(pair_forward_kernel, dom_count),
        (
            shape((30,) + tile, f32),
            shape((3, rows + SUBS, LANES), f32),
            shape((3, rows + SUBS, LANES), f32),
        ),
        [
            pltpu.VMEM((3, 16, LANES), f32),
            pltpu.VMEM((30,) + tile, f32),
            pltpu.VMEM((3 * PARTS, 10) + tile, f32),
            pltpu.VMEM((left_rows, link_slots), f32),
        ],
        1,
        (stiff, partial, index, mine, other, sibling, vectors),
    )
    came = across(sent)
    mine = along(kept[:, rows:] + came[:, rows:])
    own, part = call(
        pair_sum_kernel,
        (shape((3, rows, LANES), f32), shape((6,) + tile, f32)),
        [pltpu.VMEM((1,) + tile, i32), pltpu.VMEM((3, rows, LANES), f32)],
        0,
        (kept, came, pack),
    )
    mine, part = lax.optimization_barrier((mine, part))
    other = across(mine)
    came = beside(jnp.concatenate([part, mine, other], axis=0))
    weighted, outbound = call(
        functools.partial(pair_owner_kernel, dom_count),
        (shape((3, rows, LANES), f32), shape((3,) + tile, f32)),
        [
            pltpu.VMEM((2, 3 * PARTS * owned_high, link_slots), f32),
            pltpu.VMEM((2,) + tile, i32),
            pltpu.VMEM((3, 2 * rows, LANES), f32),
        ],
        0,
        (own, part, mine, other, came, pack, sibling, obs),
    )
    mine = along(outbound)
    near = call(
        pair_near_kernel,
        shape(tile, f32),
        [pltpu.VMEM((30,) + tile, f32)],
        0,
        (weighted, index, coupled),
    )
    mine, near = lax.optimization_barrier((mine, near))
    other = across(mine)
    hess, sums = call(
        functools.partial(pair_adjoint_kernel, dom_count, rows),
        (shape(tile, f32), shape((4 * dom_count, SUMS, LANES), f32)),
        [pltpu.VMEM((3, 16, LANES), f32), pltpu.VMEM((30,) + tile, f32)],
        0,
        (near, mine, other, outbound, index, coupled, vectors),
    )
    return hess, sums, vectors


def general_step(
    background, obs, connect, live_blocks, scale, others, send_nodes, counts, ref_stiff
):
    f32, i32 = jnp.float32, jnp.int32
    shape = jax.ShapeDtypeStruct
    dom_count = lax.axis_size("dom")
    sub_count = lax.axis_size("sub")
    field_count = lax.axis_size("field")
    owned_nodes = background.shape[1]
    link_slots = send_nodes.shape[3]
    halves = link_slots // LANES
    width = link_slots
    owned_high = owned_nodes // width
    owned_rows = owned_nodes // LANES
    ghost_rows = 3 * sub_count * halves
    table_rows = owned_rows + ghost_rows
    partitions = dom_count * sub_count
    devices = partitions * field_count
    chunk = up_to(3 * halves, SUBS)
    link_tiles = up_to(ghost_rows, SUBS) // SUBS
    left_rows = 3 * PARTS * owned_high + up_to(3 * PARTS * up_to(3 * sub_count, SUBS), 16)
    dims = (dom_count, sub_count, halves)
    links = ("dom", "sub")
    cores = ("dom", "sub", "field")

    outbound = pl.pallas_call(
        functools.partial(start_kernel, dims),
        out_shape=shape((partitions, chunk, LANES), f32),
        in_specs=[SMEM, VMEM, VMEM],
        out_specs=VMEM,
        scratch_shapes=[
            pltpu.VMEM((link_tiles, SUBS, LANES), i32),
            pltpu.VMEM((3, link_tiles, SUBS, LANES), f32),
            pltpu.VMEM((3, owned_rows, LANES), f32),
        ],
    )(counts, send_nodes, background)
    arrived = lax.all_to_all(outbound, links, 0, 0, tiled=True)

    coupled, vectors, owned, outbound = pl.pallas_call(
        functools.partial(forward_kernel, dims),
        compiler_params=PARAMS,
        out_shape=(
            shape((30, SUBS, LANES), f32),
            shape((5, SUBS, LANES), f32),
            shape((3, owned_high, width), f32),
            shape((devices, chunk, LANES), f32),
        ),
        in_specs=[SMEM, SMEM] + [VMEM] * 8,
        out_specs=(VMEM,) * 4,
        scratch_shapes=[
            pltpu.VMEM((3, table_rows, LANES), f32),
            pltpu.VMEM((10, SUBS, LANES), i32),
            pltpu.VMEM((30, SUBS, LANES), f32),
            pltpu.VMEM((3 * PARTS, 10, SUBS, LANES), f32),
            pltpu.VMEM((left_rows, width), f32),
        ],
    )(
        live_blocks,
        ref_stiff,
        background,
        arrived,
        connect,
        scale,
        *others,
    )
    swapped = lax.ppermute(
        owned, "field", [(i, (i + 1) % field_count) for i in range(field_count)]
    )
    arrived = lax.all_to_all(outbound, cores, 0, 0, tiled=True)

    weighted, outbound = pl.pallas_call(
        functools.partial(owner_kernel, dims),
        compiler_params=PARAMS,
        out_shape=(
            shape((3, owned_rows, LANES), f32),
            shape((partitions, chunk, LANES), f32),
        ),
        in_specs=[SMEM] + [VMEM] * 5,
        out_specs=(VMEM,) * 2,
        scratch_shapes=[
            pltpu.VMEM((link_tiles, SUBS, LANES), i32),
            pltpu.VMEM((3, link_tiles, SUBS, LANES), f32),
        ],
    )(counts, send_nodes, owned, swapped, arrived, obs)
    arrived = lax.all_to_all(outbound, links, 0, 0, tiled=True)

    hess, sums = pl.pallas_call(
        functools.partial(adjoint_kernel, dims),
        compiler_params=PARAMS,
        out_shape=(shape((SUBS, LANES), f32), shape((devices, SUMS, LANES), f32)),
        in_specs=[VMEM] * 5,
        out_specs=(VMEM,) * 2,
        scratch_shapes=[
            pltpu.VMEM((3, table_rows, LANES), f32),
            pltpu.VMEM((10, SUBS, LANES), i32),
            pltpu.VMEM((10, 3, SUBS, LANES), f32),
        ],
    )(weighted, arrived, connect, coupled, vectors)
    return hess, sums, vectors


def on_device(
    background,
    obs_weight,
    connect,
    live_blocks,
    elem_scale,
    reg_weight,
    iterate,
    residual,
    direction,
    send_nodes,
    send_count,
    ref_stiff,
):
    f32 = jnp.float32
    shape = jax.ShapeDtypeStruct
    tiled = lambda x: x.reshape(-1, LANES)
    scale, reg, guess, remain, search = map(
        tiled, (elem_scale, reg_weight, iterate, residual, direction)
    )
    obs = tiled(obs_weight)
    counts = jnp.swapaxes(send_count, 1, 2)
    two = lax.axis_size("sub") == 2 and lax.axis_size("field") == 2
    paired = two and send_nodes.shape[3] == 2 * LANES
    hess, sums, vectors = (pair_step if paired else general_step)(
        background,
        obs,
        connect,
        live_blocks,
        scale,
        (search, remain, guess, reg),
        send_nodes,
        counts,
        ref_stiff,
    )
    cores = ("dom", "sub", "field")
    sums = lax.all_to_all(sums, cores, 0, 0, tiled=True)

    results = pl.pallas_call(
        update_kernel,
        compiler_params=PARAMS,
        out_shape=(shape((SUBS, LANES), f32),) * 3,
        in_specs=[VMEM] * 3,
        out_specs=(VMEM,) * 3,
    )(sums, hess, vectors)
    return tuple(x.reshape(-1) for x in results)


def solution(mesh):
    placed = (
        P(None, ("groups", "dom", "sub")),
        P(("groups", "dom", "sub")),
        P(None, ("groups", "dom", "sub", "field")),
        P(("groups", "dom", "sub", "field")),
        P(("groups", "dom", "sub", "field")),
        P(("groups", "dom", "sub", "field")),
        P(("groups", "dom", "sub", "field")),
        P(("groups", "dom", "sub", "field")),
        P(("groups", "dom", "sub", "field")),
        P(("groups", "dom", "sub"), None, None, None),
        P(("groups", "dom", "sub"), None, None),
        P(),
    )
    return jax.shard_map(
        on_device,
        mesh=mesh,
        in_specs=placed,
        out_specs=(
            P(("groups", "dom", "sub", "field")),
            P(("groups", "dom", "sub", "field")),
            P(("groups", "dom", "sub", "field")),
        ),
        check_vma=False,
    )
```

```python
import functools

import jax
import jax.numpy as jnp
from jax import lax
from jax.experimental import pallas as pl
from jax.experimental.pallas import tpu as pltpu
from jax.sharding import PartitionSpec as P

BLK = 128
LANES = 128
SUBS = 8
PARTS = 2
UNROLL = 10
SUMS = 4
LANE_BITS = 7

VMEM = pl.BlockSpec(memory_space=pltpu.VMEM)
SMEM = pl.BlockSpec(memory_space=pltpu.SMEM)
PARAMS = pltpu.CompilerParams(vmem_limit_bytes=16 * 2**20)


def up_to(count, step):
    return -(-count // step) * step


def lookup(table, rows, index, store, begin=None, first=0, comps=3):
    def one(tile):
        entry = index[tile]
        high = lax.shift_right_logical(entry, LANE_BITS)
        low = entry & (LANES - 1)
        found = [0.0 if begin is None else begin(tile, c) for c in range(comps)]
        for row in range(rows):
            here = high == first + row
            for c in range(comps):
                line = jnp.broadcast_to(table[c, row : row + 1, :], (SUBS, LANES))
                value = jnp.take_along_axis(
                    line, low, axis=1, mode="promise_in_bounds"
                )
                found[c] = jnp.where(here, value, found[c])
        for c in range(comps):
            store(tile, c, found[c])

    def step(tile, carry):
        one(tile)
        return carry

    if index.shape[0] == 1:
        one(0)
    else:
        lax.fori_loop(0, index.shape[0], step, 0, unroll=min(2 if rows > 16 else 5, index.shape[0]))


def split_parts(value, count=PARTS):
    pieces = []
    for _ in range(count - 1):
        piece = value.astype(jnp.bfloat16).astype(jnp.float32)
        pieces.append(piece)
        value = value - piece
    pieces.append(value.astype(jnp.bfloat16).astype(jnp.float32))
    return pieces


def spread(line, rows):
    return jnp.broadcast_to(line, (rows, LANES)).astype(jnp.bfloat16)


def row_numbers(rows):
    row = lax.broadcasted_iota(jnp.int32, (rows, LANES), 0)
    return row.astype(jnp.float32).astype(jnp.bfloat16)


def one_hot_pair(lines, index, owned_high, ghost_high, width):
    none = jnp.zeros((), jnp.bfloat16)
    unit = jnp.ones((), jnp.bfloat16)
    high = index // width
    low = (index & (width - 1)).astype(jnp.float32)
    here = row_numbers(owned_high) == spread(high.astype(jnp.float32), owned_high)
    blocks = [jnp.where(here, spread(x, owned_high), none) for x in lines]
    if ghost_high:
        row = lax.broadcasted_iota(jnp.int32, (ghost_high, LANES), 0) + owned_high
        here = row == jnp.broadcast_to(high, row.shape)
        rest = [jnp.where(here, jnp.broadcast_to(x, row.shape), 0.0) for x in lines]
        spare = up_to(len(lines) * ghost_high, 16) - len(lines) * ghost_high
        if spare:
            rest.append(jnp.zeros((spare, LANES), jnp.float32))
        blocks.append(jnp.concatenate(rest, axis=0).astype(jnp.bfloat16))
    left = jnp.concatenate(blocks, axis=0)
    right = jnp.where(row_numbers(width) == spread(low, width), unit, none)
    return left, right


def contract(left, right):
    return lax.dot_general(
        left, right, (((1,), (1,)), ((), ())), preferred_element_type=jnp.float32
    )


def link_rows(sub_count, halves):
    return [
        (o, t, h, (o * sub_count + t) * halves + h)
        for o in range(3)
        for t in range(sub_count)
        for h in range(halves)
    ]


def load_links(nodes, index, sub_count, halves):
    for o, t, h, row in link_rows(sub_count, halves):
        index[row // SUBS, row % SUBS : row % SUBS + 1, :] = nodes[
            0, o, t : t + 1, h * LANES : (h + 1) * LANES
        ]
    for row in range(3 * sub_count * halves, index.shape[0] * SUBS):
        index[row // SUBS, row % SUBS : row % SUBS + 1, :] = jnp.zeros((1, LANES), jnp.int32)


def open_lanes(counts, o, t, h):
    lane = lax.broadcasted_iota(jnp.int32, (1, LANES), 1) + h * LANES
    return lane < counts[0, t, o]


def send_links(table, table_rows, counts, index, values, out, dom_count, sub_count, halves):
    def store(tile, c, value):
        values[c, tile] = value

    lookup(table, table_rows, index, store)

    def clear(p, carry):
        out[p] = jnp.zeros(out.shape[1:], jnp.float32)
        return carry

    lax.fori_loop(0, out.shape[0], clear, 0)
    dom = lax.axis_index("dom")
    for o in range(3):
        place = dom + o - 1

        @pl.when((place >= 0) & (place < dom_count))
        def _():
            for t in range(sub_count):
                for h in range(halves):
                    row = (o * sub_count + t) * halves + h
                    here = open_lanes(counts, o, t, h)
                    for c in range(3):
                        line = values[c, row // SUBS, row % SUBS : row % SUBS + 1, :]
                        out[place * sub_count + t, c * halves + h : c * halves + h + 1, :] = (
                            jnp.where(here, line, 0.0)
                        )


def fill_ghosts(table, first, arrived, dom_count, sub_count, halves):
    dom = lax.axis_index("dom")
    for o in range(3):
        place = dom + o - 1
        inside = (place >= 0) & (place < dom_count)
        safe = jnp.clip(place, 0, dom_count - 1)
        for t in range(sub_count):
            chunk = arrived[safe * sub_count + t]
            chunk = jnp.where(inside, chunk, 0.0)
            for c in range(3):
                row = first + (o * sub_count + t) * halves
                table[c, row : row + halves, :] = chunk[c * halves : (c + 1) * halves, :]


def start_kernel(dims, counts, nodes, background, out, index, values, table):
    dom_count, sub_count, halves = dims
    rows = background.shape[1] // LANES
    for c in range(3):
        for r in range(rows):
            table[c, r : r + 1, :] = background[c : c + 1, r * LANES : (r + 1) * LANES]
    load_links(nodes, index, sub_count, halves)
    send_links(table, rows, counts, index, values, out, dom_count, sub_count, halves)


def load_index(connect, index):
    for k in range(10):
        for b in range(SUBS):
            index[k, b : b + 1, :] = connect[k : k + 1, b * LANES : (b + 1) * LANES]


def couple(live, stiff, scale, others, state, coupled, vectors, pieces):
    element_vectors(live, scale, others, vectors)
    forward_terms(stiff, state, coupled, vectors, pieces)


def live_mask(blocks):
    element = (
        lax.broadcasted_iota(jnp.int32, (SUBS, LANES), 0) * LANES
        + lax.broadcasted_iota(jnp.int32, (SUBS, LANES), 1)
    )
    return (element < BLK * blocks).astype(jnp.float32)


def element_vectors(live, scale, others, vectors):
    direction, residual, iterate, reg = others
    mask = live_mask(live[0])
    search = mask * direction[...]
    vectors[0] = search
    vectors[1] = mask * residual[...]
    vectors[2] = mask * iterate[...]
    vectors[3] = reg[...] * search
    vectors[4] = mask * scale[...]


def forward_terms(stiff, state, coupled, vectors, pieces):
    search, factor = vectors[0], vectors[4]
    for c in range(3):
        sums = [None] * 10
        for j in range(30):
            value = state[j]
            for k in range(10):
                term = stiff[c * 10 + k, j] * value
                sums[k] = term if j == 0 else sums[k] + term
        for k in range(10):
            result = factor * sums[k]
            coupled[c * 10 + k] = result
            for part, piece in enumerate(split_parts(search * result)):
                pieces[part * 3 + c, k] = piece


def assemble(pieces, index, total, owned_high, ghost_high, width):
    total[...] = jnp.zeros_like(total)

    def scatter(k, carry):
        pairs = [
            one_hot_pair(
                [pieces[q, k, b : b + 1, :] for q in range(3 * PARTS)],
                index[k, b : b + 1, :],
                owned_high,
                ghost_high,
                width,
            )
            for b in range(SUBS)
        ]
        total[...] += contract(*[jnp.concatenate(x, axis=1) for x in zip(*pairs)])
        return carry

    lax.fori_loop(0, 10, scatter, 0, unroll=UNROLL)


def summed(total, first, step, count):
    value = None
    for part in reversed(range(PARTS)):
        base = first + part * 3 * step
        piece = total[base : base + count, :]
        value = piece if value is None else value + piece
    return value


def forward_kernel(
    dims,
    live,
    stiff,
    background,
    arrived,
    connect,
    scale,
    direction,
    residual,
    iterate,
    reg,
    coupled,
    vectors,
    owned,
    outbound,
    table,
    index,
    state,
    pieces,
    total,
):
    dom_count, sub_count, halves = dims
    width = halves * LANES
    rows = background.shape[1] // LANES
    owned_high = background.shape[1] // width
    ghost_rows = 3 * sub_count * halves
    for c in range(3):
        for r in range(rows):
            table[c, r : r + 1, :] = background[c : c + 1, r * LANES : (r + 1) * LANES]
    fill_ghosts(table, rows, arrived, dom_count, sub_count, halves)
    load_index(connect, index)

    def keep(k, c, value):
        state[c * 10 + k] = value

    lookup(table, rows + ghost_rows, index, keep)
    couple(
        live,
        stiff,
        scale,
        (direction, residual, iterate, reg),
        state,
        coupled,
        vectors,
        pieces,
    )
    ghost_high = up_to(3 * sub_count, SUBS)
    assemble(pieces, index, total, owned_high, ghost_high, width)

    def clear(p, carry):
        outbound[p] = jnp.zeros(outbound.shape[1:], jnp.float32)
        return carry

    lax.fori_loop(0, outbound.shape[0], clear, 0)
    dom = lax.axis_index("dom")
    fields = outbound.shape[0] // (dom_count * sub_count)
    ghost = [None] * 3
    for c in range(3):
        owned[c] = summed(total, c * owned_high, owned_high, owned_high)
        ghost[c] = summed(
            total, 3 * PARTS * owned_high + c * ghost_high, ghost_high, 3 * sub_count
        )
    for o in range(3):
        place = dom + o - 1

        @pl.when((place >= 0) & (place < dom_count))
        def _():
            for t in range(sub_count):
                for c in range(3):
                    for h in range(halves):
                        line = ghost[c][
                            o * sub_count + t : o * sub_count + t + 1,
                            h * LANES : (h + 1) * LANES,
                        ]
                        spot = c * halves + h
                        for f in range(fields):
                            outbound[
                                (place * sub_count + t) * fields + f, spot : spot + 1, :
                            ] = line


def owner_kernel(
    dims,
    counts,
    nodes,
    mine,
    other,
    arrived,
    obs,
    weighted,
    out,
    index,
    values,
):
    dom_count, sub_count, halves = dims
    width = halves * LANES
    fields = arrived.shape[0] // (dom_count * sub_count)
    owned_high = mine.shape[1]
    load_links(nodes, index, sub_count, halves)
    dom = lax.axis_index("dom")
    pairs = []
    for o in range(3):
        place = dom + o - 1
        inside = (place >= 0) & (place < dom_count)
        safe = jnp.clip(place, 0, dom_count - 1)
        for t in range(sub_count):
            chunk = arrived[(safe * sub_count + t) * fields]
            for f in range(1, fields):
                chunk = chunk + arrived[(safe * sub_count + t) * fields + f]
            chunk = jnp.where(inside, chunk, 0.0)
            split = split_parts(chunk)
            for h in range(halves):
                row = (o * sub_count + t) * halves + h
                here = open_lanes(counts, o, t, h)
                lines = [
                    jnp.where(here, split[part][c * halves + h : c * halves + h + 1, :], 0.0)
                    for part in range(PARTS)
                    for c in range(3)
                ]
                a, m = one_hot_pair(lines, index[row // SUBS, row % SUBS : row % SUBS + 1, :], owned_high, 0, width)
                pairs.append((a, m))
    total = contract(*[jnp.concatenate(x, axis=1) for x in zip(*pairs)])
    for c in range(3):
        value = mine[c] + other[c]
        landed = None
        for part in reversed(range(PARTS)):
            base = (part * 3 + c) * owned_high
            piece = total[base : base + owned_high, :]
            landed = piece if landed is None else landed + piece
        value = value + landed
        for h in range(halves):
            weight = obs[pl.ds(h, owned_high, stride=halves), :]
            weighted[c, pl.ds(h, owned_high, stride=halves), :] = (
                weight * value[:, h * LANES : (h + 1) * LANES]
            )
    rows = owned_high * halves
    send_links(weighted, rows, counts, index, values, out, dom_count, sub_count, halves)


def adjoint_kernel(
    dims, weighted, arrived, connect, coupled, vectors, hess, sums, table, index, pulled
):
    dom_count, sub_count, halves = dims
    rows = weighted.shape[1]
    table[:, 0:rows, :] = weighted[...]
    fill_ghosts(table, rows, arrived, dom_count, sub_count, halves)
    load_index(connect, index)

    def keep(k, c, value):
        pulled[k, c] = value

    lookup(table, rows + 3 * sub_count * halves, index, keep)
    search, remain = vectors[0], vectors[1]
    image = None
    for c in range(3):
        for k in range(10):
            term = coupled[c * 10 + k] * pulled[k, c]
            image = term if image is None else image + term
    image = image + vectors[3]
    hess[...] = image
    for i, product in enumerate(
        (remain * remain, search * image, remain * image, image * image)
    ):
        line = jnp.sum(product, axis=0, keepdims=True)
        for p in range(sums.shape[0]):
            sums[p, i : i + 1, :] = line


def update_kernel(sums, hess, vectors, iterate_out, residual_out, direction_out):
    totals = []
    for i in range(4):
        line = sums[0, i : i + 1, :]
        for p in range(1, sums.shape[0]):
            line = line + sums[p, i : i + 1, :]
        line = jnp.sum(line, axis=1, keepdims=True)
        totals.append(jnp.broadcast_to(line, (SUBS, LANES)))
    squared_before, curvature_sum, cross_term, image_square = totals
    search, remain, guess = vectors[0], vectors[1], vectors[2]
    step_length = squared_before / curvature_sum
    squared_after = (
        squared_before
        - 2.0 * step_length * cross_term
        + step_length * step_length * image_square
    )
    residual_next = remain - step_length * hess[...]
    iterate_out[...] = guess + step_length * search
    residual_out[...] = residual_next
    direction_out[...] = residual_next + squared_after / squared_before * search


def own_table(source, table):
    for c in range(3):
        for r in range(source.shape[1] // LANES):
            table[c, r : r + 1, :] = source[c : c + 1, r * LANES : (r + 1) * LANES]


def link_line(nodes, o, k, h):
    zero = nodes[0, o, 0:1, h * LANES : (h + 1) * LANES]
    one = nodes[0, o, 1:2, h * LANES : (h + 1) * LANES]
    return jnp.where((lax.axis_index("sub") ^ k) == 0, zero, one)


def link_limit(counts, o, k):
    return counts[0, lax.axis_index("sub") ^ k, o]


def link_tile(nodes, tile, links):
    tile[0] = jnp.zeros((SUBS, LANES), jnp.int32)
    for i, (o, k) in enumerate(links):
        for h in range(2):
            tile[0, 2 * i + h : 2 * i + h + 1, :] = link_line(nodes, o, k, h)


def pair_start_kernel(counts, nodes, background, out, index, table):
    step = jnp.where(lax.axis_index("field") == 0, 2, 0)
    links = ((step, 0), (step, 1), (1, 1))
    own_table(background, table)
    link_tile(nodes, index, links)
    row = lax.broadcasted_iota(jnp.int32, (SUBS, LANES), 0)
    slot = lax.broadcasted_iota(jnp.int32, (SUBS, LANES), 1) + row % 2 * LANES
    limit = jnp.zeros((SUBS, LANES), jnp.int32)
    for i, (o, k) in enumerate(links):
        limit = jnp.where(row // 2 == i, link_limit(counts, o, k), limit)

    def keep(tile, c, value):
        out[c] = jnp.where(slot < limit, value, 0.0)

    lookup(table, table.shape[1], index, keep)


BLOCKS = ((0, 0), (0, 1), (1, 0), (0, 2), (1, 1), (2, 0))


def pair_ghosts(dom_count, mine, other, middle, table):
    dom = lax.axis_index("dom")
    first = lax.axis_index("field") == 0
    for c in range(3):
        below = jnp.where(first, mine[c], other[c])
        above = jnp.where(first, other[c], mine[c])
        below = jnp.where(dom > 0, below, 0.0)
        above = jnp.where(dom < dom_count - 1, above, 0.0)
        table[c, 0:4, :] = below[0:4, :]
        table[c, 4:6, :] = jnp.zeros((2, LANES), jnp.float32)
        table[c, 6:8, :] = middle[c, 4:6, :]
        table[c, 8:12, :] = above[0:4, :]


def pair_join_kernel(straight, slanted, out):
    for c in range(3):
        out[c, 0:4, :] = straight[c, 0:4, :]
        out[c, 4:8, :] = slanted[c, 0:4, :]


def pair_own_kernel(
    link_slots,
    background,
    connect,
    stiff,
    live,
    scale,
    direction,
    index,
    partial,
    wide,
    marks,
    table,
):
    mask = live_mask(live[...])
    marks[0] = mask * direction[...]
    marks[1] = mask
    marks[2] = mask * scale[...]
    wide[...] = jnp.zeros_like(wide)
    size = stiff.shape[0]
    split = split_parts(stiff[...], 3)
    for i, (piece, _) in enumerate(BLOCKS):
        wide[0:size, i * 32 : i * 32 + size] = split[piece]
    sub = lax.axis_index("sub")
    own_table(background, table)
    load_index(connect, index)
    owned_nodes = background.shape[1]
    for k in range(10):
        entry = index[k]
        index[k] = jnp.where(entry >= owned_nodes, entry ^ (sub * link_slots), entry)

    def keep(k, c, value):
        partial[c * 10 + k] = value

    lookup(table, table.shape[1], index, keep)


def pair_forward_kernel(
    dom_count,
    wide,
    partial,
    index,
    mine,
    other,
    middle,
    marks,
    coupled,
    kept,
    sent,
    ghosts,
    state,
    pieces,
    total,
):
    owned_high = kept.shape[1] // 2 - SUBS // 2
    pair_ghosts(dom_count, mine, other, middle, ghosts)

    def begin(k, c):
        return partial[c * 10 + k]

    def keep(k, c, value):
        at = pl.multiple_of((c * 10 + k) * SUBS, SUBS)
        state[0, pl.ds(at, SUBS), :] = value

    lookup(ghosts, 12, index, keep, begin, 2 * owned_high)
    spare = state.shape[1] - 30 * SUBS
    state[0, 30 * SUBS :, :] = jnp.zeros((spare, LANES), jnp.float32)
    weights = wide[...].astype(jnp.bfloat16)
    for b in range(0, SUBS, 2):
        lines = jnp.concatenate(
            [state[0, pl.ds(b + i, 32, stride=SUBS), :] for i in range(2)], axis=1
        )
        split = [x.astype(jnp.bfloat16) for x in split_parts(lines, 3)]
        product = lax.dot_general(
            weights,
            jnp.concatenate([split[his] for _, his in BLOCKS], axis=0),
            (((1,), (0,)), ((), ())),
            preferred_element_type=jnp.float32,
        )
        for i in range(2):
            state[1, pl.ds(b + i, 32, stride=SUBS), :] = product[
                :, i * LANES : (i + 1) * LANES
            ]
    search, factor = marks[0], marks[2]
    for c in range(3):
        for k in range(10):
            at = (c * 10 + k) * SUBS
            result = factor * state[1, at : at + SUBS, :]
            coupled[c * 10 + k] = result
            for part, piece in enumerate(split_parts(search * result)):
                pieces[part * 3 + c, k] = piece
    width = 2 * LANES
    assemble(pieces, index, total, owned_high, SUBS, width)
    first = lax.axis_index("field") == 0
    base = 2 * owned_high
    for c in range(3):
        own = summed(total, c * owned_high, owned_high, owned_high)
        ghost = summed(total, 3 * PARTS * owned_high + c * SUBS, SUBS, SUBS)
        for h in range(2):
            half = own[:, h * LANES : (h + 1) * LANES]
            kept[c, h * owned_high : (h + 1) * owned_high, :] = half
            sent[c, h * owned_high : (h + 1) * owned_high, :] = half
            lines = ghost[:, h * LANES : (h + 1) * LANES]
            for k in range(2):
                below, above = lines[k : k + 1, :], lines[4 + k : 5 + k, :]
                at = base + 2 * k + h
                kept[c, at : at + 1, :] = jnp.where(first, above, below)
                sent[c, at : at + 1, :] = jnp.where(first, below, above)
            for out in (kept, sent):
                out[c, base + 4 + h : base + 5 + h, :] = lines[3:4, :]
                out[c, base + 6 + h : base + 7 + h, :] = jnp.zeros((1, LANES), jnp.float32)


def pair_sum_kernel(
    counts, nodes, obs, kept, came, own, link, index, table, weights
):
    part, fixed = link.at[0:3], link.at[3:6]
    rows = own.shape[1]
    half = rows // 2
    for c in range(3):
        both = kept[c, 0:rows, :] + came[c, 0:rows, :]
        own[c] = both
        for h in range(2):
            table[c, pl.ds(h, half, stride=2), :] = both[h * half : (h + 1) * half]
    link_tile(nodes, index, ((0, 1), (1, 1), (2, 1)))
    weights[0] = obs[...]

    def keep(tile, c, value):
        part[c] = value

    lookup(table, rows, index, keep)
    for c in range(3):
        part[c, 6:8, :] = (
            kept[c, rows + 4 : rows + 6, :] + came[c, rows + 4 : rows + 6, :]
        )

    def keep_weight(tile, c, value):
        fixed[2] = value

    lookup(weights, rows, index, keep_weight, comps=1)
    fixed[1] = jnp.full((SUBS, LANES), -1.0, jnp.float32)
    lane = lax.broadcasted_iota(jnp.int32, (1, LANES), 1)
    for o in range(3):
        for k in range(2):
            for h in range(2):
                at = (o * 2 + k) * 2 + h
                here = lane + h * LANES < link_limit(counts, o, k)
                fixed[at // SUBS, at % SUBS : at % SUBS + 1, :] = jnp.where(
                    here, link_line(nodes, o, k, h), -1
                ).astype(jnp.float32)


def landing(nodes, lines, owned_high, width):
    pairs = []
    for (o, k), source in lines:
        for h in range(2):
            at = (o * 2 + k) * 2 + h
            entry = nodes[at // SUBS, at % SUBS : at % SUBS + 1, :].astype(jnp.int32)
            values = [source(c, h) for c in range(3)]
            split = [split_parts(v) for v in values]
            pairs.append(
                one_hot_pair(
                    [split[c][part] for part in range(PARTS) for c in range(3)],
                    entry,
                    owned_high,
                    0,
                    width,
                )
            )
    return contract(*[jnp.concatenate(x, axis=1) for x in zip(*pairs)])


def pair_owner_kernel(
    dom_count,
    own,
    link,
    mine,
    other,
    came,
    obs,
    weighted,
    out,
    total,
    index,
    table,
):
    rows = own.shape[1]
    owned_high = rows // 2
    width = 2 * LANES
    dom = lax.axis_index("dom")
    first = lax.axis_index("field") == 0

    def pick(here, there, inside):
        def line(k):
            def get(c, h):
                at = 2 * k + h
                return jnp.where(
                    inside, jnp.where(first, here(c, at), there(c, at)), 0.0
                )

            return get

        return line

    def row_of(tiles, base, shift):
        return lambda c, at: tiles[base + c, shift + at : shift + at + 1, :]

    part, fixed, his_fixed = link.at[0:3], link.at[3:6], came.at[3:6]
    low, high = dom > 0, dom < dom_count - 1
    mine_at, other_at = row_of(mine, 0, 0), row_of(other, 0, 0)
    his_mine, his_other = row_of(mine, 0, 4), row_of(other, 0, 4)
    below = pick(mine_at, other_at, low)
    above = pick(other_at, mine_at, high)
    his_below = pick(his_mine, his_other, low)
    his_above = pick(his_other, his_mine, high)
    own_middle, his_middle = row_of(part, 0, 6), row_of(came, 0, 6)
    own_lines = (
        ((0, 0), below(0)),
        ((0, 1), his_below(1)),
        ((1, 1), his_middle),
        ((2, 0), above(0)),
        ((2, 1), his_above(1)),
    )
    his_lines = (
        ((0, 0), his_below(0)),
        ((0, 1), below(1)),
        ((1, 1), own_middle),
        ((2, 0), his_above(0)),
        ((2, 1), above(1)),
    )
    total[0] = landing(fixed, own_lines, owned_high, width)
    total[1] = landing(his_fixed, his_lines, owned_high, width)
    for c in range(3):
        landed = summed(total.at[0], c * owned_high, owned_high, owned_high)
        his = summed(total.at[1], c * owned_high, owned_high, owned_high)
        for h in range(2):
            at = pl.ds(h, owned_high, stride=2)
            value = own[c, h * owned_high : (h + 1) * owned_high, :]
            value = obs[at, :] * (value + landed[:, h * LANES : (h + 1) * LANES])
            weighted[c, at, :] = value
            table[c, at, :] = value
            table[c, pl.ds(rows + h, owned_high, stride=2), :] = his[
                :, h * LANES : (h + 1) * LANES
            ]

    def node(tiles, o, k, h):
        at = (o * 2 + k) * 2 + h
        return tiles[at // SUBS, at % SUBS : at % SUBS + 1, :].astype(jnp.int32)

    index[0] = jnp.full((SUBS, LANES), -1, jnp.int32)
    index[1] = jnp.zeros((SUBS, LANES), jnp.int32)
    shift = rows * LANES
    for h in range(2):
        line = jnp.where(first, node(fixed, 2, 0, h), node(fixed, 0, 0, h))
        index[0, h : h + 1, :] = line
        for at, line in (
            (2, jnp.where(first, node(his_fixed, 2, 1, h), node(his_fixed, 0, 1, h))),
            (4, node(his_fixed, 1, 1, h)),
        ):
            index[0, at + h : at + h + 1, :] = jnp.where(line < 0, line, line + shift)
    is_open = index[0] >= 0
    index[0] = jnp.maximum(index[0], 0)
    row = lax.broadcasted_iota(jnp.int32, (SUBS, LANES), 0)

    def lined_up(tile):
        lines = []
        for h in range(2):
            lines.append(jnp.where(first, tile[4 + h : 5 + h, :], tile[h : h + 1, :]))
        lines += [tile[2:3, :], tile[3:4, :]]
        blank = jnp.zeros((2, LANES), jnp.float32)
        return jnp.concatenate([blank] + lines + [blank], axis=0)

    weight = lined_up(his_fixed[2])

    def keep(tile, c, value):
        value = jnp.where(row < 2, value, weight * (lined_up(came[c]) + value))
        out[c] = jnp.where(is_open, value, 0.0)

    lookup(table, 2 * rows, index.at[0:1], keep)


def pair_near_kernel(weighted, index, coupled, near, pulled):
    def keep(k, c, value):
        pulled[c * 10 + k] = value

    lookup(weighted, weighted.shape[1], index, keep)
    image = None
    for i in range(30):
        term = coupled[i] * pulled[i]
        image = term if image is None else image + term
    near[...] = image


def write_sums(search, remain, image, sums):
    for i, product in enumerate(
        (remain * remain, search * image, remain * image, image * image)
    ):
        line = jnp.sum(product, axis=0, keepdims=True)
        for p in range(sums.shape[0]):
            sums[p, i : i + 1, :] = line


def pair_adjoint_kernel(
    dom_count,
    rows,
    near,
    mine,
    other,
    middle,
    index,
    coupled,
    marks,
    residual,
    iterate,
    reg,
    hess,
    sums,
    vectors,
    ghosts,
    pulled,
):
    pair_ghosts(dom_count, mine, other, middle, ghosts)

    def keep(k, c, value):
        pulled[c * 10 + k] = value

    lookup(ghosts, 12, index, keep, first=rows)
    image = near[...]
    for i in range(30):
        image = image + coupled[i] * pulled[i]
    search, mask = marks[0], marks[1]
    remain = mask * residual[...]
    image = image + reg[...] * search
    hess[...] = image
    vectors[0] = search
    vectors[1] = remain
    vectors[2] = mask * iterate[...]
    write_sums(search, remain, image, sums)


def pair_step(background, obs, connect, live_blocks, scale, others, nodes, counts, stiff):
    f32, i32 = jnp.float32, jnp.int32
    shape = jax.ShapeDtypeStruct
    dom_count = lax.axis_size("dom")
    owned_nodes = background.shape[1]
    link_slots = nodes.shape[3]
    rows = owned_nodes // LANES
    owned_high = owned_nodes // link_slots
    tile = (SUBS, LANES)
    swap = [(0, 1), (1, 0)]
    last = dom_count - 1

    def core(d, t, f):
        return (2 * d + t) * 2 + f

    def ring(turn):
        pairs = []
        for t in range(2):
            for d in range(last):
                pairs.append((core(d, t, 0), core(d + 1, t ^ turn, 0)))
                pairs.append((core(d + 1, t, 1), core(d, t ^ turn, 1)))
            pairs.append((core(last, t, 0), core(last, t, 1)))
            pairs.append((core(0, t, 1), core(0, t, 0)))
        return pairs

    left_rows = 3 * PARTS * owned_high + up_to(3 * PARTS * SUBS, 16)

    def across(x):
        return lax.ppermute(x, "field", swap)

    def beside(x):
        return lax.ppermute(x, "sub", swap)

    def along(x, turn=0):
        return lax.ppermute(x, ("dom", "sub", "field"), ring(turn))

    def call(kernel, outs, scratch, smem, args, params=PARAMS):
        return pl.pallas_call(
            kernel,
            compiler_params=params,
            out_shape=outs,
            in_specs=[SMEM] * smem + [VMEM] * (len(args) - smem),
            out_specs=jax.tree.map(lambda x: VMEM, outs),
            scratch_shapes=scratch,
            cost_estimate=pl.CostEstimate(
                flops=2**20, bytes_accessed=2**16, transcendentals=0
            ),
        )(*args)

    packed = call(
        pair_start_kernel,
        shape((3,) + tile, f32),
        [pltpu.VMEM((1,) + tile, i32), pltpu.VMEM((3, rows, LANES), f32)],
        1,
        (counts, nodes, background),
        None,
    )
    straight, slanted, middle = along(packed), along(packed, 1), beside(packed)
    direction, residual, iterate, reg = others
    index, partial, wide, marks = call(
        functools.partial(pair_own_kernel, link_slots),
        (
            shape((10,) + tile, i32),
            shape((30,) + tile, f32),
            shape((32, 32 * len(BLOCKS)), f32),
            shape((3,) + tile, f32),
        ),
        [pltpu.VMEM((3, rows, LANES), f32)],
        0,
        (background, connect, stiff, live_blocks.reshape(1, 1), scale, direction),
    )
    straight, partial = lax.optimization_barrier((straight, partial))
    upper = lax.broadcasted_iota(i32, (3,) + tile, 1) < 2
    mine = jnp.where(upper, straight, slanted)
    other = across(mine)
    coupled, kept, sent = call(
        functools.partial(pair_forward_kernel, dom_count),
        (
            shape((30,) + tile, f32),
            shape((3, rows + SUBS, LANES), f32),
            shape((3, rows + SUBS, LANES), f32),
        ),
        [
            pltpu.VMEM((3, 16, LANES), f32),
            pltpu.VMEM((2, 32 * SUBS, LANES), f32),
            pltpu.VMEM((3 * PARTS, 10) + tile, f32),
            pltpu.VMEM((left_rows, link_slots), f32),
        ],
        0,
        (wide, partial, index, mine, other, middle, marks),
    )
    came = across(sent)
    linked = kept[:, rows:] + came[:, rows:]
    straight, slanted = along(linked), along(linked, 1)
    own, link = call(
        pair_sum_kernel,
        (shape((3, rows, LANES), f32), shape((6,) + tile, f32)),
        [
            pltpu.VMEM((1,) + tile, i32),
            pltpu.VMEM((3, rows, LANES), f32),
            pltpu.VMEM((1, rows, LANES), f32),
        ],
        1,
        (counts, nodes, obs, kept, came),
    )
    straight, link = lax.optimization_barrier((straight, link))
    came = beside(link)
    mine = call(
        pair_join_kernel, shape((3,) + tile, f32), [], 0, (straight, slanted)
    )
    other = across(mine)
    weighted, outbound = call(
        functools.partial(pair_owner_kernel, dom_count),
        (shape((3, rows, LANES), f32), shape((3,) + tile, f32)),
        [
            pltpu.VMEM((2, 3 * PARTS * owned_high, link_slots), f32),
            pltpu.VMEM((2,) + tile, i32),
            pltpu.VMEM((3, 2 * rows, LANES), f32),
        ],
        0,
        (own, link, mine, other, came, obs),
    )
    mine = along(outbound)
    inner = call(
        pair_near_kernel,
        shape(tile, f32),
        [pltpu.VMEM((30,) + tile, f32)],
        0,
        (weighted, index, coupled),
    )
    mine, inner = lax.optimization_barrier((mine, inner))
    other = across(mine)
    hess, sums, vectors = call(
        functools.partial(pair_adjoint_kernel, dom_count, rows),
        (
            shape(tile, f32),
            shape((4 * dom_count, SUMS, LANES), f32),
            shape((3,) + tile, f32),
        ),
        [pltpu.VMEM((3, 16, LANES), f32), pltpu.VMEM((30,) + tile, f32)],
        0,
        (inner, mine, other, outbound, index, coupled, marks, residual, iterate, reg),
    )
    return hess, sums, vectors


def general_step(
    background, obs, connect, live_blocks, scale, others, send_nodes, counts, ref_stiff
):
    f32, i32 = jnp.float32, jnp.int32
    shape = jax.ShapeDtypeStruct
    dom_count = lax.axis_size("dom")
    sub_count = lax.axis_size("sub")
    field_count = lax.axis_size("field")
    owned_nodes = background.shape[1]
    link_slots = send_nodes.shape[3]
    halves = link_slots // LANES
    width = link_slots
    owned_high = owned_nodes // width
    owned_rows = owned_nodes // LANES
    ghost_rows = 3 * sub_count * halves
    table_rows = owned_rows + ghost_rows
    partitions = dom_count * sub_count
    devices = partitions * field_count
    chunk = up_to(3 * halves, SUBS)
    link_tiles = up_to(ghost_rows, SUBS) // SUBS
    left_rows = 3 * PARTS * owned_high + up_to(3 * PARTS * up_to(3 * sub_count, SUBS), 16)
    dims = (dom_count, sub_count, halves)
    links = ("dom", "sub")
    cores = ("dom", "sub", "field")

    outbound = pl.pallas_call(
        functools.partial(start_kernel, dims),
        out_shape=shape((partitions, chunk, LANES), f32),
        in_specs=[SMEM, VMEM, VMEM],
        out_specs=VMEM,
        scratch_shapes=[
            pltpu.VMEM((link_tiles, SUBS, LANES), i32),
            pltpu.VMEM((3, link_tiles, SUBS, LANES), f32),
            pltpu.VMEM((3, owned_rows, LANES), f32),
        ],
    )(counts, send_nodes, background)
    arrived = lax.all_to_all(outbound, links, 0, 0, tiled=True)

    coupled, vectors, owned, outbound = pl.pallas_call(
        functools.partial(forward_kernel, dims),
        compiler_params=PARAMS,
        out_shape=(
            shape((30, SUBS, LANES), f32),
            shape((5, SUBS, LANES), f32),
            shape((3, owned_high, width), f32),
            shape((devices, chunk, LANES), f32),
        ),
        in_specs=[SMEM, SMEM] + [VMEM] * 8,
        out_specs=(VMEM,) * 4,
        scratch_shapes=[
            pltpu.VMEM((3, table_rows, LANES), f32),
            pltpu.VMEM((10, SUBS, LANES), i32),
            pltpu.VMEM((30, SUBS, LANES), f32),
            pltpu.VMEM((3 * PARTS, 10, SUBS, LANES), f32),
            pltpu.VMEM((left_rows, width), f32),
        ],
    )(
        live_blocks,
        ref_stiff,
        background,
        arrived,
        connect,
        scale,
        *others,
    )
    swapped = lax.ppermute(
        owned, "field", [(i, (i + 1) % field_count) for i in range(field_count)]
    )
    arrived = lax.all_to_all(outbound, cores, 0, 0, tiled=True)

    weighted, outbound = pl.pallas_call(
        functools.partial(owner_kernel, dims),
        compiler_params=PARAMS,
        out_shape=(
            shape((3, owned_rows, LANES), f32),
            shape((partitions, chunk, LANES), f32),
        ),
        in_specs=[SMEM] + [VMEM] * 5,
        out_specs=(VMEM,) * 2,
        scratch_shapes=[
            pltpu.VMEM((link_tiles, SUBS, LANES), i32),
            pltpu.VMEM((3, link_tiles, SUBS, LANES), f32),
        ],
    )(counts, send_nodes, owned, swapped, arrived, obs)
    arrived = lax.all_to_all(outbound, links, 0, 0, tiled=True)

    hess, sums = pl.pallas_call(
        functools.partial(adjoint_kernel, dims),
        compiler_params=PARAMS,
        out_shape=(shape((SUBS, LANES), f32), shape((devices, SUMS, LANES), f32)),
        in_specs=[VMEM] * 5,
        out_specs=(VMEM,) * 2,
        scratch_shapes=[
            pltpu.VMEM((3, table_rows, LANES), f32),
            pltpu.VMEM((10, SUBS, LANES), i32),
            pltpu.VMEM((10, 3, SUBS, LANES), f32),
        ],
    )(weighted, arrived, connect, coupled, vectors)
    return hess, sums, vectors


def on_device(
    background,
    obs_weight,
    connect,
    live_blocks,
    elem_scale,
    reg_weight,
    iterate,
    residual,
    direction,
    send_nodes,
    send_count,
    ref_stiff,
):
    f32 = jnp.float32
    shape = jax.ShapeDtypeStruct
    tiled = lambda x: x.reshape(-1, LANES)
    scale, reg, guess, remain, search = map(
        tiled, (elem_scale, reg_weight, iterate, residual, direction)
    )
    obs = tiled(obs_weight)
    counts = jnp.swapaxes(send_count, 1, 2)
    two = lax.axis_size("sub") == 2 and lax.axis_size("field") == 2
    paired = two and send_nodes.shape[3] == 2 * LANES
    hess, sums, vectors = (pair_step if paired else general_step)(
        background,
        obs,
        connect,
        live_blocks,
        scale,
        (search, remain, guess, reg),
        send_nodes,
        counts,
        ref_stiff,
    )
    cores = ("dom", "sub", "field")
    sums = lax.all_to_all(sums, cores, 0, 0, tiled=True)

    results = pl.pallas_call(
        update_kernel,
        compiler_params=PARAMS,
        out_shape=(shape((SUBS, LANES), f32),) * 3,
        in_specs=[VMEM] * 3,
        out_specs=(VMEM,) * 3,
    )(sums, hess, vectors)
    return tuple(x.reshape(-1) for x in results)


def solution(mesh):
    placed = (
        P(None, ("groups", "dom", "sub")),
        P(("groups", "dom", "sub")),
        P(None, ("groups", "dom", "sub", "field")),
        P(("groups", "dom", "sub", "field")),
        P(("groups", "dom", "sub", "field")),
        P(("groups", "dom", "sub", "field")),
        P(("groups", "dom", "sub", "field")),
        P(("groups", "dom", "sub", "field")),
        P(("groups", "dom", "sub", "field")),
        P(("groups", "dom", "sub"), None, None, None),
        P(("groups", "dom", "sub"), None, None),
        P(),
    )
    return jax.shard_map(
        on_device,
        mesh=mesh,
        in_specs=placed,
        out_specs=(
            P(("groups", "dom", "sub", "field")),
            P(("groups", "dom", "sub", "field")),
            P(("groups", "dom", "sub", "field")),
        ),
        check_vma=False,
    )
```

```python
import functools

import jax
import jax.numpy as jnp
from jax import lax
from jax.experimental import pallas as pl
from jax.experimental.pallas import tpu as pltpu
from jax.sharding import PartitionSpec as P

BLK = 128
LANES = 128
SUBS = 8
PARTS = 2
UNROLL = 10
SUMS = 4
LANE_BITS = 7

VMEM = pl.BlockSpec(memory_space=pltpu.VMEM)
SMEM = pl.BlockSpec(memory_space=pltpu.SMEM)
FIRST = None
PARAMS = pltpu.CompilerParams(vmem_limit_bytes=16 * 2**20)


def up_to(count, step):
    return -(-count // step) * step


def lookup(table, rows, index, store, begin=None, first=0, comps=3, skip=()):
    def one(tile):
        entry = index[tile]
        high = lax.shift_right_logical(entry, LANE_BITS)
        low = entry & (LANES - 1)
        found = [0.0 if begin is None else begin(tile, c) for c in range(comps)]
        for row in range(rows):
            if row in skip:
                continue
            here = high == first + row
            for c in range(comps):
                line = jnp.broadcast_to(table[c, row : row + 1, :], (SUBS, LANES))
                value = jnp.take_along_axis(
                    line, low, axis=1, mode="promise_in_bounds"
                )
                found[c] = jnp.where(here, value, found[c])
        for c in range(comps):
            store(tile, c, found[c])

    def step(tile, carry):
        one(tile)
        return carry

    if index.shape[0] == 1:
        one(0)
    else:
        lax.fori_loop(0, index.shape[0], step, 0, unroll=min(2 if rows > 16 else 5, index.shape[0]))


def split_parts(value, count=PARTS):
    pieces = []
    for _ in range(count - 1):
        piece = value.astype(jnp.bfloat16).astype(jnp.float32)
        pieces.append(piece)
        value = value - piece
    pieces.append(value.astype(jnp.bfloat16).astype(jnp.float32))
    return pieces


def spread(line, rows):
    return jnp.broadcast_to(line, (rows, LANES)).astype(jnp.bfloat16)


def row_numbers(rows):
    row = lax.broadcasted_iota(jnp.int32, (rows, LANES), 0)
    return row.astype(jnp.float32).astype(jnp.bfloat16)


def one_hot_pair(lines, index, owned_high, ghost_high, width):
    none = jnp.zeros((), jnp.bfloat16)
    unit = jnp.ones((), jnp.bfloat16)
    high = index // width
    low = (index & (width - 1)).astype(jnp.float32)
    here = row_numbers(owned_high) == spread(high.astype(jnp.float32), owned_high)
    blocks = [jnp.where(here, spread(x, owned_high), none) for x in lines]
    if ghost_high:
        row = lax.broadcasted_iota(jnp.int32, (ghost_high, LANES), 0) + owned_high
        here = row == jnp.broadcast_to(high, row.shape)
        rest = [jnp.where(here, jnp.broadcast_to(x, row.shape), 0.0) for x in lines]
        spare = up_to(len(lines) * ghost_high, 16) - len(lines) * ghost_high
        if spare:
            rest.append(jnp.zeros((spare, LANES), jnp.float32))
        blocks.append(jnp.concatenate(rest, axis=0).astype(jnp.bfloat16))
    left = jnp.concatenate(blocks, axis=0)
    right = jnp.where(row_numbers(width) == spread(low, width), unit, none)
    return left, right


def contract(left, right):
    return lax.dot_general(
        left, right, (((1,), (1,)), ((), ())), preferred_element_type=jnp.float32
    )


def link_rows(sub_count, halves):
    return [
        (o, t, h, (o * sub_count + t) * halves + h)
        for o in range(3)
        for t in range(sub_count)
        for h in range(halves)
    ]


def load_links(nodes, index, sub_count, halves):
    for o, t, h, row in link_rows(sub_count, halves):
        index[row // SUBS, row % SUBS : row % SUBS + 1, :] = nodes[
            0, o, t : t + 1, h * LANES : (h + 1) * LANES
        ]
    for row in range(3 * sub_count * halves, index.shape[0] * SUBS):
        index[row // SUBS, row % SUBS : row % SUBS + 1, :] = jnp.zeros((1, LANES), jnp.int32)


def open_lanes(counts, o, t, h):
    lane = lax.broadcasted_iota(jnp.int32, (1, LANES), 1) + h * LANES
    return lane < counts[0, t, o]


def send_links(table, table_rows, counts, index, values, out, dom_count, sub_count, halves):
    def store(tile, c, value):
        values[c, tile] = value

    lookup(table, table_rows, index, store)

    def clear(p, carry):
        out[p] = jnp.zeros(out.shape[1:], jnp.float32)
        return carry

    lax.fori_loop(0, out.shape[0], clear, 0)
    dom = lax.axis_index("dom")
    for o in range(3):
        place = dom + o - 1

        @pl.when((place >= 0) & (place < dom_count))
        def _():
            for t in range(sub_count):
                for h in range(halves):
                    row = (o * sub_count + t) * halves + h
                    here = open_lanes(counts, o, t, h)
                    for c in range(3):
                        line = values[c, row // SUBS, row % SUBS : row % SUBS + 1, :]
                        out[place * sub_count + t, c * halves + h : c * halves + h + 1, :] = (
                            jnp.where(here, line, 0.0)
                        )


def fill_ghosts(table, first, arrived, dom_count, sub_count, halves):
    dom = lax.axis_index("dom")
    for o in range(3):
        place = dom + o - 1
        inside = (place >= 0) & (place < dom_count)
        safe = jnp.clip(place, 0, dom_count - 1)
        for t in range(sub_count):
            chunk = arrived[safe * sub_count + t]
            chunk = jnp.where(inside, chunk, 0.0)
            for c in range(3):
                row = first + (o * sub_count + t) * halves
                table[c, row : row + halves, :] = chunk[c * halves : (c + 1) * halves, :]


def start_kernel(dims, counts, nodes, background, out, index, values, table):
    dom_count, sub_count, halves = dims
    rows = background.shape[1] // LANES
    for c in range(3):
        for r in range(rows):
            table[c, r : r + 1, :] = background[c : c + 1, r * LANES : (r + 1) * LANES]
    load_links(nodes, index, sub_count, halves)
    send_links(table, rows, counts, index, values, out, dom_count, sub_count, halves)


def load_index(connect, index):
    for k in range(10):
        for b in range(SUBS):
            index[k, b : b + 1, :] = connect[k : k + 1, b * LANES : (b + 1) * LANES]


def couple(live, stiff, scale, others, state, coupled, vectors, pieces):
    element_vectors(live, scale, others, vectors)
    forward_terms(stiff, state, coupled, vectors, pieces)


def live_mask(blocks):
    element = (
        lax.broadcasted_iota(jnp.int32, (SUBS, LANES), 0) * LANES
        + lax.broadcasted_iota(jnp.int32, (SUBS, LANES), 1)
    )
    return (element < BLK * blocks).astype(jnp.float32)


def element_vectors(live, scale, others, vectors):
    direction, residual, iterate, reg = others
    mask = live_mask(live[0])
    search = mask * direction[...]
    vectors[0] = search
    vectors[1] = mask * residual[...]
    vectors[2] = mask * iterate[...]
    vectors[3] = reg[...] * search
    vectors[4] = mask * scale[...]


def forward_terms(stiff, state, coupled, vectors, pieces):
    search, factor = vectors[0], vectors[4]
    for c in range(3):
        sums = [None] * 10
        for j in range(30):
            value = state[j]
            for k in range(10):
                term = stiff[c * 10 + k, j] * value
                sums[k] = term if j == 0 else sums[k] + term
        for k in range(10):
            result = factor * sums[k]
            coupled[c * 10 + k] = result
            for part, piece in enumerate(split_parts(search * result)):
                pieces[part * 3 + c, k] = piece


def assemble(pieces, index, total, owned_high, ghost_high, width):
    total[...] = jnp.zeros_like(total)

    def scatter(k, carry):
        pairs = [
            one_hot_pair(
                [pieces[q, k, b : b + 1, :] for q in range(3 * PARTS)],
                index[k, b : b + 1, :],
                owned_high,
                ghost_high,
                width,
            )
            for b in range(SUBS)
        ]
        total[...] += contract(*[jnp.concatenate(x, axis=1) for x in zip(*pairs)])
        return carry

    lax.fori_loop(0, 10, scatter, 0, unroll=UNROLL)


def summed(total, first, step, count):
    value = None
    for part in reversed(range(PARTS)):
        base = first + part * 3 * step
        piece = total[base : base + count, :]
        value = piece if value is None else value + piece
    return value


def forward_kernel(
    dims,
    live,
    stiff,
    background,
    arrived,
    connect,
    scale,
    direction,
    residual,
    iterate,
    reg,
    coupled,
    vectors,
    owned,
    outbound,
    table,
    index,
    state,
    pieces,
    total,
):
    dom_count, sub_count, halves = dims
    width = halves * LANES
    rows = background.shape[1] // LANES
    owned_high = background.shape[1] // width
    ghost_rows = 3 * sub_count * halves
    for c in range(3):
        for r in range(rows):
            table[c, r : r + 1, :] = background[c : c + 1, r * LANES : (r + 1) * LANES]
    fill_ghosts(table, rows, arrived, dom_count, sub_count, halves)
    load_index(connect, index)

    def keep(k, c, value):
        state[c * 10 + k] = value

    lookup(table, rows + ghost_rows, index, keep)
    couple(
        live,
        stiff,
        scale,
        (direction, residual, iterate, reg),
        state,
        coupled,
        vectors,
        pieces,
    )
    ghost_high = up_to(3 * sub_count, SUBS)
    assemble(pieces, index, total, owned_high, ghost_high, width)

    def clear(p, carry):
        outbound[p] = jnp.zeros(outbound.shape[1:], jnp.float32)
        return carry

    lax.fori_loop(0, outbound.shape[0], clear, 0)
    dom = lax.axis_index("dom")
    fields = outbound.shape[0] // (dom_count * sub_count)
    ghost = [None] * 3
    for c in range(3):
        owned[c] = summed(total, c * owned_high, owned_high, owned_high)
        ghost[c] = summed(
            total, 3 * PARTS * owned_high + c * ghost_high, ghost_high, 3 * sub_count
        )
    for o in range(3):
        place = dom + o - 1

        @pl.when((place >= 0) & (place < dom_count))
        def _():
            for t in range(sub_count):
                for c in range(3):
                    for h in range(halves):
                        line = ghost[c][
                            o * sub_count + t : o * sub_count + t + 1,
                            h * LANES : (h + 1) * LANES,
                        ]
                        spot = c * halves + h
                        for f in range(fields):
                            outbound[
                                (place * sub_count + t) * fields + f, spot : spot + 1, :
                            ] = line


def owner_kernel(
    dims,
    counts,
    nodes,
    mine,
    other,
    arrived,
    obs,
    weighted,
    out,
    index,
    values,
):
    dom_count, sub_count, halves = dims
    width = halves * LANES
    fields = arrived.shape[0] // (dom_count * sub_count)
    owned_high = mine.shape[1]
    load_links(nodes, index, sub_count, halves)
    dom = lax.axis_index("dom")
    pairs = []
    for o in range(3):
        place = dom + o - 1
        inside = (place >= 0) & (place < dom_count)
        safe = jnp.clip(place, 0, dom_count - 1)
        for t in range(sub_count):
            chunk = arrived[(safe * sub_count + t) * fields]
            for f in range(1, fields):
                chunk = chunk + arrived[(safe * sub_count + t) * fields + f]
            chunk = jnp.where(inside, chunk, 0.0)
            split = split_parts(chunk)
            for h in range(halves):
                row = (o * sub_count + t) * halves + h
                here = open_lanes(counts, o, t, h)
                lines = [
                    jnp.where(here, split[part][c * halves + h : c * halves + h + 1, :], 0.0)
                    for part in range(PARTS)
                    for c in range(3)
                ]
                a, m = one_hot_pair(lines, index[row // SUBS, row % SUBS : row % SUBS + 1, :], owned_high, 0, width)
                pairs.append((a, m))
    total = contract(*[jnp.concatenate(x, axis=1) for x in zip(*pairs)])
    for c in range(3):
        value = mine[c] + other[c]
        landed = None
        for part in reversed(range(PARTS)):
            base = (part * 3 + c) * owned_high
            piece = total[base : base + owned_high, :]
            landed = piece if landed is None else landed + piece
        value = value + landed
        for h in range(halves):
            weight = obs[pl.ds(h, owned_high, stride=halves), :]
            weighted[c, pl.ds(h, owned_high, stride=halves), :] = (
                weight * value[:, h * LANES : (h + 1) * LANES]
            )
    rows = owned_high * halves
    send_links(weighted, rows, counts, index, values, out, dom_count, sub_count, halves)


def adjoint_kernel(
    dims, weighted, arrived, connect, coupled, vectors, hess, sums, table, index, pulled
):
    dom_count, sub_count, halves = dims
    rows = weighted.shape[1]
    table[:, 0:rows, :] = weighted[...]
    fill_ghosts(table, rows, arrived, dom_count, sub_count, halves)
    load_index(connect, index)

    def keep(k, c, value):
        pulled[k, c] = value

    lookup(table, rows + 3 * sub_count * halves, index, keep)
    search, remain = vectors[0], vectors[1]
    image = None
    for c in range(3):
        for k in range(10):
            term = coupled[c * 10 + k] * pulled[k, c]
            image = term if image is None else image + term
    image = image + vectors[3]
    hess[...] = image
    for i, product in enumerate(
        (remain * remain, search * image, remain * image, image * image)
    ):
        line = jnp.sum(product, axis=0, keepdims=True)
        for p in range(sums.shape[0]):
            sums[p, i : i + 1, :] = line


def update_kernel(sums, hess, vectors, iterate_out, residual_out, direction_out):
    totals = []
    for i in range(4):
        line = sums[0, i : i + 1, :]
        for p in range(1, sums.shape[0]):
            line = line + sums[p, i : i + 1, :]
        line = jnp.sum(line, axis=1, keepdims=True)
        totals.append(jnp.broadcast_to(line, (SUBS, LANES)))
    squared_before, curvature_sum, cross_term, image_square = totals
    search, remain, guess = vectors[0], vectors[1], vectors[2]
    step_length = squared_before / curvature_sum
    squared_after = (
        squared_before
        - 2.0 * step_length * cross_term
        + step_length * step_length * image_square
    )
    residual_next = remain - step_length * hess[...]
    iterate_out[...] = guess + step_length * search
    residual_out[...] = residual_next
    direction_out[...] = residual_next + squared_after / squared_before * search


def own_table(source, table):
    for c in range(3):
        for r in range(source.shape[1] // LANES):
            table[c, r : r + 1, :] = source[c : c + 1, r * LANES : (r + 1) * LANES]


def link_line(nodes, o, k, h):
    zero = nodes[0, o, 0:1, h * LANES : (h + 1) * LANES]
    one = nodes[0, o, 1:2, h * LANES : (h + 1) * LANES]
    return jnp.where((lax.axis_index("sub") ^ k) == 0, zero, one)


def link_limit(counts, o, k):
    return counts[0, lax.axis_index("sub") ^ k, o]


def link_tile(nodes, tile, links):
    tile[0] = jnp.zeros((SUBS, LANES), jnp.int32)
    for i, (o, k) in enumerate(links):
        for h in range(2):
            tile[0, 2 * i + h : 2 * i + h + 1, :] = link_line(nodes, o, k, h)


def pair_start_kernel(counts, nodes, background, out, index, table):
    step = jnp.where(lax.axis_index("field") == 0, 2, 0)
    links = ((step, 0), (step, 1), (1, 1))
    own_table(background, table)
    link_tile(nodes, index, links)
    row = lax.broadcasted_iota(jnp.int32, (SUBS, LANES), 0)
    slot = lax.broadcasted_iota(jnp.int32, (SUBS, LANES), 1) + row % 2 * LANES
    limit = jnp.zeros((SUBS, LANES), jnp.int32)
    for i, (o, k) in enumerate(links):
        limit = jnp.where(row // 2 == i, link_limit(counts, o, k), limit)

    def keep(tile, c, value):
        out[c] = jnp.where(slot < limit, value, 0.0)

    lookup(table, table.shape[1], index, keep)


BLOCKS = ((0, 0), (0, 1), (1, 0), (0, 2), (1, 1), (2, 0))


NOBODY = (4, 5)


def pair_ghosts(dom_count, mine, other, middle, table):
    dom = lax.axis_index("dom")
    first = lax.axis_index("field") == 0
    for c in range(3):
        below = jnp.where(first, mine[c], other[c])
        above = jnp.where(first, other[c], mine[c])
        below = jnp.where(dom > 0, below, 0.0)
        above = jnp.where(dom < dom_count - 1, above, 0.0)
        table[c, 0:4, :] = below[0:4, :]
        table[c, 6:8, :] = middle[c, 4:6, :]
        table[c, 8:12, :] = above[0:4, :]


def pair_join_kernel(straight, slanted, out):
    for c in range(3):
        out[c, 0:4, :] = straight[c, 0:4, :]
        out[c, 4:8, :] = slanted[c, 0:4, :]


def pair_own_kernel(
    link_slots,
    background,
    connect,
    stiff,
    scale,
    direction,
    index,
    partial,
    wide,
    vectors,
    table,
):
    vectors[0] = direction[...]
    vectors[1] = scale[...]
    wide[...] = jnp.zeros_like(wide)
    size = stiff.shape[0]
    split = split_parts(stiff[...], 3)
    for i, (piece, _) in enumerate(BLOCKS):
        wide[0:size, i * 32 : i * 32 + size] = split[piece]
    sub = lax.axis_index("sub")
    own_table(background, table)
    load_index(connect, index)
    owned_nodes = background.shape[1]
    for k in range(10):
        entry = index[k]
        index[k] = jnp.where(entry >= owned_nodes, entry ^ (sub * link_slots), entry)

    def keep(k, c, value):
        partial[c * 10 + k] = value

    lookup(table, table.shape[1], index, keep)


def pair_forward_kernel(
    dom_count,
    wide,
    partial,
    index,
    mine,
    other,
    middle,
    live,
    vectors,
    coupled,
    marks,
    kept,
    sent,
    ghosts,
    state,
    pieces,
    total,
):
    owned_high = kept.shape[1] // 2 - SUBS // 2
    pair_ghosts(dom_count, mine, other, middle, ghosts)

    def begin(k, c):
        return partial[c * 10 + k]

    def keep(k, c, value):
        at = pl.multiple_of((c * 10 + k) * SUBS, SUBS)
        state[0, pl.ds(at, SUBS), :] = value

    lookup(ghosts, 12, index, keep, begin, 2 * owned_high, skip=NOBODY)
    spare = state.shape[1] - 30 * SUBS
    state[0, 30 * SUBS :, :] = jnp.zeros((spare, LANES), jnp.float32)
    weights = wide[...].astype(jnp.bfloat16)
    for b in range(0, SUBS, 2):
        lines = jnp.concatenate(
            [state[0, pl.ds(b + i, 32, stride=SUBS), :] for i in range(2)], axis=1
        )
        split = [x.astype(jnp.bfloat16) for x in split_parts(lines, 3)]
        product = lax.dot_general(
            weights,
            jnp.concatenate([split[his] for _, his in BLOCKS], axis=0),
            (((1,), (0,)), ((), ())),
            preferred_element_type=jnp.float32,
        )
        for i in range(2):
            state[1, pl.ds(b + i, 32, stride=SUBS), :] = product[
                :, i * LANES : (i + 1) * LANES
            ]
    mask = live_mask(live[...])
    search, factor = mask * vectors[0], mask * vectors[1]
    marks[0] = search
    marks[1] = mask
    for c in range(3):
        for k in range(10):
            at = (c * 10 + k) * SUBS
            result = factor * state[1, at : at + SUBS, :]
            coupled[c * 10 + k] = result
            for part, piece in enumerate(split_parts(search * result)):
                pieces[part * 3 + c, k] = piece
    width = 2 * LANES
    assemble(pieces, index, total, owned_high, SUBS, width)
    first = lax.axis_index("field") == 0
    base = 2 * owned_high
    for c in range(3):
        own = summed(total, c * owned_high, owned_high, owned_high)
        ghost = summed(total, 3 * PARTS * owned_high + c * SUBS, SUBS, SUBS)
        for h in range(2):
            half = own[:, h * LANES : (h + 1) * LANES]
            kept[c, h * owned_high : (h + 1) * owned_high, :] = half
            sent[c, h * owned_high : (h + 1) * owned_high, :] = half
            lines = ghost[:, h * LANES : (h + 1) * LANES]
            for k in range(2):
                below, above = lines[k : k + 1, :], lines[4 + k : 5 + k, :]
                at = base + 2 * k + h
                kept[c, at : at + 1, :] = jnp.where(first, above, below)
                sent[c, at : at + 1, :] = jnp.where(first, below, above)
            for out in (kept, sent):
                out[c, base + 4 + h : base + 5 + h, :] = lines[3:4, :]
                out[c, base + 6 + h : base + 7 + h, :] = jnp.zeros((1, LANES), jnp.float32)


def pair_sum_kernel(
    counts, nodes, obs, kept, came, own, link, index, table, weights
):
    part, fixed = link.at[0:3], link.at[3:6]
    rows = own.shape[1]
    half = rows // 2
    for c in range(3):
        both = kept[c, 0:rows, :] + came[c, 0:rows, :]
        own[c] = both
        for h in range(2):
            table[c, pl.ds(h, half, stride=2), :] = both[h * half : (h + 1) * half]
    link_tile(nodes, index, ((0, 1), (1, 1), (2, 1)))
    weights[0] = obs[...]

    def keep(tile, c, value):
        part[c] = value

    lookup(table, rows, index, keep)
    for c in range(3):
        part[c, 6:8, :] = (
            kept[c, rows + 4 : rows + 6, :] + came[c, rows + 4 : rows + 6, :]
        )

    def keep_weight(tile, c, value):
        fixed[2] = value

    lookup(weights, rows, index, keep_weight, comps=1)
    fixed[1] = jnp.full((SUBS, LANES), -1.0, jnp.float32)
    lane = lax.broadcasted_iota(jnp.int32, (1, LANES), 1)
    for o in range(3):
        for k in range(2):
            for h in range(2):
                at = (o * 2 + k) * 2 + h
                here = lane + h * LANES < link_limit(counts, o, k)
                fixed[at // SUBS, at % SUBS : at % SUBS + 1, :] = jnp.where(
                    here, link_line(nodes, o, k, h), -1
                ).astype(jnp.float32)


def landing(nodes, lines, owned_high, width):
    pairs = []
    for (o, k), source in lines:
        for h in range(2):
            at = (o * 2 + k) * 2 + h
            entry = nodes[at // SUBS, at % SUBS : at % SUBS + 1, :].astype(jnp.int32)
            values = [source(c, h) for c in range(3)]
            split = [split_parts(v) for v in values]
            pairs.append(
                one_hot_pair(
                    [split[c][part] for part in range(PARTS) for c in range(3)],
                    entry,
                    owned_high,
                    0,
                    width,
                )
            )
    return contract(*[jnp.concatenate(x, axis=1) for x in zip(*pairs)])


def pair_owner_kernel(
    dom_count,
    own,
    link,
    mine,
    other,
    came,
    obs,
    weighted,
    out,
    total,
    index,
    table,
):
    rows = own.shape[1]
    owned_high = rows // 2
    width = 2 * LANES
    dom = lax.axis_index("dom")
    first = lax.axis_index("field") == 0

    def pick(here, there, inside):
        def line(k):
            def get(c, h):
                at = 2 * k + h
                return jnp.where(
                    inside, jnp.where(first, here(c, at), there(c, at)), 0.0
                )

            return get

        return line

    def row_of(tiles, base, shift):
        return lambda c, at: tiles[base + c, shift + at : shift + at + 1, :]

    part, fixed, his_fixed = link.at[0:3], link.at[3:6], came.at[3:6]
    low, high = dom > 0, dom < dom_count - 1
    mine_at, other_at = row_of(mine, 0, 0), row_of(other, 0, 0)
    his_mine, his_other = row_of(mine, 0, 4), row_of(other, 0, 4)
    below = pick(mine_at, other_at, low)
    above = pick(other_at, mine_at, high)
    his_below = pick(his_mine, his_other, low)
    his_above = pick(his_other, his_mine, high)
    own_middle, his_middle = row_of(part, 0, 6), row_of(came, 0, 6)
    own_lines = (
        ((0, 0), below(0)),
        ((0, 1), his_below(1)),
        ((1, 1), his_middle),
        ((2, 0), above(0)),
        ((2, 1), his_above(1)),
    )
    his_lines = (
        ((0, 0), his_below(0)),
        ((0, 1), below(1)),
        ((1, 1), own_middle),
        ((2, 0), his_above(0)),
        ((2, 1), above(1)),
    )
    total[0] = landing(fixed, own_lines, owned_high, width)
    total[1] = landing(his_fixed, his_lines, owned_high, width)
    for c in range(3):
        landed = summed(total.at[0], c * owned_high, owned_high, owned_high)
        his = summed(total.at[1], c * owned_high, owned_high, owned_high)
        for h in range(2):
            at = pl.ds(h, owned_high, stride=2)
            value = own[c, h * owned_high : (h + 1) * owned_high, :]
            value = obs[at, :] * (value + landed[:, h * LANES : (h + 1) * LANES])
            weighted[c, at, :] = value
            table[c, at, :] = value
            table[c, pl.ds(rows + h, owned_high, stride=2), :] = his[
                :, h * LANES : (h + 1) * LANES
            ]

    def node(tiles, o, k, h):
        at = (o * 2 + k) * 2 + h
        return tiles[at // SUBS, at % SUBS : at % SUBS + 1, :].astype(jnp.int32)

    index[0] = jnp.full((SUBS, LANES), -1, jnp.int32)
    index[1] = jnp.zeros((SUBS, LANES), jnp.int32)
    shift = rows * LANES
    for h in range(2):
        line = jnp.where(first, node(fixed, 2, 0, h), node(fixed, 0, 0, h))
        index[0, h : h + 1, :] = line
        for at, line in (
            (2, jnp.where(first, node(his_fixed, 2, 1, h), node(his_fixed, 0, 1, h))),
            (4, node(his_fixed, 1, 1, h)),
        ):
            index[0, at + h : at + h + 1, :] = jnp.where(line < 0, line, line + shift)
    is_open = index[0] >= 0
    index[0] = jnp.maximum(index[0], 0)
    row = lax.broadcasted_iota(jnp.int32, (SUBS, LANES), 0)

    def lined_up(tile):
        lines = []
        for h in range(2):
            lines.append(jnp.where(first, tile[4 + h : 5 + h, :], tile[h : h + 1, :]))
        lines += [tile[2:3, :], tile[3:4, :]]
        blank = jnp.zeros((2, LANES), jnp.float32)
        return jnp.concatenate([blank] + lines + [blank], axis=0)

    weight = lined_up(his_fixed[2])

    def keep(tile, c, value):
        value = jnp.where(row < 2, value, weight * (lined_up(came[c]) + value))
        out[c] = jnp.where(is_open, value, 0.0)

    lookup(table, 2 * rows, index.at[0:1], keep)


def pair_near_kernel(weighted, index, coupled, near, pulled):
    def keep(k, c, value):
        pulled[c * 10 + k] = value

    lookup(weighted, weighted.shape[1], index, keep)
    image = None
    for i in range(30):
        term = coupled[i] * pulled[i]
        image = term if image is None else image + term
    near[...] = image


def write_sums(search, remain, image, sums):
    for i, product in enumerate(
        (remain * remain, search * image, remain * image, image * image)
    ):
        line = jnp.sum(product, axis=0, keepdims=True)
        for p in range(sums.shape[0]):
            sums[p, i : i + 1, :] = line


def pair_adjoint_kernel(
    dom_count,
    rows,
    near,
    mine,
    other,
    middle,
    index,
    coupled,
    marks,
    residual,
    iterate,
    reg,
    hess,
    sums,
    vectors,
    ghosts,
    pulled,
):
    pair_ghosts(dom_count, mine, other, middle, ghosts)

    def keep(k, c, value):
        pulled[c * 10 + k] = value

    lookup(ghosts, 12, index, keep, first=rows, skip=NOBODY)
    image = near[...]
    for i in range(30):
        image = image + coupled[i] * pulled[i]
    search, mask = marks[0], marks[1]
    remain = mask * residual[...]
    image = image + reg[...] * search
    hess[...] = image
    vectors[0] = search
    vectors[1] = remain
    vectors[2] = mask * iterate[...]
    write_sums(search, remain, image, sums)


def pair_step(background, obs, connect, live_blocks, scale, others, nodes, counts, stiff):
    f32, i32 = jnp.float32, jnp.int32
    shape = jax.ShapeDtypeStruct
    dom_count = lax.axis_size("dom")
    owned_nodes = background.shape[1]
    link_slots = nodes.shape[3]
    rows = owned_nodes // LANES
    owned_high = owned_nodes // link_slots
    tile = (SUBS, LANES)
    swap = [(0, 1), (1, 0)]
    last = dom_count - 1

    def core(d, t, f):
        return (2 * d + t) * 2 + f

    def ring(turn):
        pairs = []
        for t in range(2):
            for d in range(last):
                pairs.append((core(d, t, 0), core(d + 1, t ^ turn, 0)))
                pairs.append((core(d + 1, t, 1), core(d, t ^ turn, 1)))
            pairs.append((core(last, t, 0), core(last, t, 1)))
            pairs.append((core(0, t, 1), core(0, t, 0)))
        return pairs

    left_rows = 3 * PARTS * owned_high + up_to(3 * PARTS * SUBS, 16)

    def across(x):
        return lax.ppermute(x, "field", swap)

    def beside(x):
        return lax.ppermute(x, "sub", swap)

    def along(x, turn=0):
        return lax.ppermute(x, ("dom", "sub", "field"), ring(turn))

    def call(kernel, outs, scratch, smem, args, params=PARAMS):
        return pl.pallas_call(
            kernel,
            compiler_params=params,
            out_shape=outs,
            in_specs=[SMEM] * smem + [VMEM] * (len(args) - smem),
            out_specs=jax.tree.map(lambda x: VMEM, outs),
            scratch_shapes=scratch,
            cost_estimate=pl.CostEstimate(
                flops=2**20, bytes_accessed=2**16, transcendentals=0
            ),
        )(*args)

    packed = call(
        pair_start_kernel,
        shape((3,) + tile, f32),
        [pltpu.VMEM((1,) + tile, i32), pltpu.VMEM((3, rows, LANES), f32)],
        1,
        (counts, nodes, background),
        FIRST,
    )
    middle, slanted, straight = beside(packed), along(packed, 1), along(packed)
    direction, residual, iterate, reg = others
    index, partial, wide, vectors = call(
        functools.partial(pair_own_kernel, link_slots),
        (
            shape((10,) + tile, i32),
            shape((30,) + tile, f32),
            shape((32, 32 * len(BLOCKS)), f32),
            shape((2,) + tile, f32),
        ),
        [pltpu.VMEM((3, rows, LANES), f32)],
        0,
        (background, connect, stiff, scale, direction),
    )
    straight, partial = lax.optimization_barrier((straight, partial))
    upper = lax.broadcasted_iota(i32, (3,) + tile, 1) < 2
    mine = jnp.where(upper, straight, slanted)
    other = across(mine)
    coupled, marks, kept, sent = call(
        functools.partial(pair_forward_kernel, dom_count),
        (
            shape((30,) + tile, f32),
            shape((2,) + tile, f32),
            shape((3, rows + SUBS, LANES), f32),
            shape((3, rows + SUBS, LANES), f32),
        ),
        [
            pltpu.VMEM((3, 16, LANES), f32),
            pltpu.VMEM((2, 32 * SUBS, LANES), f32),
            pltpu.VMEM((3 * PARTS, 10) + tile, f32),
            pltpu.VMEM((left_rows, link_slots), f32),
        ],
        0,
        (
            wide,
            partial,
            index,
            mine,
            other,
            middle,
            live_blocks.reshape(1, 1),
            vectors,
        ),
    )
    came = across(sent)
    linked = kept[:, rows:] + came[:, rows:]
    straight, slanted = along(linked), along(linked, 1)
    own, link = call(
        pair_sum_kernel,
        (shape((3, rows, LANES), f32), shape((6,) + tile, f32)),
        [
            pltpu.VMEM((1,) + tile, i32),
            pltpu.VMEM((3, rows, LANES), f32),
            pltpu.VMEM((1, rows, LANES), f32),
        ],
        1,
        (counts, nodes, obs, kept, came),
    )
    came = beside(link)
    straight, slanted, _ = lax.optimization_barrier((straight, slanted, link))
    mine = call(
        pair_join_kernel, shape((3,) + tile, f32), [], 0, (straight, slanted)
    )
    other = across(mine)
    weighted, outbound = call(
        functools.partial(pair_owner_kernel, dom_count),
        (shape((3, rows, LANES), f32), shape((3,) + tile, f32)),
        [
            pltpu.VMEM((2, 3 * PARTS * owned_high, link_slots), f32),
            pltpu.VMEM((2,) + tile, i32),
            pltpu.VMEM((3, 2 * rows, LANES), f32),
        ],
        0,
        (own, link, mine, other, came, obs),
    )
    mine = along(outbound)
    inner = call(
        pair_near_kernel,
        shape(tile, f32),
        [pltpu.VMEM((30,) + tile, f32)],
        0,
        (weighted, index, coupled),
    )
    mine, inner = lax.optimization_barrier((mine, inner))
    other = across(mine)
    hess, sums, vectors = call(
        functools.partial(pair_adjoint_kernel, dom_count, rows),
        (
            shape(tile, f32),
            shape((4 * dom_count, SUMS, LANES), f32),
            shape((3,) + tile, f32),
        ),
        [pltpu.VMEM((3, 16, LANES), f32), pltpu.VMEM((30,) + tile, f32)],
        0,
        (inner, mine, other, outbound, index, coupled, marks, residual, iterate, reg),
    )
    return hess, sums, vectors


def general_step(
    background, obs, connect, live_blocks, scale, others, send_nodes, counts, ref_stiff
):
    f32, i32 = jnp.float32, jnp.int32
    shape = jax.ShapeDtypeStruct
    dom_count = lax.axis_size("dom")
    sub_count = lax.axis_size("sub")
    field_count = lax.axis_size("field")
    owned_nodes = background.shape[1]
    link_slots = send_nodes.shape[3]
    halves = link_slots // LANES
    width = link_slots
    owned_high = owned_nodes // width
    owned_rows = owned_nodes // LANES
    ghost_rows = 3 * sub_count * halves
    table_rows = owned_rows + ghost_rows
    partitions = dom_count * sub_count
    devices = partitions * field_count
    chunk = up_to(3 * halves, SUBS)
    link_tiles = up_to(ghost_rows, SUBS) // SUBS
    left_rows = 3 * PARTS * owned_high + up_to(3 * PARTS * up_to(3 * sub_count, SUBS), 16)
    dims = (dom_count, sub_count, halves)
    links = ("dom", "sub")
    cores = ("dom", "sub", "field")

    outbound = pl.pallas_call(
        functools.partial(start_kernel, dims),
        out_shape=shape((partitions, chunk, LANES), f32),
        in_specs=[SMEM, VMEM, VMEM],
        out_specs=VMEM,
        scratch_shapes=[
            pltpu.VMEM((link_tiles, SUBS, LANES), i32),
            pltpu.VMEM((3, link_tiles, SUBS, LANES), f32),
            pltpu.VMEM((3, owned_rows, LANES), f32),
        ],
    )(counts, send_nodes, background)
    arrived = lax.all_to_all(outbound, links, 0, 0, tiled=True)

    coupled, vectors, owned, outbound = pl.pallas_call(
        functools.partial(forward_kernel, dims),
        compiler_params=PARAMS,
        out_shape=(
            shape((30, SUBS, LANES), f32),
            shape((5, SUBS, LANES), f32),
            shape((3, owned_high, width), f32),
            shape((devices, chunk, LANES), f32),
        ),
        in_specs=[SMEM, SMEM] + [VMEM] * 8,
        out_specs=(VMEM,) * 4,
        scratch_shapes=[
            pltpu.VMEM((3, table_rows, LANES), f32),
            pltpu.VMEM((10, SUBS, LANES), i32),
            pltpu.VMEM((30, SUBS, LANES), f32),
            pltpu.VMEM((3 * PARTS, 10, SUBS, LANES), f32),
            pltpu.VMEM((left_rows, width), f32),
        ],
    )(
        live_blocks,
        ref_stiff,
        background,
        arrived,
        connect,
        scale,
        *others,
    )
    swapped = lax.ppermute(
        owned, "field", [(i, (i + 1) % field_count) for i in range(field_count)]
    )
    arrived = lax.all_to_all(outbound, cores, 0, 0, tiled=True)

    weighted, outbound = pl.pallas_call(
        functools.partial(owner_kernel, dims),
        compiler_params=PARAMS,
        out_shape=(
            shape((3, owned_rows, LANES), f32),
            shape((partitions, chunk, LANES), f32),
        ),
        in_specs=[SMEM] + [VMEM] * 5,
        out_specs=(VMEM,) * 2,
        scratch_shapes=[
            pltpu.VMEM((link_tiles, SUBS, LANES), i32),
            pltpu.VMEM((3, link_tiles, SUBS, LANES), f32),
        ],
    )(counts, send_nodes, owned, swapped, arrived, obs)
    arrived = lax.all_to_all(outbound, links, 0, 0, tiled=True)

    hess, sums = pl.pallas_call(
        functools.partial(adjoint_kernel, dims),
        compiler_params=PARAMS,
        out_shape=(shape((SUBS, LANES), f32), shape((devices, SUMS, LANES), f32)),
        in_specs=[VMEM] * 5,
        out_specs=(VMEM,) * 2,
        scratch_shapes=[
            pltpu.VMEM((3, table_rows, LANES), f32),
            pltpu.VMEM((10, SUBS, LANES), i32),
            pltpu.VMEM((10, 3, SUBS, LANES), f32),
        ],
    )(weighted, arrived, connect, coupled, vectors)
    return hess, sums, vectors


def on_device(
    background,
    obs_weight,
    connect,
    live_blocks,
    elem_scale,
    reg_weight,
    iterate,
    residual,
    direction,
    send_nodes,
    send_count,
    ref_stiff,
):
    f32 = jnp.float32
    shape = jax.ShapeDtypeStruct
    tiled = lambda x: x.reshape(-1, LANES)
    scale, reg, guess, remain, search = map(
        tiled, (elem_scale, reg_weight, iterate, residual, direction)
    )
    obs = tiled(obs_weight)
    counts = jnp.swapaxes(send_count, 1, 2)
    two = lax.axis_size("sub") == 2 and lax.axis_size("field") == 2
    paired = two and send_nodes.shape[3] == 2 * LANES
    hess, sums, vectors = (pair_step if paired else general_step)(
        background,
        obs,
        connect,
        live_blocks,
        scale,
        (search, remain, guess, reg),
        send_nodes,
        counts,
        ref_stiff,
    )
    cores = ("dom", "sub", "field")
    sums = lax.all_to_all(sums, cores, 0, 0, tiled=True)

    results = pl.pallas_call(
        update_kernel,
        compiler_params=PARAMS,
        out_shape=(shape((SUBS, LANES), f32),) * 3,
        in_specs=[VMEM] * 3,
        out_specs=(VMEM,) * 3,
    )(sums, hess, vectors)
    return tuple(x.reshape(-1) for x in results)


def solution(mesh):
    placed = (
        P(None, ("groups", "dom", "sub")),
        P(("groups", "dom", "sub")),
        P(None, ("groups", "dom", "sub", "field")),
        P(("groups", "dom", "sub", "field")),
        P(("groups", "dom", "sub", "field")),
        P(("groups", "dom", "sub", "field")),
        P(("groups", "dom", "sub", "field")),
        P(("groups", "dom", "sub", "field")),
        P(("groups", "dom", "sub", "field")),
        P(("groups", "dom", "sub"), None, None, None),
        P(("groups", "dom", "sub"), None, None),
        P(),
    )
    return jax.shard_map(
        on_device,
        mesh=mesh,
        in_specs=placed,
        out_specs=(
            P(("groups", "dom", "sub", "field")),
            P(("groups", "dom", "sub", "field")),
            P(("groups", "dom", "sub", "field")),
        ),
        check_vma=False,
    )
```

```python
import functools

import jax
import jax.numpy as jnp
from jax import lax
from jax.experimental import pallas as pl
from jax.experimental.pallas import tpu as pltpu
from jax.sharding import PartitionSpec as P

BLK = 128
LANES = 128
SUBS = 8
PARTS = 2
UNROLL = 10
SUMS = 4
LANE_BITS = 7

VMEM = pl.BlockSpec(memory_space=pltpu.VMEM)
SMEM = pl.BlockSpec(memory_space=pltpu.SMEM)
PARAMS = pltpu.CompilerParams(vmem_limit_bytes=16 * 2**20)


def up_to(count, step):
    return -(-count // step) * step


def lookup(table, rows, index, store, begin=None, first=0, comps=3, skip=()):
    def one(tile):
        entry = index[tile]
        high = lax.shift_right_logical(entry, LANE_BITS)
        low = entry & (LANES - 1)
        found = [0.0 if begin is None else begin(tile, c) for c in range(comps)]
        for row in range(rows):
            if row in skip:
                continue
            here = high == first + row
            for c in range(comps):
                line = jnp.broadcast_to(table[c, row : row + 1, :], (SUBS, LANES))
                value = jnp.take_along_axis(
                    line, low, axis=1, mode="promise_in_bounds"
                )
                found[c] = jnp.where(here, value, found[c])
        for c in range(comps):
            store(tile, c, found[c])

    def step(tile, carry):
        one(tile)
        return carry

    if index.shape[0] == 1:
        one(0)
    else:
        lax.fori_loop(0, index.shape[0], step, 0, unroll=min(2 if rows > 16 else 5, index.shape[0]))


def split_parts(value, count=PARTS):
    pieces = []
    for _ in range(count - 1):
        piece = value.astype(jnp.bfloat16).astype(jnp.float32)
        pieces.append(piece)
        value = value - piece
    pieces.append(value.astype(jnp.bfloat16).astype(jnp.float32))
    return pieces


def spread(line, rows):
    return jnp.broadcast_to(line, (rows, LANES)).astype(jnp.bfloat16)


def row_numbers(rows):
    row = lax.broadcasted_iota(jnp.int32, (rows, LANES), 0)
    return row.astype(jnp.float32).astype(jnp.bfloat16)


def one_hot_pair(lines, index, owned_high, ghost_high, width):
    none = jnp.zeros((), jnp.bfloat16)
    unit = jnp.ones((), jnp.bfloat16)
    high = index // width
    low = (index & (width - 1)).astype(jnp.float32)
    here = row_numbers(owned_high) == spread(high.astype(jnp.float32), owned_high)
    blocks = [jnp.where(here, spread(x, owned_high), none) for x in lines]
    if ghost_high:
        row = lax.broadcasted_iota(jnp.int32, (ghost_high, LANES), 0) + owned_high
        here = row == jnp.broadcast_to(high, row.shape)
        rest = [jnp.where(here, jnp.broadcast_to(x, row.shape), 0.0) for x in lines]
        spare = up_to(len(lines) * ghost_high, 16) - len(lines) * ghost_high
        if spare:
            rest.append(jnp.zeros((spare, LANES), jnp.float32))
        blocks.append(jnp.concatenate(rest, axis=0).astype(jnp.bfloat16))
    left = jnp.concatenate(blocks, axis=0)
    right = jnp.where(row_numbers(width) == spread(low, width), unit, none)
    return left, right


def contract(left, right):
    return lax.dot_general(
        left, right, (((1,), (1,)), ((), ())), preferred_element_type=jnp.float32
    )


def link_rows(sub_count, halves):
    return [
        (o, t, h, (o * sub_count + t) * halves + h)
        for o in range(3)
        for t in range(sub_count)
        for h in range(halves)
    ]


def load_links(nodes, index, sub_count, halves):
    for o, t, h, row in link_rows(sub_count, halves):
        index[row // SUBS, row % SUBS : row % SUBS + 1, :] = nodes[
            0, o, t : t + 1, h * LANES : (h + 1) * LANES
        ]
    for row in range(3 * sub_count * halves, index.shape[0] * SUBS):
        index[row // SUBS, row % SUBS : row % SUBS + 1, :] = jnp.zeros((1, LANES), jnp.int32)


def open_lanes(counts, o, t, h):
    lane = lax.broadcasted_iota(jnp.int32, (1, LANES), 1) + h * LANES
    return lane < counts[0, t, o]


def send_links(table, table_rows, counts, index, values, out, dom_count, sub_count, halves):
    def store(tile, c, value):
        values[c, tile] = value

    lookup(table, table_rows, index, store)

    def clear(p, carry):
        out[p] = jnp.zeros(out.shape[1:], jnp.float32)
        return carry

    lax.fori_loop(0, out.shape[0], clear, 0)
    dom = lax.axis_index("dom")
    for o in range(3):
        place = dom + o - 1

        @pl.when((place >= 0) & (place < dom_count))
        def _():
            for t in range(sub_count):
                for h in range(halves):
                    row = (o * sub_count + t) * halves + h
                    here = open_lanes(counts, o, t, h)
                    for c in range(3):
                        line = values[c, row // SUBS, row % SUBS : row % SUBS + 1, :]
                        out[place * sub_count + t, c * halves + h : c * halves + h + 1, :] = (
                            jnp.where(here, line, 0.0)
                        )


def fill_ghosts(table, first, arrived, dom_count, sub_count, halves):
    dom = lax.axis_index("dom")
    for o in range(3):
        place = dom + o - 1
        inside = (place >= 0) & (place < dom_count)
        safe = jnp.clip(place, 0, dom_count - 1)
        for t in range(sub_count):
            chunk = arrived[safe * sub_count + t]
            chunk = jnp.where(inside, chunk, 0.0)
            for c in range(3):
                row = first + (o * sub_count + t) * halves
                table[c, row : row + halves, :] = chunk[c * halves : (c + 1) * halves, :]


def start_kernel(dims, counts, nodes, background, out, index, values, table):
    dom_count, sub_count, halves = dims
    rows = background.shape[1] // LANES
    for c in range(3):
        for r in range(rows):
            table[c, r : r + 1, :] = background[c : c + 1, r * LANES : (r + 1) * LANES]
    load_links(nodes, index, sub_count, halves)
    send_links(table, rows, counts, index, values, out, dom_count, sub_count, halves)


def load_index(connect, index):
    for k in range(10):
        for b in range(SUBS):
            index[k, b : b + 1, :] = connect[k : k + 1, b * LANES : (b + 1) * LANES]


def couple(live, stiff, scale, others, state, coupled, vectors, pieces):
    element_vectors(live, scale, others, vectors)
    forward_terms(stiff, state, coupled, vectors, pieces)


def live_mask(blocks):
    element = (
        lax.broadcasted_iota(jnp.int32, (SUBS, LANES), 0) * LANES
        + lax.broadcasted_iota(jnp.int32, (SUBS, LANES), 1)
    )
    return (element < BLK * blocks).astype(jnp.float32)


def element_vectors(live, scale, others, vectors):
    direction, residual, iterate, reg = others
    mask = live_mask(live[0])
    search = mask * direction[...]
    vectors[0] = search
    vectors[1] = mask * residual[...]
    vectors[2] = mask * iterate[...]
    vectors[3] = reg[...] * search
    vectors[4] = mask * scale[...]


def forward_terms(stiff, state, coupled, vectors, pieces):
    search, factor = vectors[0], vectors[4]
    for c in range(3):
        sums = [None] * 10
        for j in range(30):
            value = state[j]
            for k in range(10):
                term = stiff[c * 10 + k, j] * value
                sums[k] = term if j == 0 else sums[k] + term
        for k in range(10):
            result = factor * sums[k]
            coupled[c * 10 + k] = result
            for part, piece in enumerate(split_parts(search * result)):
                pieces[part * 3 + c, k] = piece


def assemble(pieces, index, total, owned_high, ghost_high, width):
    total[...] = jnp.zeros_like(total)

    def scatter(k, carry):
        pairs = [
            one_hot_pair(
                [pieces[q, k, b : b + 1, :] for q in range(3 * PARTS)],
                index[k, b : b + 1, :],
                owned_high,
                ghost_high,
                width,
            )
            for b in range(SUBS)
        ]
        total[...] += contract(*[jnp.concatenate(x, axis=1) for x in zip(*pairs)])
        return carry

    lax.fori_loop(0, 10, scatter, 0, unroll=UNROLL)


def summed(total, first, step, count):
    value = None
    for part in reversed(range(PARTS)):
        base = first + part * 3 * step
        piece = total[base : base + count, :]
        value = piece if value is None else value + piece
    return value


def forward_kernel(
    dims,
    live,
    stiff,
    background,
    arrived,
    connect,
    scale,
    direction,
    residual,
    iterate,
    reg,
    coupled,
    vectors,
    owned,
    outbound,
    table,
    index,
    state,
    pieces,
    total,
):
    dom_count, sub_count, halves = dims
    width = halves * LANES
    rows = background.shape[1] // LANES
    owned_high = background.shape[1] // width
    ghost_rows = 3 * sub_count * halves
    for c in range(3):
        for r in range(rows):
            table[c, r : r + 1, :] = background[c : c + 1, r * LANES : (r + 1) * LANES]
    fill_ghosts(table, rows, arrived, dom_count, sub_count, halves)
    load_index(connect, index)

    def keep(k, c, value):
        state[c * 10 + k] = value

    lookup(table, rows + ghost_rows, index, keep)
    couple(
        live,
        stiff,
        scale,
        (direction, residual, iterate, reg),
        state,
        coupled,
        vectors,
        pieces,
    )
    ghost_high = up_to(3 * sub_count, SUBS)
    assemble(pieces, index, total, owned_high, ghost_high, width)

    def clear(p, carry):
        outbound[p] = jnp.zeros(outbound.shape[1:], jnp.float32)
        return carry

    lax.fori_loop(0, outbound.shape[0], clear, 0)
    dom = lax.axis_index("dom")
    fields = outbound.shape[0] // (dom_count * sub_count)
    ghost = [None] * 3
    for c in range(3):
        owned[c] = summed(total, c * owned_high, owned_high, owned_high)
        ghost[c] = summed(
            total, 3 * PARTS * owned_high + c * ghost_high, ghost_high, 3 * sub_count
        )
    for o in range(3):
        place = dom + o - 1

        @pl.when((place >= 0) & (place < dom_count))
        def _():
            for t in range(sub_count):
                for c in range(3):
                    for h in range(halves):
                        line = ghost[c][
                            o * sub_count + t : o * sub_count + t + 1,
                            h * LANES : (h + 1) * LANES,
                        ]
                        spot = c * halves + h
                        for f in range(fields):
                            outbound[
                                (place * sub_count + t) * fields + f, spot : spot + 1, :
                            ] = line


def owner_kernel(
    dims,
    counts,
    nodes,
    mine,
    other,
    arrived,
    obs,
    weighted,
    out,
    index,
    values,
):
    dom_count, sub_count, halves = dims
    width = halves * LANES
    fields = arrived.shape[0] // (dom_count * sub_count)
    owned_high = mine.shape[1]
    load_links(nodes, index, sub_count, halves)
    dom = lax.axis_index("dom")
    pairs = []
    for o in range(3):
        place = dom + o - 1
        inside = (place >= 0) & (place < dom_count)
        safe = jnp.clip(place, 0, dom_count - 1)
        for t in range(sub_count):
            chunk = arrived[(safe * sub_count + t) * fields]
            for f in range(1, fields):
                chunk = chunk + arrived[(safe * sub_count + t) * fields + f]
            chunk = jnp.where(inside, chunk, 0.0)
            split = split_parts(chunk)
            for h in range(halves):
                row = (o * sub_count + t) * halves + h
                here = open_lanes(counts, o, t, h)
                lines = [
                    jnp.where(here, split[part][c * halves + h : c * halves + h + 1, :], 0.0)
                    for part in range(PARTS)
                    for c in range(3)
                ]
                a, m = one_hot_pair(lines, index[row // SUBS, row % SUBS : row % SUBS + 1, :], owned_high, 0, width)
                pairs.append((a, m))
    total = contract(*[jnp.concatenate(x, axis=1) for x in zip(*pairs)])
    for c in range(3):
        value = mine[c] + other[c]
        landed = None
        for part in reversed(range(PARTS)):
            base = (part * 3 + c) * owned_high
            piece = total[base : base + owned_high, :]
            landed = piece if landed is None else landed + piece
        value = value + landed
        for h in range(halves):
            weight = obs[pl.ds(h, owned_high, stride=halves), :]
            weighted[c, pl.ds(h, owned_high, stride=halves), :] = (
                weight * value[:, h * LANES : (h + 1) * LANES]
            )
    rows = owned_high * halves
    send_links(weighted, rows, counts, index, values, out, dom_count, sub_count, halves)


def adjoint_kernel(
    dims, weighted, arrived, connect, coupled, vectors, hess, sums, table, index, pulled
):
    dom_count, sub_count, halves = dims
    rows = weighted.shape[1]
    table[:, 0:rows, :] = weighted[...]
    fill_ghosts(table, rows, arrived, dom_count, sub_count, halves)
    load_index(connect, index)

    def keep(k, c, value):
        pulled[k, c] = value

    lookup(table, rows + 3 * sub_count * halves, index, keep)
    search, remain = vectors[0], vectors[1]
    image = None
    for c in range(3):
        for k in range(10):
            term = coupled[c * 10 + k] * pulled[k, c]
            image = term if image is None else image + term
    image = image + vectors[3]
    hess[...] = image
    for i, product in enumerate(
        (remain * remain, search * image, remain * image, image * image)
    ):
        line = jnp.sum(product, axis=0, keepdims=True)
        for p in range(sums.shape[0]):
            sums[p, i : i + 1, :] = line


def update_kernel(sums, hess, vectors, iterate_out, residual_out, direction_out):
    totals = []
    for i in range(4):
        line = sums[0, i : i + 1, :]
        for p in range(1, sums.shape[0]):
            line = line + sums[p, i : i + 1, :]
        line = jnp.sum(line, axis=1, keepdims=True)
        totals.append(jnp.broadcast_to(line, (SUBS, LANES)))
    squared_before, curvature_sum, cross_term, image_square = totals
    search, remain, guess = vectors[0], vectors[1], vectors[2]
    step_length = squared_before / curvature_sum
    squared_after = (
        squared_before
        - 2.0 * step_length * cross_term
        + step_length * step_length * image_square
    )
    residual_next = remain - step_length * hess[...]
    iterate_out[...] = guess + step_length * search
    residual_out[...] = residual_next
    direction_out[...] = residual_next + squared_after / squared_before * search


def own_table(source, table):
    for c in range(3):
        for r in range(source.shape[1] // LANES):
            table[c, r : r + 1, :] = source[c : c + 1, r * LANES : (r + 1) * LANES]


def link_line(nodes, o, k, h):
    zero = nodes[0, o, 0:1, h * LANES : (h + 1) * LANES]
    one = nodes[0, o, 1:2, h * LANES : (h + 1) * LANES]
    return jnp.where((lax.axis_index("sub") ^ k) == 0, zero, one)


def link_limit(counts, o, k):
    return counts[0, lax.axis_index("sub") ^ k, o]


def link_tile(nodes, tile, links):
    tile[0] = jnp.zeros((SUBS, LANES), jnp.int32)
    for i, (o, k) in enumerate(links):
        for h in range(2):
            tile[0, 2 * i + h : 2 * i + h + 1, :] = link_line(nodes, o, k, h)


def pair_start_kernel(counts, nodes, background, out, index, table):
    step = jnp.where(lax.axis_index("field") == 0, 2, 0)
    links = ((step, 0), (step, 1), (1, 1))
    own_table(background, table)
    link_tile(nodes, index, links)
    row = lax.broadcasted_iota(jnp.int32, (SUBS, LANES), 0)
    slot = lax.broadcasted_iota(jnp.int32, (SUBS, LANES), 1) + row % 2 * LANES
    limit = jnp.zeros((SUBS, LANES), jnp.int32)
    for i, (o, k) in enumerate(links):
        limit = jnp.where(row // 2 == i, link_limit(counts, o, k), limit)

    def keep(tile, c, value):
        out[c] = jnp.where(slot < limit, value, 0.0)

    lookup(table, table.shape[1], index, keep)


BLOCKS = ((0, 0), (0, 1), (1, 0), (0, 2), (1, 1), (2, 0))


NOBODY = (4, 5)


def pair_ghosts(dom_count, mine, other, middle, table):
    dom = lax.axis_index("dom")
    first = lax.axis_index("field") == 0
    for c in range(3):
        below = jnp.where(first, mine[c], other[c])
        above = jnp.where(first, other[c], mine[c])
        below = jnp.where(dom > 0, below, 0.0)
        above = jnp.where(dom < dom_count - 1, above, 0.0)
        table[c, 0:4, :] = below[0:4, :]
        table[c, 6:8, :] = middle[c, 4:6, :]
        table[c, 8:12, :] = above[0:4, :]


def pair_copy_kernel(source, out):
    out[...] = source[...]


def pair_join_kernel(straight, slanted, out):
    for c in range(3):
        out[c, 0:4, :] = straight[c, 0:4, :]
        out[c, 4:8, :] = slanted[c, 0:4, :]


def pair_own_kernel(
    link_slots,
    background,
    connect,
    stiff,
    scale,
    direction,
    index,
    partial,
    wide,
    vectors,
    table,
):
    vectors[0] = direction[...]
    vectors[1] = scale[...]
    wide[...] = jnp.zeros_like(wide)
    size = stiff.shape[0]
    split = split_parts(stiff[...], 3)
    for i, (piece, _) in enumerate(BLOCKS):
        wide[0:size, i * 32 : i * 32 + size] = split[piece]
    sub = lax.axis_index("sub")
    own_table(background, table)
    load_index(connect, index)
    owned_nodes = background.shape[1]
    for k in range(10):
        entry = index[k]
        index[k] = jnp.where(entry >= owned_nodes, entry ^ (sub * link_slots), entry)

    def keep(k, c, value):
        partial[c * 10 + k] = value

    lookup(table, table.shape[1], index, keep)


def pair_forward_kernel(
    dom_count,
    wide,
    partial,
    index,
    mine,
    other,
    middle,
    live,
    vectors,
    coupled,
    marks,
    kept,
    sent,
    ghosts,
    state,
    pieces,
    total,
):
    owned_high = kept.shape[1] // 2 - SUBS // 2
    pair_ghosts(dom_count, mine, other, middle, ghosts)

    def begin(k, c):
        return partial[c * 10 + k]

    def keep(k, c, value):
        at = pl.multiple_of((c * 10 + k) * SUBS, SUBS)
        state[0, pl.ds(at, SUBS), :] = value

    lookup(ghosts, 12, index, keep, begin, 2 * owned_high, skip=NOBODY)
    spare = state.shape[1] - 30 * SUBS
    state[0, 30 * SUBS :, :] = jnp.zeros((spare, LANES), jnp.float32)
    weights = wide[...].astype(jnp.bfloat16)
    for b in range(0, SUBS, 2):
        lines = jnp.concatenate(
            [state[0, pl.ds(b + i, 32, stride=SUBS), :] for i in range(2)], axis=1
        )
        split = [x.astype(jnp.bfloat16) for x in split_parts(lines, 3)]
        product = lax.dot_general(
            weights,
            jnp.concatenate([split[his] for _, his in BLOCKS], axis=0),
            (((1,), (0,)), ((), ())),
            preferred_element_type=jnp.float32,
        )
        for i in range(2):
            state[1, pl.ds(b + i, 32, stride=SUBS), :] = product[
                :, i * LANES : (i + 1) * LANES
            ]
    mask = live_mask(live[...])
    search, factor = mask * vectors[0], mask * vectors[1]
    marks[0] = search
    marks[1] = mask
    for c in range(3):
        for k in range(10):
            at = (c * 10 + k) * SUBS
            result = factor * state[1, at : at + SUBS, :]
            coupled[c * 10 + k] = result
            for part, piece in enumerate(split_parts(search * result)):
                pieces[part * 3 + c, k] = piece
    width = 2 * LANES
    assemble(pieces, index, total, owned_high, SUBS, width)
    first = lax.axis_index("field") == 0
    base = 2 * owned_high
    for c in range(3):
        own = summed(total, c * owned_high, owned_high, owned_high)
        ghost = summed(total, 3 * PARTS * owned_high + c * SUBS, SUBS, SUBS)
        for h in range(2):
            half = own[:, h * LANES : (h + 1) * LANES]
            kept[c, h * owned_high : (h + 1) * owned_high, :] = half
            sent[c, h * owned_high : (h + 1) * owned_high, :] = half
            lines = ghost[:, h * LANES : (h + 1) * LANES]
            for k in range(2):
                below, above = lines[k : k + 1, :], lines[4 + k : 5 + k, :]
                at = base + 2 * k + h
                kept[c, at : at + 1, :] = jnp.where(first, above, below)
                sent[c, at : at + 1, :] = jnp.where(first, below, above)
            for out in (kept, sent):
                out[c, base + 4 + h : base + 5 + h, :] = lines[3:4, :]
                out[c, base + 6 + h : base + 7 + h, :] = jnp.zeros((1, LANES), jnp.float32)


def pair_fixed_kernel(counts, nodes, obs, fixed, index, weights):
    rows = obs.shape[0]
    weights[0] = obs[...]
    link_tile(nodes, index, ((0, 1), (1, 1), (2, 1)))
    fixed[3] = index[0].astype(jnp.float32)

    def keep_weight(tile, c, value):
        fixed[2] = value

    lookup(weights, rows, index, keep_weight, comps=1)
    fixed[1] = jnp.full((SUBS, LANES), -1.0, jnp.float32)
    lane = lax.broadcasted_iota(jnp.int32, (1, LANES), 1)
    for o in range(3):
        for k in range(2):
            for h in range(2):
                at = (o * 2 + k) * 2 + h
                here = lane + h * LANES < link_limit(counts, o, k)
                fixed[at // SUBS, at % SUBS : at % SUBS + 1, :] = jnp.where(
                    here, link_line(nodes, o, k, h), -1
                ).astype(jnp.float32)


def pair_sum_kernel(fixed, kept, came, own, link, index, table):
    rows = own.shape[1]
    half = rows // 2
    for c in range(3):
        both = kept[c, 0:rows, :] + came[c, 0:rows, :]
        own[c] = both
        for h in range(2):
            table[c, pl.ds(h, half, stride=2), :] = both[h * half : (h + 1) * half]
    index[0] = fixed[3].astype(jnp.int32)

    def keep(tile, c, value):
        link[c] = value

    lookup(table, rows, index, keep)
    for c in range(3):
        link[c, 6:8, :] = (
            kept[c, rows + 4 : rows + 6, :] + came[c, rows + 4 : rows + 6, :]
        )
        link[3 + c] = fixed[c]


def landing(nodes, lines, owned_high, width):
    pairs = []
    for (o, k), source in lines:
        for h in range(2):
            at = (o * 2 + k) * 2 + h
            entry = nodes[at // SUBS, at % SUBS : at % SUBS + 1, :].astype(jnp.int32)
            values = [source(c, h) for c in range(3)]
            split = [split_parts(v) for v in values]
            pairs.append(
                one_hot_pair(
                    [split[c][part] for part in range(PARTS) for c in range(3)],
                    entry,
                    owned_high,
                    0,
                    width,
                )
            )
    return contract(*[jnp.concatenate(x, axis=1) for x in zip(*pairs)])


def pair_owner_kernel(
    dom_count,
    own,
    link,
    mine,
    other,
    came,
    obs,
    weighted,
    out,
    total,
    index,
    table,
):
    rows = own.shape[1]
    owned_high = rows // 2
    width = 2 * LANES
    dom = lax.axis_index("dom")
    first = lax.axis_index("field") == 0

    def pick(here, there, inside):
        def line(k):
            def get(c, h):
                at = 2 * k + h
                return jnp.where(
                    inside, jnp.where(first, here(c, at), there(c, at)), 0.0
                )

            return get

        return line

    def row_of(tiles, base, shift):
        return lambda c, at: tiles[base + c, shift + at : shift + at + 1, :]

    part, fixed, his_fixed = link.at[0:3], link.at[3:6], came.at[3:6]
    low, high = dom > 0, dom < dom_count - 1
    mine_at, other_at = row_of(mine, 0, 0), row_of(other, 0, 0)
    his_mine, his_other = row_of(mine, 0, 4), row_of(other, 0, 4)
    below = pick(mine_at, other_at, low)
    above = pick(other_at, mine_at, high)
    his_below = pick(his_mine, his_other, low)
    his_above = pick(his_other, his_mine, high)
    own_middle, his_middle = row_of(part, 0, 6), row_of(came, 0, 6)
    own_lines = (
        ((0, 0), below(0)),
        ((0, 1), his_below(1)),
        ((1, 1), his_middle),
        ((2, 0), above(0)),
        ((2, 1), his_above(1)),
    )
    his_lines = (
        ((0, 0), his_below(0)),
        ((0, 1), below(1)),
        ((1, 1), own_middle),
        ((2, 0), his_above(0)),
        ((2, 1), above(1)),
    )
    total[0] = landing(fixed, own_lines, owned_high, width)
    total[1] = landing(his_fixed, his_lines, owned_high, width)
    for c in range(3):
        landed = summed(total.at[0], c * owned_high, owned_high, owned_high)
        his = summed(total.at[1], c * owned_high, owned_high, owned_high)
        for h in range(2):
            at = pl.ds(h, owned_high, stride=2)
            value = own[c, h * owned_high : (h + 1) * owned_high, :]
            value = obs[at, :] * (value + landed[:, h * LANES : (h + 1) * LANES])
            weighted[c, at, :] = value
            table[c, at, :] = value
            table[c, pl.ds(rows + h, owned_high, stride=2), :] = his[
                :, h * LANES : (h + 1) * LANES
            ]

    def node(tiles, o, k, h):
        at = (o * 2 + k) * 2 + h
        return tiles[at // SUBS, at % SUBS : at % SUBS + 1, :].astype(jnp.int32)

    index[0] = jnp.full((SUBS, LANES), -1, jnp.int32)
    index[1] = jnp.zeros((SUBS, LANES), jnp.int32)
    shift = rows * LANES
    for h in range(2):
        line = jnp.where(first, node(fixed, 2, 0, h), node(fixed, 0, 0, h))
        index[0, h : h + 1, :] = line
        for at, line in (
            (2, jnp.where(first, node(his_fixed, 2, 1, h), node(his_fixed, 0, 1, h))),
            (4, node(his_fixed, 1, 1, h)),
        ):
            index[0, at + h : at + h + 1, :] = jnp.where(line < 0, line, line + shift)
    is_open = index[0] >= 0
    index[0] = jnp.maximum(index[0], 0)
    row = lax.broadcasted_iota(jnp.int32, (SUBS, LANES), 0)

    def lined_up(tile):
        lines = []
        for h in range(2):
            lines.append(jnp.where(first, tile[4 + h : 5 + h, :], tile[h : h + 1, :]))
        lines += [tile[2:3, :], tile[3:4, :]]
        blank = jnp.zeros((2, LANES), jnp.float32)
        return jnp.concatenate([blank] + lines + [blank], axis=0)

    weight = lined_up(his_fixed[2])

    def keep(tile, c, value):
        value = jnp.where(row < 2, value, weight * (lined_up(came[c]) + value))
        out[c] = jnp.where(is_open, value, 0.0)

    lookup(table, 2 * rows, index.at[0:1], keep)


def pair_near_kernel(weighted, index, coupled, near, pulled):
    def keep(k, c, value):
        pulled[c * 10 + k] = value

    lookup(weighted, weighted.shape[1], index, keep)
    image = None
    for i in range(30):
        term = coupled[i] * pulled[i]
        image = term if image is None else image + term
    near[...] = image


def write_sums(search, remain, image, sums):
    for i, product in enumerate(
        (remain * remain, search * image, remain * image, image * image)
    ):
        line = jnp.sum(product, axis=0, keepdims=True)
        for p in range(sums.shape[0]):
            sums[p, i : i + 1, :] = line


def pair_adjoint_kernel(
    dom_count,
    rows,
    near,
    mine,
    other,
    middle,
    index,
    coupled,
    marks,
    residual,
    iterate,
    reg,
    hess,
    sums,
    vectors,
    ghosts,
    pulled,
):
    pair_ghosts(dom_count, mine, other, middle, ghosts)

    def keep(k, c, value):
        pulled[c * 10 + k] = value

    lookup(ghosts, 12, index, keep, first=rows, skip=NOBODY)
    image = near[...]
    for i in range(30):
        image = image + coupled[i] * pulled[i]
    search, mask = marks[0], marks[1]
    remain = mask * residual[...]
    image = image + reg[...] * search
    hess[...] = image
    vectors[0] = search
    vectors[1] = remain
    vectors[2] = mask * iterate[...]
    write_sums(search, remain, image, sums)


def pair_step(background, obs, connect, live_blocks, scale, others, nodes, counts, stiff):
    f32, i32 = jnp.float32, jnp.int32
    shape = jax.ShapeDtypeStruct
    dom_count = lax.axis_size("dom")
    owned_nodes = background.shape[1]
    link_slots = nodes.shape[3]
    rows = owned_nodes // LANES
    owned_high = owned_nodes // link_slots
    tile = (SUBS, LANES)
    swap = [(0, 1), (1, 0)]
    last = dom_count - 1

    def core(d, t, f):
        return (2 * d + t) * 2 + f

    def ring(turn):
        pairs = []
        for t in range(2):
            for d in range(last):
                pairs.append((core(d, t, 0), core(d + 1, t ^ turn, 0)))
                pairs.append((core(d + 1, t, 1), core(d, t ^ turn, 1)))
            pairs.append((core(last, t, 0), core(last, t, 1)))
            pairs.append((core(0, t, 1), core(0, t, 0)))
        return pairs

    left_rows = 3 * PARTS * owned_high + up_to(3 * PARTS * SUBS, 16)

    def across(x):
        return lax.ppermute(x, "field", swap)

    def beside(x):
        return lax.ppermute(x, "sub", swap)

    def along(x, turn=0):
        return lax.ppermute(x, ("dom", "sub", "field"), ring(turn))

    def call(kernel, outs, scratch, smem, args, params=PARAMS):
        return pl.pallas_call(
            kernel,
            compiler_params=params,
            out_shape=outs,
            in_specs=[SMEM] * smem + [VMEM] * (len(args) - smem),
            out_specs=jax.tree.map(lambda x: VMEM, outs),
            scratch_shapes=scratch,
            cost_estimate=pl.CostEstimate(
                flops=2**20, bytes_accessed=2**16, transcendentals=0
            ),
        )(*args)

    packed = call(
        pair_start_kernel,
        shape((3,) + tile, f32),
        [pltpu.VMEM((1,) + tile, i32), pltpu.VMEM((3, rows, LANES), f32)],
        1,
        (counts, nodes, background),
        None,
    )
    straight, slanted = along(packed), along(packed, 1)
    middle = beside(call(pair_copy_kernel, shape((3,) + tile, f32), [], 0, (packed,)))
    direction, residual, iterate, reg = others
    index, partial, wide, vectors = call(
        functools.partial(pair_own_kernel, link_slots),
        (
            shape((10,) + tile, i32),
            shape((30,) + tile, f32),
            shape((32, 32 * len(BLOCKS)), f32),
            shape((2,) + tile, f32),
        ),
        [pltpu.VMEM((3, rows, LANES), f32)],
        0,
        (background, connect, stiff, scale, direction),
    )
    straight, partial = lax.optimization_barrier((straight, partial))
    upper = lax.broadcasted_iota(i32, (3,) + tile, 1) < 2
    mine = jnp.where(upper, straight, slanted)
    other = across(mine)
    coupled, marks, kept, sent = call(
        functools.partial(pair_forward_kernel, dom_count),
        (
            shape((30,) + tile, f32),
            shape((2,) + tile, f32),
            shape((3, rows + SUBS, LANES), f32),
            shape((3, rows + SUBS, LANES), f32),
        ),
        [
            pltpu.VMEM((3, 16, LANES), f32),
            pltpu.VMEM((2, 32 * SUBS, LANES), f32),
            pltpu.VMEM((3 * PARTS, 10) + tile, f32),
            pltpu.VMEM((left_rows, link_slots), f32),
        ],
        0,
        (
            wide,
            partial,
            index,
            mine,
            other,
            middle,
            live_blocks.reshape(1, 1),
            vectors,
        ),
    )
    came = across(sent)
    nodes, _ = lax.optimization_barrier((nodes, sent))
    fixed = call(
        pair_fixed_kernel,
        shape((4,) + tile, f32),
        [pltpu.VMEM((1,) + tile, i32), pltpu.VMEM((1, rows, LANES), f32)],
        1,
        (counts, nodes, obs),
    )
    came, fixed = lax.optimization_barrier((came, fixed))
    linked = kept[:, rows:] + came[:, rows:]
    straight, slanted = along(linked), along(linked, 1)
    own, link = call(
        pair_sum_kernel,
        (shape((3, rows, LANES), f32), shape((6,) + tile, f32)),
        [pltpu.VMEM((1,) + tile, i32), pltpu.VMEM((3, rows, LANES), f32)],
        0,
        (fixed, kept, came),
    )
    came = beside(link)
    straight, slanted, _ = lax.optimization_barrier((straight, slanted, link))
    mine = call(
        pair_join_kernel, shape((3,) + tile, f32), [], 0, (straight, slanted)
    )
    other = across(mine)
    weighted, outbound = call(
        functools.partial(pair_owner_kernel, dom_count),
        (shape((3, rows, LANES), f32), shape((3,) + tile, f32)),
        [
            pltpu.VMEM((2, 3 * PARTS * owned_high, link_slots), f32),
            pltpu.VMEM((2,) + tile, i32),
            pltpu.VMEM((3, 2 * rows, LANES), f32),
        ],
        0,
        (own, link, mine, other, came, obs),
    )
    mine = along(outbound)
    inner = call(
        pair_near_kernel,
        shape(tile, f32),
        [pltpu.VMEM((30,) + tile, f32)],
        0,
        (weighted, index, coupled),
    )
    mine, inner = lax.optimization_barrier((mine, inner))
    other = across(mine)
    hess, sums, vectors = call(
        functools.partial(pair_adjoint_kernel, dom_count, rows),
        (
            shape(tile, f32),
            shape((4 * dom_count, SUMS, LANES), f32),
            shape((3,) + tile, f32),
        ),
        [pltpu.VMEM((3, 16, LANES), f32), pltpu.VMEM((30,) + tile, f32)],
        0,
        (inner, mine, other, outbound, index, coupled, marks, residual, iterate, reg),
    )
    return hess, sums, vectors


def general_step(
    background, obs, connect, live_blocks, scale, others, send_nodes, counts, ref_stiff
):
    f32, i32 = jnp.float32, jnp.int32
    shape = jax.ShapeDtypeStruct
    dom_count = lax.axis_size("dom")
    sub_count = lax.axis_size("sub")
    field_count = lax.axis_size("field")
    owned_nodes = background.shape[1]
    link_slots = send_nodes.shape[3]
    halves = link_slots // LANES
    width = link_slots
    owned_high = owned_nodes // width
    owned_rows = owned_nodes // LANES
    ghost_rows = 3 * sub_count * halves
    table_rows = owned_rows + ghost_rows
    partitions = dom_count * sub_count
    devices = partitions * field_count
    chunk = up_to(3 * halves, SUBS)
    link_tiles = up_to(ghost_rows, SUBS) // SUBS
    left_rows = 3 * PARTS * owned_high + up_to(3 * PARTS * up_to(3 * sub_count, SUBS), 16)
    dims = (dom_count, sub_count, halves)
    links = ("dom", "sub")
    cores = ("dom", "sub", "field")

    outbound = pl.pallas_call(
        functools.partial(start_kernel, dims),
        out_shape=shape((partitions, chunk, LANES), f32),
        in_specs=[SMEM, VMEM, VMEM],
        out_specs=VMEM,
        scratch_shapes=[
            pltpu.VMEM((link_tiles, SUBS, LANES), i32),
            pltpu.VMEM((3, link_tiles, SUBS, LANES), f32),
            pltpu.VMEM((3, owned_rows, LANES), f32),
        ],
    )(counts, send_nodes, background)
    arrived = lax.all_to_all(outbound, links, 0, 0, tiled=True)

    coupled, vectors, owned, outbound = pl.pallas_call(
        functools.partial(forward_kernel, dims),
        compiler_params=PARAMS,
        out_shape=(
            shape((30, SUBS, LANES), f32),
            shape((5, SUBS, LANES), f32),
            shape((3, owned_high, width), f32),
            shape((devices, chunk, LANES), f32),
        ),
        in_specs=[SMEM, SMEM] + [VMEM] * 8,
        out_specs=(VMEM,) * 4,
        scratch_shapes=[
            pltpu.VMEM((3, table_rows, LANES), f32),
            pltpu.VMEM((10, SUBS, LANES), i32),
            pltpu.VMEM((30, SUBS, LANES), f32),
            pltpu.VMEM((3 * PARTS, 10, SUBS, LANES), f32),
            pltpu.VMEM((left_rows, width), f32),
        ],
    )(
        live_blocks,
        ref_stiff,
        background,
        arrived,
        connect,
        scale,
        *others,
    )
    swapped = lax.ppermute(
        owned, "field", [(i, (i + 1) % field_count) for i in range(field_count)]
    )
    arrived = lax.all_to_all(outbound, cores, 0, 0, tiled=True)

    weighted, outbound = pl.pallas_call(
        functools.partial(owner_kernel, dims),
        compiler_params=PARAMS,
        out_shape=(
            shape((3, owned_rows, LANES), f32),
            shape((partitions, chunk, LANES), f32),
        ),
        in_specs=[SMEM] + [VMEM] * 5,
        out_specs=(VMEM,) * 2,
        scratch_shapes=[
            pltpu.VMEM((link_tiles, SUBS, LANES), i32),
            pltpu.VMEM((3, link_tiles, SUBS, LANES), f32),
        ],
    )(counts, send_nodes, owned, swapped, arrived, obs)
    arrived = lax.all_to_all(outbound, links, 0, 0, tiled=True)

    hess, sums = pl.pallas_call(
        functools.partial(adjoint_kernel, dims),
        compiler_params=PARAMS,
        out_shape=(shape((SUBS, LANES), f32), shape((devices, SUMS, LANES), f32)),
        in_specs=[VMEM] * 5,
        out_specs=(VMEM,) * 2,
        scratch_shapes=[
            pltpu.VMEM((3, table_rows, LANES), f32),
            pltpu.VMEM((10, SUBS, LANES), i32),
            pltpu.VMEM((10, 3, SUBS, LANES), f32),
        ],
    )(weighted, arrived, connect, coupled, vectors)
    return hess, sums, vectors


def on_device(
    background,
    obs_weight,
    connect,
    live_blocks,
    elem_scale,
    reg_weight,
    iterate,
    residual,
    direction,
    send_nodes,
    send_count,
    ref_stiff,
):
    f32 = jnp.float32
    shape = jax.ShapeDtypeStruct
    tiled = lambda x: x.reshape(-1, LANES)
    scale, reg, guess, remain, search = map(
        tiled, (elem_scale, reg_weight, iterate, residual, direction)
    )
    obs = tiled(obs_weight)
    counts = jnp.swapaxes(send_count, 1, 2)
    two = lax.axis_size("sub") == 2 and lax.axis_size("field") == 2
    paired = two and send_nodes.shape[3] == 2 * LANES
    hess, sums, vectors = (pair_step if paired else general_step)(
        background,
        obs,
        connect,
        live_blocks,
        scale,
        (search, remain, guess, reg),
        send_nodes,
        counts,
        ref_stiff,
    )
    cores = ("dom", "sub", "field")
    sums = lax.all_to_all(sums, cores, 0, 0, tiled=True)

    results = pl.pallas_call(
        update_kernel,
        compiler_params=PARAMS,
        out_shape=(shape((SUBS, LANES), f32),) * 3,
        in_specs=[VMEM] * 3,
        out_specs=(VMEM,) * 3,
    )(sums, hess, vectors)
    return tuple(x.reshape(-1) for x in results)


def solution(mesh):
    placed = (
        P(None, ("groups", "dom", "sub")),
        P(("groups", "dom", "sub")),
        P(None, ("groups", "dom", "sub", "field")),
        P(("groups", "dom", "sub", "field")),
        P(("groups", "dom", "sub", "field")),
        P(("groups", "dom", "sub", "field")),
        P(("groups", "dom", "sub", "field")),
        P(("groups", "dom", "sub", "field")),
        P(("groups", "dom", "sub", "field")),
        P(("groups", "dom", "sub"), None, None, None),
        P(("groups", "dom", "sub"), None, None),
        P(),
    )
    return jax.shard_map(
        on_device,
        mesh=mesh,
        in_specs=placed,
        out_specs=(
            P(("groups", "dom", "sub", "field")),
            P(("groups", "dom", "sub", "field")),
            P(("groups", "dom", "sub", "field")),
        ),
        check_vma=False,
    )
```

```python
import functools

import jax
import jax.numpy as jnp
from jax import lax
from jax.experimental import pallas as pl
from jax.experimental.pallas import tpu as pltpu
from jax.sharding import PartitionSpec as P

BLK = 128
LANES = 128
SUBS = 8
PARTS = 2
UNROLL = 10
SUMS = 4
LANE_BITS = 7

VMEM = pl.BlockSpec(memory_space=pltpu.VMEM)
SMEM = pl.BlockSpec(memory_space=pltpu.SMEM)
PARAMS = pltpu.CompilerParams(vmem_limit_bytes=16 * 2**20)


def up_to(count, step):
    return -(-count // step) * step


def lookup(table, rows, index, store, begin=None, first=0, comps=3, skip=()):
    def one(tile):
        entry = index[tile]
        high = lax.shift_right_logical(entry, LANE_BITS)
        low = entry & (LANES - 1)
        found = [0.0 if begin is None else begin(tile, c) for c in range(comps)]
        for row in range(rows):
            if row in skip:
                continue
            here = high == first + row
            for c in range(comps):
                line = jnp.broadcast_to(table[c, row : row + 1, :], (SUBS, LANES))
                value = jnp.take_along_axis(
                    line, low, axis=1, mode="promise_in_bounds"
                )
                found[c] = jnp.where(here, value, found[c])
        for c in range(comps):
            store(tile, c, found[c])

    def step(tile, carry):
        one(tile)
        return carry

    if index.shape[0] == 1:
        one(0)
    else:
        lax.fori_loop(0, index.shape[0], step, 0, unroll=min(2 if rows > 16 else 5, index.shape[0]))


def split_parts(value, count=PARTS):
    pieces = []
    for _ in range(count - 1):
        piece = value.astype(jnp.bfloat16).astype(jnp.float32)
        pieces.append(piece)
        value = value - piece
    pieces.append(value.astype(jnp.bfloat16).astype(jnp.float32))
    return pieces


def spread(line, rows):
    return jnp.broadcast_to(line, (rows, LANES)).astype(jnp.bfloat16)


def row_numbers(rows):
    row = lax.broadcasted_iota(jnp.int32, (rows, LANES), 0)
    return row.astype(jnp.float32).astype(jnp.bfloat16)


def one_hot_pair(lines, index, owned_high, ghost_high, width):
    none = jnp.zeros((), jnp.bfloat16)
    unit = jnp.ones((), jnp.bfloat16)
    high = index // width
    low = (index & (width - 1)).astype(jnp.float32)
    here = row_numbers(owned_high) == spread(high.astype(jnp.float32), owned_high)
    blocks = [jnp.where(here, spread(x, owned_high), none) for x in lines]
    if ghost_high:
        row = lax.broadcasted_iota(jnp.int32, (ghost_high, LANES), 0) + owned_high
        here = row == jnp.broadcast_to(high, row.shape)
        rest = [jnp.where(here, jnp.broadcast_to(x, row.shape), 0.0) for x in lines]
        spare = up_to(len(lines) * ghost_high, 16) - len(lines) * ghost_high
        if spare:
            rest.append(jnp.zeros((spare, LANES), jnp.float32))
        blocks.append(jnp.concatenate(rest, axis=0).astype(jnp.bfloat16))
    left = jnp.concatenate(blocks, axis=0)
    right = jnp.where(row_numbers(width) == spread(low, width), unit, none)
    return left, right


def contract(left, right):
    return lax.dot_general(
        left, right, (((1,), (1,)), ((), ())), preferred_element_type=jnp.float32
    )


def link_rows(sub_count, halves):
    return [
        (o, t, h, (o * sub_count + t) * halves + h)
        for o in range(3)
        for t in range(sub_count)
        for h in range(halves)
    ]


def load_links(nodes, index, sub_count, halves):
    for o, t, h, row in link_rows(sub_count, halves):
        index[row // SUBS, row % SUBS : row % SUBS + 1, :] = nodes[
            0, o, t : t + 1, h * LANES : (h + 1) * LANES
        ]
    for row in range(3 * sub_count * halves, index.shape[0] * SUBS):
        index[row // SUBS, row % SUBS : row % SUBS + 1, :] = jnp.zeros((1, LANES), jnp.int32)


def open_lanes(counts, o, t, h):
    lane = lax.broadcasted_iota(jnp.int32, (1, LANES), 1) + h * LANES
    return lane < counts[0, t, o]


def send_links(table, table_rows, counts, index, values, out, dom_count, sub_count, halves):
    def store(tile, c, value):
        values[c, tile] = value

    lookup(table, table_rows, index, store)

    def clear(p, carry):
        out[p] = jnp.zeros(out.shape[1:], jnp.float32)
        return carry

    lax.fori_loop(0, out.shape[0], clear, 0)
    dom = lax.axis_index("dom")
    for o in range(3):
        place = dom + o - 1

        @pl.when((place >= 0) & (place < dom_count))
        def _():
            for t in range(sub_count):
                for h in range(halves):
                    row = (o * sub_count + t) * halves + h
                    here = open_lanes(counts, o, t, h)
                    for c in range(3):
                        line = values[c, row // SUBS, row % SUBS : row % SUBS + 1, :]
                        out[place * sub_count + t, c * halves + h : c * halves + h + 1, :] = (
                            jnp.where(here, line, 0.0)
                        )


def fill_ghosts(table, first, arrived, dom_count, sub_count, halves):
    dom = lax.axis_index("dom")
    for o in range(3):
        place = dom + o - 1
        inside = (place >= 0) & (place < dom_count)
        safe = jnp.clip(place, 0, dom_count - 1)
        for t in range(sub_count):
            chunk = arrived[safe * sub_count + t]
            chunk = jnp.where(inside, chunk, 0.0)
            for c in range(3):
                row = first + (o * sub_count + t) * halves
                table[c, row : row + halves, :] = chunk[c * halves : (c + 1) * halves, :]


def start_kernel(dims, counts, nodes, background, out, index, values, table):
    dom_count, sub_count, halves = dims
    rows = background.shape[1] // LANES
    for c in range(3):
        for r in range(rows):
            table[c, r : r + 1, :] = background[c : c + 1, r * LANES : (r + 1) * LANES]
    load_links(nodes, index, sub_count, halves)
    send_links(table, rows, counts, index, values, out, dom_count, sub_count, halves)


def load_index(connect, index):
    for k in range(10):
        for b in range(SUBS):
            index[k, b : b + 1, :] = connect[k : k + 1, b * LANES : (b + 1) * LANES]


def couple(live, stiff, scale, others, state, coupled, vectors, pieces):
    element_vectors(live, scale, others, vectors)
    forward_terms(stiff, state, coupled, vectors, pieces)


def live_mask(blocks):
    element = (
        lax.broadcasted_iota(jnp.int32, (SUBS, LANES), 0) * LANES
        + lax.broadcasted_iota(jnp.int32, (SUBS, LANES), 1)
    )
    return (element < BLK * blocks).astype(jnp.float32)


def element_vectors(live, scale, others, vectors):
    direction, residual, iterate, reg = others
    mask = live_mask(live[0])
    search = mask * direction[...]
    vectors[0] = search
    vectors[1] = mask * residual[...]
    vectors[2] = mask * iterate[...]
    vectors[3] = reg[...] * search
    vectors[4] = mask * scale[...]


def forward_terms(stiff, state, coupled, vectors, pieces):
    search, factor = vectors[0], vectors[4]
    for c in range(3):
        sums = [None] * 10
        for j in range(30):
            value = state[j]
            for k in range(10):
                term = stiff[c * 10 + k, j] * value
                sums[k] = term if j == 0 else sums[k] + term
        for k in range(10):
            result = factor * sums[k]
            coupled[c * 10 + k] = result
            for part, piece in enumerate(split_parts(search * result)):
                pieces[part * 3 + c, k] = piece


def assemble(pieces, index, total, owned_high, ghost_high, width):
    total[...] = jnp.zeros_like(total)

    def scatter(k, carry):
        pairs = [
            one_hot_pair(
                [pieces[q, k, b : b + 1, :] for q in range(3 * PARTS)],
                index[k, b : b + 1, :],
                owned_high,
                ghost_high,
                width,
            )
            for b in range(SUBS)
        ]
        total[...] += contract(*[jnp.concatenate(x, axis=1) for x in zip(*pairs)])
        return carry

    lax.fori_loop(0, 10, scatter, 0, unroll=UNROLL)


def summed(total, first, step, count):
    value = None
    for part in reversed(range(PARTS)):
        base = first + part * 3 * step
        piece = total[base : base + count, :]
        value = piece if value is None else value + piece
    return value


def forward_kernel(
    dims,
    live,
    stiff,
    background,
    arrived,
    connect,
    scale,
    direction,
    residual,
    iterate,
    reg,
    coupled,
    vectors,
    owned,
    outbound,
    table,
    index,
    state,
    pieces,
    total,
):
    dom_count, sub_count, halves = dims
    width = halves * LANES
    rows = background.shape[1] // LANES
    owned_high = background.shape[1] // width
    ghost_rows = 3 * sub_count * halves
    for c in range(3):
        for r in range(rows):
            table[c, r : r + 1, :] = background[c : c + 1, r * LANES : (r + 1) * LANES]
    fill_ghosts(table, rows, arrived, dom_count, sub_count, halves)
    load_index(connect, index)

    def keep(k, c, value):
        state[c * 10 + k] = value

    lookup(table, rows + ghost_rows, index, keep)
    couple(
        live,
        stiff,
        scale,
        (direction, residual, iterate, reg),
        state,
        coupled,
        vectors,
        pieces,
    )
    ghost_high = up_to(3 * sub_count, SUBS)
    assemble(pieces, index, total, owned_high, ghost_high, width)

    def clear(p, carry):
        outbound[p] = jnp.zeros(outbound.shape[1:], jnp.float32)
        return carry

    lax.fori_loop(0, outbound.shape[0], clear, 0)
    dom = lax.axis_index("dom")
    fields = outbound.shape[0] // (dom_count * sub_count)
    ghost = [None] * 3
    for c in range(3):
        owned[c] = summed(total, c * owned_high, owned_high, owned_high)
        ghost[c] = summed(
            total, 3 * PARTS * owned_high + c * ghost_high, ghost_high, 3 * sub_count
        )
    for o in range(3):
        place = dom + o - 1

        @pl.when((place >= 0) & (place < dom_count))
        def _():
            for t in range(sub_count):
                for c in range(3):
                    for h in range(halves):
                        line = ghost[c][
                            o * sub_count + t : o * sub_count + t + 1,
                            h * LANES : (h + 1) * LANES,
                        ]
                        spot = c * halves + h
                        for f in range(fields):
                            outbound[
                                (place * sub_count + t) * fields + f, spot : spot + 1, :
                            ] = line


def owner_kernel(
    dims,
    counts,
    nodes,
    mine,
    other,
    arrived,
    obs,
    weighted,
    out,
    index,
    values,
):
    dom_count, sub_count, halves = dims
    width = halves * LANES
    fields = arrived.shape[0] // (dom_count * sub_count)
    owned_high = mine.shape[1]
    load_links(nodes, index, sub_count, halves)
    dom = lax.axis_index("dom")
    pairs = []
    for o in range(3):
        place = dom + o - 1
        inside = (place >= 0) & (place < dom_count)
        safe = jnp.clip(place, 0, dom_count - 1)
        for t in range(sub_count):
            chunk = arrived[(safe * sub_count + t) * fields]
            for f in range(1, fields):
                chunk = chunk + arrived[(safe * sub_count + t) * fields + f]
            chunk = jnp.where(inside, chunk, 0.0)
            split = split_parts(chunk)
            for h in range(halves):
                row = (o * sub_count + t) * halves + h
                here = open_lanes(counts, o, t, h)
                lines = [
                    jnp.where(here, split[part][c * halves + h : c * halves + h + 1, :], 0.0)
                    for part in range(PARTS)
                    for c in range(3)
                ]
                a, m = one_hot_pair(lines, index[row // SUBS, row % SUBS : row % SUBS + 1, :], owned_high, 0, width)
                pairs.append((a, m))
    total = contract(*[jnp.concatenate(x, axis=1) for x in zip(*pairs)])
    for c in range(3):
        value = mine[c] + other[c]
        landed = None
        for part in reversed(range(PARTS)):
            base = (part * 3 + c) * owned_high
            piece = total[base : base + owned_high, :]
            landed = piece if landed is None else landed + piece
        value = value + landed
        for h in range(halves):
            weight = obs[pl.ds(h, owned_high, stride=halves), :]
            weighted[c, pl.ds(h, owned_high, stride=halves), :] = (
                weight * value[:, h * LANES : (h + 1) * LANES]
            )
    rows = owned_high * halves
    send_links(weighted, rows, counts, index, values, out, dom_count, sub_count, halves)


def adjoint_kernel(
    dims, weighted, arrived, connect, coupled, vectors, hess, sums, table, index, pulled
):
    dom_count, sub_count, halves = dims
    rows = weighted.shape[1]
    table[:, 0:rows, :] = weighted[...]
    fill_ghosts(table, rows, arrived, dom_count, sub_count, halves)
    load_index(connect, index)

    def keep(k, c, value):
        pulled[k, c] = value

    lookup(table, rows + 3 * sub_count * halves, index, keep)
    search, remain = vectors[0], vectors[1]
    image = None
    for c in range(3):
        for k in range(10):
            term = coupled[c * 10 + k] * pulled[k, c]
            image = term if image is None else image + term
    image = image + vectors[3]
    hess[...] = image
    for i, product in enumerate(
        (remain * remain, search * image, remain * image, image * image)
    ):
        line = jnp.sum(product, axis=0, keepdims=True)
        for p in range(sums.shape[0]):
            sums[p, i : i + 1, :] = line


def update_kernel(sums, hess, vectors, iterate_out, residual_out, direction_out):
    totals = []
    for i in range(4):
        line = sums[0, i : i + 1, :]
        for p in range(1, sums.shape[0]):
            line = line + sums[p, i : i + 1, :]
        line = jnp.sum(line, axis=1, keepdims=True)
        totals.append(jnp.broadcast_to(line, (SUBS, LANES)))
    squared_before, curvature_sum, cross_term, image_square = totals
    search, remain, guess = vectors[0], vectors[1], vectors[2]
    step_length = squared_before / curvature_sum
    squared_after = (
        squared_before
        - 2.0 * step_length * cross_term
        + step_length * step_length * image_square
    )
    residual_next = remain - step_length * hess[...]
    iterate_out[...] = guess + step_length * search
    residual_out[...] = residual_next
    direction_out[...] = residual_next + squared_after / squared_before * search


def own_table(source, table):
    for c in range(3):
        for r in range(source.shape[1] // LANES):
            table[c, r : r + 1, :] = source[c : c + 1, r * LANES : (r + 1) * LANES]


def link_line(nodes, o, k, h):
    zero = nodes[0, o, 0:1, h * LANES : (h + 1) * LANES]
    one = nodes[0, o, 1:2, h * LANES : (h + 1) * LANES]
    return jnp.where((lax.axis_index("sub") ^ k) == 0, zero, one)


def link_limit(counts, o, k):
    return counts[0, lax.axis_index("sub") ^ k, o]


def link_tile(nodes, tile, links):
    tile[0] = jnp.zeros((SUBS, LANES), jnp.int32)
    for i, (o, k) in enumerate(links):
        for h in range(2):
            tile[0, 2 * i + h : 2 * i + h + 1, :] = link_line(nodes, o, k, h)


def pair_start_kernel(counts, nodes, background, out, index, table):
    step = jnp.where(lax.axis_index("field") == 0, 2, 0)
    links = ((step, 0), (step, 1), (1, 1))
    own_table(background, table)
    link_tile(nodes, index, links)
    row = lax.broadcasted_iota(jnp.int32, (SUBS, LANES), 0)
    slot = lax.broadcasted_iota(jnp.int32, (SUBS, LANES), 1) + row % 2 * LANES
    limit = jnp.zeros((SUBS, LANES), jnp.int32)
    for i, (o, k) in enumerate(links):
        limit = jnp.where(row // 2 == i, link_limit(counts, o, k), limit)

    def keep(tile, c, value):
        out[c] = jnp.where(slot < limit, value, 0.0)

    lookup(table, table.shape[1], index, keep)


BLOCKS = ((0, 0), (0, 1), (1, 0), (0, 2), (1, 1), (2, 0))


NOBODY = (4, 5)


def pair_ghosts(dom_count, mine, other, middle, table):
    dom = lax.axis_index("dom")
    first = lax.axis_index("field") == 0
    for c in range(3):
        below = jnp.where(first, mine[c], other[c])
        above = jnp.where(first, other[c], mine[c])
        below = jnp.where(dom > 0, below, 0.0)
        above = jnp.where(dom < dom_count - 1, above, 0.0)
        table[c, 0:4, :] = below[0:4, :]
        table[c, 6:8, :] = middle[c, 4:6, :]
        table[c, 8:12, :] = above[0:4, :]


def pair_copy_kernel(source, out):
    out[...] = source[...]


def pair_join_kernel(straight, slanted, out):
    for c in range(3):
        out[c, 0:4, :] = straight[c, 0:4, :]
        out[c, 4:8, :] = slanted[c, 0:4, :]


def pair_own_kernel(
    link_slots,
    background,
    connect,
    stiff,
    scale,
    direction,
    index,
    partial,
    wide,
    vectors,
    table,
):
    vectors[0] = direction[...]
    vectors[1] = scale[...]
    wide[...] = jnp.zeros_like(wide)
    size = stiff.shape[0]
    split = split_parts(stiff[...], 3)
    for i, (piece, _) in enumerate(BLOCKS):
        wide[0:size, i * 32 : i * 32 + size] = split[piece]
    sub = lax.axis_index("sub")
    own_table(background, table)
    load_index(connect, index)
    owned_nodes = background.shape[1]
    for k in range(10):
        entry = index[k]
        index[k] = jnp.where(entry >= owned_nodes, entry ^ (sub * link_slots), entry)

    def keep(k, c, value):
        partial[c * 10 + k] = value

    lookup(table, table.shape[1], index, keep)


def pair_forward_kernel(
    dom_count,
    wide,
    partial,
    index,
    mine,
    other,
    middle,
    live,
    vectors,
    coupled,
    marks,
    kept,
    sent,
    ghosts,
    state,
    pieces,
    total,
):
    owned_high = kept.shape[1] // 2 - SUBS // 2
    pair_ghosts(dom_count, mine, other, middle, ghosts)

    def begin(k, c):
        return partial[c * 10 + k]

    def keep(k, c, value):
        at = pl.multiple_of((c * 10 + k) * SUBS, SUBS)
        state[0, pl.ds(at, SUBS), :] = value

    lookup(ghosts, 12, index, keep, begin, 2 * owned_high, skip=NOBODY)
    spare = state.shape[1] - 30 * SUBS
    state[0, 30 * SUBS :, :] = jnp.zeros((spare, LANES), jnp.float32)
    weights = wide[...].astype(jnp.bfloat16)
    for b in range(0, SUBS, 2):
        lines = jnp.concatenate(
            [state[0, pl.ds(b + i, 32, stride=SUBS), :] for i in range(2)], axis=1
        )
        split = [x.astype(jnp.bfloat16) for x in split_parts(lines, 3)]
        product = lax.dot_general(
            weights,
            jnp.concatenate([split[his] for _, his in BLOCKS], axis=0),
            (((1,), (0,)), ((), ())),
            preferred_element_type=jnp.float32,
        )
        for i in range(2):
            state[1, pl.ds(b + i, 32, stride=SUBS), :] = product[
                :, i * LANES : (i + 1) * LANES
            ]
    mask = live_mask(live[...])
    search, factor = mask * vectors[0], mask * vectors[1]
    marks[0] = search
    marks[1] = mask
    for c in range(3):
        for k in range(10):
            at = (c * 10 + k) * SUBS
            result = factor * state[1, at : at + SUBS, :]
            coupled[c * 10 + k] = result
            for part, piece in enumerate(split_parts(search * result)):
                pieces[part * 3 + c, k] = piece
    width = 2 * LANES
    assemble(pieces, index, total, owned_high, SUBS, width)
    first = lax.axis_index("field") == 0
    base = 2 * owned_high
    for c in range(3):
        own = summed(total, c * owned_high, owned_high, owned_high)
        ghost = summed(total, 3 * PARTS * owned_high + c * SUBS, SUBS, SUBS)
        for h in range(2):
            half = own[:, h * LANES : (h + 1) * LANES]
            kept[c, h * owned_high : (h + 1) * owned_high, :] = half
            sent[c, h * owned_high : (h + 1) * owned_high, :] = half
            lines = ghost[:, h * LANES : (h + 1) * LANES]
            for k in range(2):
                below, above = lines[k : k + 1, :], lines[4 + k : 5 + k, :]
                at = base + 2 * k + h
                kept[c, at : at + 1, :] = jnp.where(first, above, below)
                sent[c, at : at + 1, :] = jnp.where(first, below, above)
            for out in (kept, sent):
                out[c, base + 4 + h : base + 5 + h, :] = lines[3:4, :]
                out[c, base + 6 + h : base + 7 + h, :] = jnp.zeros((1, LANES), jnp.float32)


def pair_fixed_kernel(counts, nodes, obs, fixed, index, weights):
    rows = obs.shape[0]
    weights[0] = obs[...]
    link_tile(nodes, index, ((0, 1), (1, 1), (2, 1)))
    fixed[3] = index[0].astype(jnp.float32)

    def keep_weight(tile, c, value):
        fixed[2] = value

    lookup(weights, rows, index, keep_weight, comps=1)
    fixed[1] = jnp.full((SUBS, LANES), -1.0, jnp.float32)
    lane = lax.broadcasted_iota(jnp.int32, (1, LANES), 1)
    for o in range(3):
        for k in range(2):
            for h in range(2):
                at = (o * 2 + k) * 2 + h
                here = lane + h * LANES < link_limit(counts, o, k)
                fixed[at // SUBS, at % SUBS : at % SUBS + 1, :] = jnp.where(
                    here, link_line(nodes, o, k, h), -1
                ).astype(jnp.float32)


def pair_sum_kernel(fixed, kept, came, own, link, index, table):
    rows = own.shape[1]
    half = rows // 2
    for c in range(3):
        both = kept[c, 0:rows, :] + came[c, 0:rows, :]
        own[c] = both
        for h in range(2):
            table[c, pl.ds(h, half, stride=2), :] = both[h * half : (h + 1) * half]
    index[0] = fixed[3].astype(jnp.int32)

    def keep(tile, c, value):
        link[c] = value

    lookup(table, rows, index, keep)
    for c in range(3):
        link[c, 6:8, :] = (
            kept[c, rows + 4 : rows + 6, :] + came[c, rows + 4 : rows + 6, :]
        )
        link[3 + c] = fixed[c]


def landing(nodes, lines, owned_high, width):
    pairs = []
    for (o, k), source in lines:
        for h in range(2):
            at = (o * 2 + k) * 2 + h
            entry = nodes[at // SUBS, at % SUBS : at % SUBS + 1, :].astype(jnp.int32)
            values = [source(c, h) for c in range(3)]
            split = [split_parts(v) for v in values]
            pairs.append(
                one_hot_pair(
                    [split[c][part] for part in range(PARTS) for c in range(3)],
                    entry,
                    owned_high,
                    0,
                    width,
                )
            )
    return contract(*[jnp.concatenate(x, axis=1) for x in zip(*pairs)])


def pair_owner_kernel(
    dom_count,
    own,
    link,
    mine,
    other,
    came,
    obs,
    weighted,
    out,
    total,
    index,
    table,
):
    rows = own.shape[1]
    owned_high = rows // 2
    width = 2 * LANES
    dom = lax.axis_index("dom")
    first = lax.axis_index("field") == 0

    def pick(here, there, inside):
        def line(k):
            def get(c, h):
                at = 2 * k + h
                return jnp.where(
                    inside, jnp.where(first, here(c, at), there(c, at)), 0.0
                )

            return get

        return line

    def row_of(tiles, base, shift):
        return lambda c, at: tiles[base + c, shift + at : shift + at + 1, :]

    part, fixed, his_fixed = link.at[0:3], link.at[3:6], came.at[3:6]
    low, high = dom > 0, dom < dom_count - 1
    mine_at, other_at = row_of(mine, 0, 0), row_of(other, 0, 0)
    his_mine, his_other = row_of(mine, 0, 4), row_of(other, 0, 4)
    below = pick(mine_at, other_at, low)
    above = pick(other_at, mine_at, high)
    his_below = pick(his_mine, his_other, low)
    his_above = pick(his_other, his_mine, high)
    own_middle, his_middle = row_of(part, 0, 6), row_of(came, 0, 6)
    own_lines = (
        ((0, 0), below(0)),
        ((0, 1), his_below(1)),
        ((1, 1), his_middle),
        ((2, 0), above(0)),
        ((2, 1), his_above(1)),
    )
    his_lines = (
        ((0, 0), his_below(0)),
        ((0, 1), below(1)),
        ((1, 1), own_middle),
        ((2, 0), his_above(0)),
        ((2, 1), above(1)),
    )
    total[0] = landing(fixed, own_lines, owned_high, width)
    total[1] = landing(his_fixed, his_lines, owned_high, width)
    for c in range(3):
        landed = summed(total.at[0], c * owned_high, owned_high, owned_high)
        his = summed(total.at[1], c * owned_high, owned_high, owned_high)
        for h in range(2):
            at = pl.ds(h, owned_high, stride=2)
            value = own[c, h * owned_high : (h + 1) * owned_high, :]
            value = obs[at, :] * (value + landed[:, h * LANES : (h + 1) * LANES])
            weighted[c, at, :] = value
            table[c, at, :] = value
            table[c, pl.ds(rows + h, owned_high, stride=2), :] = his[
                :, h * LANES : (h + 1) * LANES
            ]

    def node(tiles, o, k, h):
        at = (o * 2 + k) * 2 + h
        return tiles[at // SUBS, at % SUBS : at % SUBS + 1, :].astype(jnp.int32)

    index[0] = jnp.full((SUBS, LANES), -1, jnp.int32)
    index[1] = jnp.zeros((SUBS, LANES), jnp.int32)
    shift = rows * LANES
    for h in range(2):
        line = jnp.where(first, node(fixed, 2, 0, h), node(fixed, 0, 0, h))
        index[0, h : h + 1, :] = line
        for at, line in (
            (2, jnp.where(first, node(his_fixed, 2, 1, h), node(his_fixed, 0, 1, h))),
            (4, node(his_fixed, 1, 1, h)),
        ):
            index[0, at + h : at + h + 1, :] = jnp.where(line < 0, line, line + shift)
    is_open = index[0] >= 0
    index[0] = jnp.maximum(index[0], 0)
    row = lax.broadcasted_iota(jnp.int32, (SUBS, LANES), 0)

    def lined_up(tile):
        lines = []
        for h in range(2):
            lines.append(jnp.where(first, tile[4 + h : 5 + h, :], tile[h : h + 1, :]))
        lines += [tile[2:3, :], tile[3:4, :]]
        blank = jnp.zeros((2, LANES), jnp.float32)
        return jnp.concatenate([blank] + lines + [blank], axis=0)

    weight = lined_up(his_fixed[2])

    def keep(tile, c, value):
        value = jnp.where(row < 2, value, weight * (lined_up(came[c]) + value))
        out[c] = jnp.where(is_open, value, 0.0)

    lookup(table, 2 * rows, index.at[0:1], keep)


def pair_near_kernel(weighted, index, coupled, near, pulled):
    def keep(k, c, value):
        pulled[c * 10 + k] = value

    lookup(weighted, weighted.shape[1], index, keep)
    image = None
    for i in range(30):
        term = coupled[i] * pulled[i]
        image = term if image is None else image + term
    near[...] = image


def write_sums(search, remain, image, sums):
    for i, product in enumerate(
        (remain * remain, search * image, remain * image, image * image)
    ):
        line = jnp.sum(product, axis=0, keepdims=True)
        for p in range(sums.shape[0]):
            sums[p, i : i + 1, :] = line


def pair_adjoint_kernel(
    dom_count,
    rows,
    near,
    mine,
    other,
    middle,
    index,
    coupled,
    marks,
    residual,
    iterate,
    reg,
    hess,
    sums,
    vectors,
    ghosts,
    pulled,
):
    pair_ghosts(dom_count, mine, other, middle, ghosts)

    def keep(k, c, value):
        pulled[c * 10 + k] = value

    lookup(ghosts, 12, index, keep, first=rows, skip=NOBODY)
    image = near[...]
    for i in range(30):
        image = image + coupled[i] * pulled[i]
    search, mask = marks[0], marks[1]
    remain = mask * residual[...]
    image = image + reg[...] * search
    hess[...] = image
    vectors[0] = search
    vectors[1] = remain
    vectors[2] = mask * iterate[...]
    write_sums(search, remain, image, sums)


def pair_step(background, obs, connect, live_blocks, scale, others, nodes, counts, stiff):
    f32, i32 = jnp.float32, jnp.int32
    shape = jax.ShapeDtypeStruct
    dom_count = lax.axis_size("dom")
    owned_nodes = background.shape[1]
    link_slots = nodes.shape[3]
    rows = owned_nodes // LANES
    owned_high = owned_nodes // link_slots
    tile = (SUBS, LANES)
    swap = [(0, 1), (1, 0)]
    last = dom_count - 1

    def core(d, t, f):
        return (2 * d + t) * 2 + f

    def ring(turn):
        pairs = []
        for t in range(2):
            for d in range(last):
                pairs.append((core(d, t, 0), core(d + 1, t ^ turn, 0)))
                pairs.append((core(d + 1, t, 1), core(d, t ^ turn, 1)))
            pairs.append((core(last, t, 0), core(last, t, 1)))
            pairs.append((core(0, t, 1), core(0, t, 0)))
        return pairs

    left_rows = 3 * PARTS * owned_high + up_to(3 * PARTS * SUBS, 16)

    def across(x):
        return lax.ppermute(x, "field", swap)

    def beside(x):
        return lax.ppermute(x, "sub", swap)

    def along(x, turn=0):
        return lax.ppermute(x, ("dom", "sub", "field"), ring(turn))

    def call(kernel, outs, scratch, smem, args, params=PARAMS):
        return pl.pallas_call(
            kernel,
            compiler_params=params,
            out_shape=outs,
            in_specs=[SMEM] * smem + [VMEM] * (len(args) - smem),
            out_specs=jax.tree.map(lambda x: VMEM, outs),
            scratch_shapes=scratch,
            cost_estimate=pl.CostEstimate(
                flops=2**34, bytes_accessed=2**16, transcendentals=0
            ),
        )(*args)

    packed = call(
        pair_start_kernel,
        shape((3,) + tile, f32),
        [pltpu.VMEM((1,) + tile, i32), pltpu.VMEM((3, rows, LANES), f32)],
        1,
        (counts, nodes, background),
        None,
    )
    straight, slanted = along(packed), along(packed, 1)
    middle = beside(call(pair_copy_kernel, shape((3,) + tile, f32), [], 0, (packed,)))
    direction, residual, iterate, reg = others
    index, partial, wide, vectors = call(
        functools.partial(pair_own_kernel, link_slots),
        (
            shape((10,) + tile, i32),
            shape((30,) + tile, f32),
            shape((32, 32 * len(BLOCKS)), f32),
            shape((2,) + tile, f32),
        ),
        [pltpu.VMEM((3, rows, LANES), f32)],
        0,
        (background, connect, stiff, scale, direction),
    )
    straight, partial = lax.optimization_barrier((straight, partial))
    upper = lax.broadcasted_iota(i32, (3,) + tile, 1) < 2
    mine = jnp.where(upper, straight, slanted)
    other = across(mine)
    coupled, marks, kept, sent = call(
        functools.partial(pair_forward_kernel, dom_count),
        (
            shape((30,) + tile, f32),
            shape((2,) + tile, f32),
            shape((3, rows + SUBS, LANES), f32),
            shape((3, rows + SUBS, LANES), f32),
        ),
        [
            pltpu.VMEM((3, 16, LANES), f32),
            pltpu.VMEM((2, 32 * SUBS, LANES), f32),
            pltpu.VMEM((3 * PARTS, 10) + tile, f32),
            pltpu.VMEM((left_rows, link_slots), f32),
        ],
        0,
        (
            wide,
            partial,
            index,
            mine,
            other,
            middle,
            live_blocks.reshape(1, 1),
            vectors,
        ),
    )
    came = across(sent)
    nodes, _ = lax.optimization_barrier((nodes, sent))
    fixed = call(
        pair_fixed_kernel,
        shape((4,) + tile, f32),
        [pltpu.VMEM((1,) + tile, i32), pltpu.VMEM((1, rows, LANES), f32)],
        1,
        (counts, nodes, obs),
    )
    came, fixed = lax.optimization_barrier((came, fixed))
    linked = kept[:, rows:] + came[:, rows:]
    straight, slanted = along(linked), along(linked, 1)
    own, link = call(
        pair_sum_kernel,
        (shape((3, rows, LANES), f32), shape((6,) + tile, f32)),
        [pltpu.VMEM((1,) + tile, i32), pltpu.VMEM((3, rows, LANES), f32)],
        0,
        (fixed, kept, came),
    )
    came = beside(link)
    straight, slanted, _ = lax.optimization_barrier((straight, slanted, link))
    mine = call(
        pair_join_kernel, shape((3,) + tile, f32), [], 0, (straight, slanted)
    )
    other = across(mine)
    weighted, outbound = call(
        functools.partial(pair_owner_kernel, dom_count),
        (shape((3, rows, LANES), f32), shape((3,) + tile, f32)),
        [
            pltpu.VMEM((2, 3 * PARTS * owned_high, link_slots), f32),
            pltpu.VMEM((2,) + tile, i32),
            pltpu.VMEM((3, 2 * rows, LANES), f32),
        ],
        0,
        (own, link, mine, other, came, obs),
    )
    mine = along(outbound)
    inner = call(
        pair_near_kernel,
        shape(tile, f32),
        [pltpu.VMEM((30,) + tile, f32)],
        0,
        (weighted, index, coupled),
    )
    mine, inner = lax.optimization_barrier((mine, inner))
    other = across(mine)
    hess, sums, vectors = call(
        functools.partial(pair_adjoint_kernel, dom_count, rows),
        (
            shape(tile, f32),
            shape((4 * dom_count, SUMS, LANES), f32),
            shape((3,) + tile, f32),
        ),
        [pltpu.VMEM((3, 16, LANES), f32), pltpu.VMEM((30,) + tile, f32)],
        0,
        (inner, mine, other, outbound, index, coupled, marks, residual, iterate, reg),
    )
    return hess, sums, vectors


def general_step(
    background, obs, connect, live_blocks, scale, others, send_nodes, counts, ref_stiff
):
    f32, i32 = jnp.float32, jnp.int32
    shape = jax.ShapeDtypeStruct
    dom_count = lax.axis_size("dom")
    sub_count = lax.axis_size("sub")
    field_count = lax.axis_size("field")
    owned_nodes = background.shape[1]
    link_slots = send_nodes.shape[3]
    halves = link_slots // LANES
    width = link_slots
    owned_high = owned_nodes // width
    owned_rows = owned_nodes // LANES
    ghost_rows = 3 * sub_count * halves
    table_rows = owned_rows + ghost_rows
    partitions = dom_count * sub_count
    devices = partitions * field_count
    chunk = up_to(3 * halves, SUBS)
    link_tiles = up_to(ghost_rows, SUBS) // SUBS
    left_rows = 3 * PARTS * owned_high + up_to(3 * PARTS * up_to(3 * sub_count, SUBS), 16)
    dims = (dom_count, sub_count, halves)
    links = ("dom", "sub")
    cores = ("dom", "sub", "field")

    outbound = pl.pallas_call(
        functools.partial(start_kernel, dims),
        out_shape=shape((partitions, chunk, LANES), f32),
        in_specs=[SMEM, VMEM, VMEM],
        out_specs=VMEM,
        scratch_shapes=[
            pltpu.VMEM((link_tiles, SUBS, LANES), i32),
            pltpu.VMEM((3, link_tiles, SUBS, LANES), f32),
            pltpu.VMEM((3, owned_rows, LANES), f32),
        ],
    )(counts, send_nodes, background)
    arrived = lax.all_to_all(outbound, links, 0, 0, tiled=True)

    coupled, vectors, owned, outbound = pl.pallas_call(
        functools.partial(forward_kernel, dims),
        compiler_params=PARAMS,
        out_shape=(
            shape((30, SUBS, LANES), f32),
            shape((5, SUBS, LANES), f32),
            shape((3, owned_high, width), f32),
            shape((devices, chunk, LANES), f32),
        ),
        in_specs=[SMEM, SMEM] + [VMEM] * 8,
        out_specs=(VMEM,) * 4,
        scratch_shapes=[
            pltpu.VMEM((3, table_rows, LANES), f32),
            pltpu.VMEM((10, SUBS, LANES), i32),
            pltpu.VMEM((30, SUBS, LANES), f32),
            pltpu.VMEM((3 * PARTS, 10, SUBS, LANES), f32),
            pltpu.VMEM((left_rows, width), f32),
        ],
    )(
        live_blocks,
        ref_stiff,
        background,
        arrived,
        connect,
        scale,
        *others,
    )
    swapped = lax.ppermute(
        owned, "field", [(i, (i + 1) % field_count) for i in range(field_count)]
    )
    arrived = lax.all_to_all(outbound, cores, 0, 0, tiled=True)

    weighted, outbound = pl.pallas_call(
        functools.partial(owner_kernel, dims),
        compiler_params=PARAMS,
        out_shape=(
            shape((3, owned_rows, LANES), f32),
            shape((partitions, chunk, LANES), f32),
        ),
        in_specs=[SMEM] + [VMEM] * 5,
        out_specs=(VMEM,) * 2,
        scratch_shapes=[
            pltpu.VMEM((link_tiles, SUBS, LANES), i32),
            pltpu.VMEM((3, link_tiles, SUBS, LANES), f32),
        ],
    )(counts, send_nodes, owned, swapped, arrived, obs)
    arrived = lax.all_to_all(outbound, links, 0, 0, tiled=True)

    hess, sums = pl.pallas_call(
        functools.partial(adjoint_kernel, dims),
        compiler_params=PARAMS,
        out_shape=(shape((SUBS, LANES), f32), shape((devices, SUMS, LANES), f32)),
        in_specs=[VMEM] * 5,
        out_specs=(VMEM,) * 2,
        scratch_shapes=[
            pltpu.VMEM((3, table_rows, LANES), f32),
            pltpu.VMEM((10, SUBS, LANES), i32),
            pltpu.VMEM((10, 3, SUBS, LANES), f32),
        ],
    )(weighted, arrived, connect, coupled, vectors)
    return hess, sums, vectors


def on_device(
    background,
    obs_weight,
    connect,
    live_blocks,
    elem_scale,
    reg_weight,
    iterate,
    residual,
    direction,
    send_nodes,
    send_count,
    ref_stiff,
):
    f32 = jnp.float32
    shape = jax.ShapeDtypeStruct
    tiled = lambda x: x.reshape(-1, LANES)
    scale, reg, guess, remain, search = map(
        tiled, (elem_scale, reg_weight, iterate, residual, direction)
    )
    obs = tiled(obs_weight)
    counts = jnp.swapaxes(send_count, 1, 2)
    two = lax.axis_size("sub") == 2 and lax.axis_size("field") == 2
    paired = two and send_nodes.shape[3] == 2 * LANES
    hess, sums, vectors = (pair_step if paired else general_step)(
        background,
        obs,
        connect,
        live_blocks,
        scale,
        (search, remain, guess, reg),
        send_nodes,
        counts,
        ref_stiff,
    )
    cores = ("dom", "sub", "field")
    sums = lax.all_to_all(sums, cores, 0, 0, tiled=True)

    results = pl.pallas_call(
        update_kernel,
        compiler_params=PARAMS,
        out_shape=(shape((SUBS, LANES), f32),) * 3,
        in_specs=[VMEM] * 3,
        out_specs=(VMEM,) * 3,
    )(sums, hess, vectors)
    return tuple(x.reshape(-1) for x in results)


def solution(mesh):
    placed = (
        P(None, ("groups", "dom", "sub")),
        P(("groups", "dom", "sub")),
        P(None, ("groups", "dom", "sub", "field")),
        P(("groups", "dom", "sub", "field")),
        P(("groups", "dom", "sub", "field")),
        P(("groups", "dom", "sub", "field")),
        P(("groups", "dom", "sub", "field")),
        P(("groups", "dom", "sub", "field")),
        P(("groups", "dom", "sub", "field")),
        P(("groups", "dom", "sub"), None, None, None),
        P(("groups", "dom", "sub"), None, None),
        P(),
    )
    return jax.shard_map(
        on_device,
        mesh=mesh,
        in_specs=placed,
        out_specs=(
            P(("groups", "dom", "sub", "field")),
            P(("groups", "dom", "sub", "field")),
            P(("groups", "dom", "sub", "field")),
        ),
        check_vma=False,
    )
```

```python
import functools

import jax
import jax.numpy as jnp
from jax import lax
from jax.experimental import pallas as pl
from jax.experimental.pallas import tpu as pltpu
from jax.sharding import PartitionSpec as P

BLK = 128
LANES = 128
SUBS = 8
PARTS = 2
UNROLL = 10
SUMS = 4
LANE_BITS = 7

VMEM = pl.BlockSpec(memory_space=pltpu.VMEM)
SMEM = pl.BlockSpec(memory_space=pltpu.SMEM)
PARAMS = pltpu.CompilerParams(vmem_limit_bytes=16 * 2**20)


def up_to(count, step):
    return -(-count // step) * step


def lookup(table, rows, index, store, begin=None, first=0, comps=3, skip=()):
    def one(tile):
        entry = index[tile]
        high = lax.shift_right_logical(entry, LANE_BITS)
        low = entry & (LANES - 1)
        found = [0.0 if begin is None else begin(tile, c) for c in range(comps)]
        for row in range(rows):
            if row in skip:
                continue
            here = high == first + row
            for c in range(comps):
                line = jnp.broadcast_to(table[c, row : row + 1, :], (SUBS, LANES))
                value = jnp.take_along_axis(
                    line, low, axis=1, mode="promise_in_bounds"
                )
                found[c] = jnp.where(here, value, found[c])
        for c in range(comps):
            store(tile, c, found[c])

    def step(tile, carry):
        one(tile)
        return carry

    if index.shape[0] == 1:
        one(0)
    else:
        lax.fori_loop(0, index.shape[0], step, 0, unroll=min(2 if rows > 16 else 5, index.shape[0]))


def split_parts(value, count=PARTS):
    pieces = []
    for _ in range(count - 1):
        piece = value.astype(jnp.bfloat16).astype(jnp.float32)
        pieces.append(piece)
        value = value - piece
    pieces.append(value.astype(jnp.bfloat16).astype(jnp.float32))
    return pieces


def spread(line, rows):
    return jnp.broadcast_to(line, (rows, LANES)).astype(jnp.bfloat16)


def row_numbers(rows):
    row = lax.broadcasted_iota(jnp.int32, (rows, LANES), 0)
    return row.astype(jnp.float32).astype(jnp.bfloat16)


def one_hot_pair(lines, index, owned_high, ghost_high, width):
    none = jnp.zeros((), jnp.bfloat16)
    unit = jnp.ones((), jnp.bfloat16)
    high = index // width
    low = (index & (width - 1)).astype(jnp.float32)
    here = row_numbers(owned_high) == spread(high.astype(jnp.float32), owned_high)
    blocks = [jnp.where(here, spread(x, owned_high), none) for x in lines]
    if ghost_high:
        row = lax.broadcasted_iota(jnp.int32, (ghost_high, LANES), 0) + owned_high
        here = row == jnp.broadcast_to(high, row.shape)
        rest = [jnp.where(here, jnp.broadcast_to(x, row.shape), 0.0) for x in lines]
        spare = up_to(len(lines) * ghost_high, 16) - len(lines) * ghost_high
        if spare:
            rest.append(jnp.zeros((spare, LANES), jnp.float32))
        blocks.append(jnp.concatenate(rest, axis=0).astype(jnp.bfloat16))
    left = jnp.concatenate(blocks, axis=0)
    right = jnp.where(row_numbers(width) == spread(low, width), unit, none)
    return left, right


def contract(left, right):
    return lax.dot_general(
        left, right, (((1,), (1,)), ((), ())), preferred_element_type=jnp.float32
    )


def link_rows(sub_count, halves):
    return [
        (o, t, h, (o * sub_count + t) * halves + h)
        for o in range(3)
        for t in range(sub_count)
        for h in range(halves)
    ]


def load_links(nodes, index, sub_count, halves):
    for o, t, h, row in link_rows(sub_count, halves):
        index[row // SUBS, row % SUBS : row % SUBS + 1, :] = nodes[
            0, o, t : t + 1, h * LANES : (h + 1) * LANES
        ]
    for row in range(3 * sub_count * halves, index.shape[0] * SUBS):
        index[row // SUBS, row % SUBS : row % SUBS + 1, :] = jnp.zeros((1, LANES), jnp.int32)


def open_lanes(counts, o, t, h):
    lane = lax.broadcasted_iota(jnp.int32, (1, LANES), 1) + h * LANES
    return lane < counts[0, t, o]


def send_links(table, table_rows, counts, index, values, out, dom_count, sub_count, halves):
    def store(tile, c, value):
        values[c, tile] = value

    lookup(table, table_rows, index, store)

    def clear(p, carry):
        out[p] = jnp.zeros(out.shape[1:], jnp.float32)
        return carry

    lax.fori_loop(0, out.shape[0], clear, 0)
    dom = lax.axis_index("dom")
    for o in range(3):
        place = dom + o - 1

        @pl.when((place >= 0) & (place < dom_count))
        def _():
            for t in range(sub_count):
                for h in range(halves):
                    row = (o * sub_count + t) * halves + h
                    here = open_lanes(counts, o, t, h)
                    for c in range(3):
                        line = values[c, row // SUBS, row % SUBS : row % SUBS + 1, :]
                        out[place * sub_count + t, c * halves + h : c * halves + h + 1, :] = (
                            jnp.where(here, line, 0.0)
                        )


def fill_ghosts(table, first, arrived, dom_count, sub_count, halves):
    dom = lax.axis_index("dom")
    for o in range(3):
        place = dom + o - 1
        inside = (place >= 0) & (place < dom_count)
        safe = jnp.clip(place, 0, dom_count - 1)
        for t in range(sub_count):
            chunk = arrived[safe * sub_count + t]
            chunk = jnp.where(inside, chunk, 0.0)
            for c in range(3):
                row = first + (o * sub_count + t) * halves
                table[c, row : row + halves, :] = chunk[c * halves : (c + 1) * halves, :]


def start_kernel(dims, counts, nodes, background, out, index, values, table):
    dom_count, sub_count, halves = dims
    rows = background.shape[1] // LANES
    for c in range(3):
        for r in range(rows):
            table[c, r : r + 1, :] = background[c : c + 1, r * LANES : (r + 1) * LANES]
    load_links(nodes, index, sub_count, halves)
    send_links(table, rows, counts, index, values, out, dom_count, sub_count, halves)


def load_index(connect, index):
    for k in range(10):
        for b in range(SUBS):
            index[k, b : b + 1, :] = connect[k : k + 1, b * LANES : (b + 1) * LANES]


def couple(live, stiff, scale, others, state, coupled, vectors, pieces):
    element_vectors(live, scale, others, vectors)
    forward_terms(stiff, state, coupled, vectors, pieces)


def live_mask(blocks):
    element = (
        lax.broadcasted_iota(jnp.int32, (SUBS, LANES), 0) * LANES
        + lax.broadcasted_iota(jnp.int32, (SUBS, LANES), 1)
    )
    return (element < BLK * blocks).astype(jnp.float32)


def element_vectors(live, scale, others, vectors):
    direction, residual, iterate, reg = others
    mask = live_mask(live[0])
    search = mask * direction[...]
    vectors[0] = search
    vectors[1] = mask * residual[...]
    vectors[2] = mask * iterate[...]
    vectors[3] = reg[...] * search
    vectors[4] = mask * scale[...]


def forward_terms(stiff, state, coupled, vectors, pieces):
    search, factor = vectors[0], vectors[4]
    for c in range(3):
        sums = [None] * 10
        for j in range(30):
            value = state[j]
            for k in range(10):
                term = stiff[c * 10 + k, j] * value
                sums[k] = term if j == 0 else sums[k] + term
        for k in range(10):
            result = factor * sums[k]
            coupled[c * 10 + k] = result
            for part, piece in enumerate(split_parts(search * result)):
                pieces[part * 3 + c, k] = piece


def assemble(pieces, index, total, owned_high, ghost_high, width):
    total[...] = jnp.zeros_like(total)

    def scatter(k, carry):
        pairs = [
            one_hot_pair(
                [pieces[q, k, b : b + 1, :] for q in range(3 * PARTS)],
                index[k, b : b + 1, :],
                owned_high,
                ghost_high,
                width,
            )
            for b in range(SUBS)
        ]
        total[...] += contract(*[jnp.concatenate(x, axis=1) for x in zip(*pairs)])
        return carry

    lax.fori_loop(0, 10, scatter, 0, unroll=UNROLL)


def summed(total, first, step, count):
    value = None
    for part in reversed(range(PARTS)):
        base = first + part * 3 * step
        piece = total[base : base + count, :]
        value = piece if value is None else value + piece
    return value


def forward_kernel(
    dims,
    live,
    stiff,
    background,
    arrived,
    connect,
    scale,
    direction,
    residual,
    iterate,
    reg,
    coupled,
    vectors,
    owned,
    outbound,
    table,
    index,
    state,
    pieces,
    total,
):
    dom_count, sub_count, halves = dims
    width = halves * LANES
    rows = background.shape[1] // LANES
    owned_high = background.shape[1] // width
    ghost_rows = 3 * sub_count * halves
    for c in range(3):
        for r in range(rows):
            table[c, r : r + 1, :] = background[c : c + 1, r * LANES : (r + 1) * LANES]
    fill_ghosts(table, rows, arrived, dom_count, sub_count, halves)
    load_index(connect, index)

    def keep(k, c, value):
        state[c * 10 + k] = value

    lookup(table, rows + ghost_rows, index, keep)
    couple(
        live,
        stiff,
        scale,
        (direction, residual, iterate, reg),
        state,
        coupled,
        vectors,
        pieces,
    )
    ghost_high = up_to(3 * sub_count, SUBS)
    assemble(pieces, index, total, owned_high, ghost_high, width)

    def clear(p, carry):
        outbound[p] = jnp.zeros(outbound.shape[1:], jnp.float32)
        return carry

    lax.fori_loop(0, outbound.shape[0], clear, 0)
    dom = lax.axis_index("dom")
    fields = outbound.shape[0] // (dom_count * sub_count)
    ghost = [None] * 3
    for c in range(3):
        owned[c] = summed(total, c * owned_high, owned_high, owned_high)
        ghost[c] = summed(
            total, 3 * PARTS * owned_high + c * ghost_high, ghost_high, 3 * sub_count
        )
    for o in range(3):
        place = dom + o - 1

        @pl.when((place >= 0) & (place < dom_count))
        def _():
            for t in range(sub_count):
                for c in range(3):
                    for h in range(halves):
                        line = ghost[c][
                            o * sub_count + t : o * sub_count + t + 1,
                            h * LANES : (h + 1) * LANES,
                        ]
                        spot = c * halves + h
                        for f in range(fields):
                            outbound[
                                (place * sub_count + t) * fields + f, spot : spot + 1, :
                            ] = line


def owner_kernel(
    dims,
    counts,
    nodes,
    mine,
    other,
    arrived,
    obs,
    weighted,
    out,
    index,
    values,
):
    dom_count, sub_count, halves = dims
    width = halves * LANES
    fields = arrived.shape[0] // (dom_count * sub_count)
    owned_high = mine.shape[1]
    load_links(nodes, index, sub_count, halves)
    dom = lax.axis_index("dom")
    pairs = []
    for o in range(3):
        place = dom + o - 1
        inside = (place >= 0) & (place < dom_count)
        safe = jnp.clip(place, 0, dom_count - 1)
        for t in range(sub_count):
            chunk = arrived[(safe * sub_count + t) * fields]
            for f in range(1, fields):
                chunk = chunk + arrived[(safe * sub_count + t) * fields + f]
            chunk = jnp.where(inside, chunk, 0.0)
            split = split_parts(chunk)
            for h in range(halves):
                row = (o * sub_count + t) * halves + h
                here = open_lanes(counts, o, t, h)
                lines = [
                    jnp.where(here, split[part][c * halves + h : c * halves + h + 1, :], 0.0)
                    for part in range(PARTS)
                    for c in range(3)
                ]
                a, m = one_hot_pair(lines, index[row // SUBS, row % SUBS : row % SUBS + 1, :], owned_high, 0, width)
                pairs.append((a, m))
    total = contract(*[jnp.concatenate(x, axis=1) for x in zip(*pairs)])
    for c in range(3):
        value = mine[c] + other[c]
        landed = None
        for part in reversed(range(PARTS)):
            base = (part * 3 + c) * owned_high
            piece = total[base : base + owned_high, :]
            landed = piece if landed is None else landed + piece
        value = value + landed
        for h in range(halves):
            weight = obs[pl.ds(h, owned_high, stride=halves), :]
            weighted[c, pl.ds(h, owned_high, stride=halves), :] = (
                weight * value[:, h * LANES : (h + 1) * LANES]
            )
    rows = owned_high * halves
    send_links(weighted, rows, counts, index, values, out, dom_count, sub_count, halves)


def adjoint_kernel(
    dims, weighted, arrived, connect, coupled, vectors, hess, sums, table, index, pulled
):
    dom_count, sub_count, halves = dims
    rows = weighted.shape[1]
    table[:, 0:rows, :] = weighted[...]
    fill_ghosts(table, rows, arrived, dom_count, sub_count, halves)
    load_index(connect, index)

    def keep(k, c, value):
        pulled[k, c] = value

    lookup(table, rows + 3 * sub_count * halves, index, keep)
    search, remain = vectors[0], vectors[1]
    image = None
    for c in range(3):
        for k in range(10):
            term = coupled[c * 10 + k] * pulled[k, c]
            image = term if image is None else image + term
    image = image + vectors[3]
    hess[...] = image
    for i, product in enumerate(
        (remain * remain, search * image, remain * image, image * image)
    ):
        line = jnp.sum(product, axis=0, keepdims=True)
        for p in range(sums.shape[0]):
            sums[p, i : i + 1, :] = line


def update_kernel(sums, hess, vectors, iterate_out, residual_out, direction_out):
    totals = []
    for i in range(4):
        line = sums[0, i : i + 1, :]
        for p in range(1, sums.shape[0]):
            line = line + sums[p, i : i + 1, :]
        line = jnp.sum(line, axis=1, keepdims=True)
        totals.append(jnp.broadcast_to(line, (SUBS, LANES)))
    squared_before, curvature_sum, cross_term, image_square = totals
    search, remain, guess = vectors[0], vectors[1], vectors[2]
    step_length = squared_before / curvature_sum
    squared_after = (
        squared_before
        - 2.0 * step_length * cross_term
        + step_length * step_length * image_square
    )
    residual_next = remain - step_length * hess[...]
    iterate_out[...] = guess + step_length * search
    residual_out[...] = residual_next
    direction_out[...] = residual_next + squared_after / squared_before * search


def own_table(source, table):
    for c in range(3):
        for r in range(source.shape[1] // LANES):
            table[c, r : r + 1, :] = source[c : c + 1, r * LANES : (r + 1) * LANES]


def link_line(nodes, o, k, h):
    zero = nodes[0, o, 0:1, h * LANES : (h + 1) * LANES]
    one = nodes[0, o, 1:2, h * LANES : (h + 1) * LANES]
    return jnp.where((lax.axis_index("sub") ^ k) == 0, zero, one)


def link_limit(counts, o, k):
    return counts[0, lax.axis_index("sub") ^ k, o]


def link_tile(nodes, tile, links):
    tile[0] = jnp.zeros((SUBS, LANES), jnp.int32)
    for i, (o, k) in enumerate(links):
        for h in range(2):
            tile[0, 2 * i + h : 2 * i + h + 1, :] = link_line(nodes, o, k, h)


def pair_start_kernel(counts, nodes, background, out, index, table):
    step = jnp.where(lax.axis_index("field") == 0, 2, 0)
    links = ((step, 0), (step, 1), (1, 1))
    own_table(background, table)
    link_tile(nodes, index, links)
    row = lax.broadcasted_iota(jnp.int32, (SUBS, LANES), 0)
    slot = lax.broadcasted_iota(jnp.int32, (SUBS, LANES), 1) + row % 2 * LANES
    limit = jnp.zeros((SUBS, LANES), jnp.int32)
    for i, (o, k) in enumerate(links):
        limit = jnp.where(row // 2 == i, link_limit(counts, o, k), limit)

    def keep(tile, c, value):
        out[c] = jnp.where(slot < limit, value, 0.0)

    lookup(table, table.shape[1], index, keep)


BLOCKS = ((0, 0), (0, 1), (1, 0), (0, 2), (1, 1), (2, 0))


NOBODY = (4, 5)


def pair_ghosts(dom_count, mine, other, middle, table):
    dom = lax.axis_index("dom")
    first = lax.axis_index("field") == 0
    for c in range(3):
        below = jnp.where(first, mine[c], other[c])
        above = jnp.where(first, other[c], mine[c])
        below = jnp.where(dom > 0, below, 0.0)
        above = jnp.where(dom < dom_count - 1, above, 0.0)
        table[c, 0:4, :] = below[0:4, :]
        table[c, 6:8, :] = middle[c, 4:6, :]
        table[c, 8:12, :] = above[0:4, :]


def pair_copy_kernel(source, out):
    out[...] = source[...]


def pair_join_kernel(straight, slanted, out):
    for c in range(3):
        out[c, 0:4, :] = straight[c, 0:4, :]
        out[c, 4:8, :] = slanted[c, 0:4, :]


def pair_own_kernel(
    link_slots,
    background,
    connect,
    stiff,
    scale,
    direction,
    index,
    partial,
    wide,
    vectors,
    table,
):
    vectors[0] = direction[...]
    vectors[1] = scale[...]
    wide[...] = jnp.zeros_like(wide)
    size = stiff.shape[0]
    split = split_parts(stiff[...], 3)
    for i, (piece, _) in enumerate(BLOCKS):
        wide[0:size, i * 32 : i * 32 + size] = split[piece]
    sub = lax.axis_index("sub")
    own_table(background, table)
    load_index(connect, index)
    owned_nodes = background.shape[1]
    for k in range(10):
        entry = index[k]
        index[k] = jnp.where(entry >= owned_nodes, entry ^ (sub * link_slots), entry)

    def keep(k, c, value):
        partial[c * 10 + k] = value

    lookup(table, table.shape[1], index, keep)


def pair_forward_kernel(
    dom_count,
    wide,
    partial,
    index,
    mine,
    other,
    middle,
    live,
    vectors,
    coupled,
    marks,
    kept,
    sent,
    ghosts,
    state,
    pieces,
    total,
):
    owned_high = kept.shape[1] // 2 - SUBS // 2
    pair_ghosts(dom_count, mine, other, middle, ghosts)

    def begin(k, c):
        return partial[c * 10 + k]

    def keep(k, c, value):
        at = pl.multiple_of((c * 10 + k) * SUBS, SUBS)
        state[0, pl.ds(at, SUBS), :] = value

    lookup(ghosts, 12, index, keep, begin, 2 * owned_high, skip=NOBODY)
    spare = state.shape[1] - 30 * SUBS
    state[0, 30 * SUBS :, :] = jnp.zeros((spare, LANES), jnp.float32)
    weights = wide[...].astype(jnp.bfloat16)
    for b in range(0, SUBS, 2):
        lines = jnp.concatenate(
            [state[0, pl.ds(b + i, 32, stride=SUBS), :] for i in range(2)], axis=1
        )
        split = [x.astype(jnp.bfloat16) for x in split_parts(lines, 3)]
        product = lax.dot_general(
            weights,
            jnp.concatenate([split[his] for _, his in BLOCKS], axis=0),
            (((1,), (0,)), ((), ())),
            preferred_element_type=jnp.float32,
        )
        for i in range(2):
            state[1, pl.ds(b + i, 32, stride=SUBS), :] = product[
                :, i * LANES : (i + 1) * LANES
            ]
    mask = live_mask(live[...])
    search, factor = mask * vectors[0], mask * vectors[1]
    marks[0] = search
    marks[1] = mask
    for c in range(3):
        for k in range(10):
            at = (c * 10 + k) * SUBS
            result = factor * state[1, at : at + SUBS, :]
            coupled[c * 10 + k] = result
            for part, piece in enumerate(split_parts(search * result)):
                pieces[part * 3 + c, k] = piece
    width = 2 * LANES
    assemble(pieces, index, total, owned_high, SUBS, width)
    first = lax.axis_index("field") == 0
    base = 2 * owned_high
    for c in range(3):
        own = summed(total, c * owned_high, owned_high, owned_high)
        ghost = summed(total, 3 * PARTS * owned_high + c * SUBS, SUBS, SUBS)
        for h in range(2):
            half = own[:, h * LANES : (h + 1) * LANES]
            kept[c, h * owned_high : (h + 1) * owned_high, :] = half
            sent[c, h * owned_high : (h + 1) * owned_high, :] = half
            lines = ghost[:, h * LANES : (h + 1) * LANES]
            for k in range(2):
                below, above = lines[k : k + 1, :], lines[4 + k : 5 + k, :]
                at = base + 2 * k + h
                kept[c, at : at + 1, :] = jnp.where(first, above, below)
                sent[c, at : at + 1, :] = jnp.where(first, below, above)
            for out in (kept, sent):
                out[c, base + 4 + h : base + 5 + h, :] = lines[3:4, :]
                out[c, base + 6 + h : base + 7 + h, :] = jnp.zeros((1, LANES), jnp.float32)


def pair_fixed_kernel(counts, nodes, obs, fixed, index, weights):
    rows = obs.shape[0]
    weights[0] = obs[...]
    link_tile(nodes, index, ((0, 1), (1, 1), (2, 1)))
    fixed[3] = index[0].astype(jnp.float32)

    def keep_weight(tile, c, value):
        fixed[2] = value

    lookup(weights, rows, index, keep_weight, comps=1)
    fixed[1] = jnp.full((SUBS, LANES), -1.0, jnp.float32)
    lane = lax.broadcasted_iota(jnp.int32, (1, LANES), 1)
    for o in range(3):
        for k in range(2):
            for h in range(2):
                at = (o * 2 + k) * 2 + h
                here = lane + h * LANES < link_limit(counts, o, k)
                fixed[at // SUBS, at % SUBS : at % SUBS + 1, :] = jnp.where(
                    here, link_line(nodes, o, k, h), -1
                ).astype(jnp.float32)


def pair_sum_kernel(fixed, kept, came, own, link, index, table):
    rows = own.shape[1]
    half = rows // 2
    for c in range(3):
        both = kept[c, 0:rows, :] + came[c, 0:rows, :]
        own[c] = both
        for h in range(2):
            table[c, pl.ds(h, half, stride=2), :] = both[h * half : (h + 1) * half]
    index[0] = fixed[3].astype(jnp.int32)

    def keep(tile, c, value):
        link[c] = value

    lookup(table, rows, index, keep)
    for c in range(3):
        link[c, 6:8, :] = (
            kept[c, rows + 4 : rows + 6, :] + came[c, rows + 4 : rows + 6, :]
        )
        link[3 + c] = fixed[c]


def landing(nodes, lines, owned_high, width):
    pairs = []
    for (o, k), source in lines:
        for h in range(2):
            at = (o * 2 + k) * 2 + h
            entry = nodes[at // SUBS, at % SUBS : at % SUBS + 1, :].astype(jnp.int32)
            values = [source(c, h) for c in range(3)]
            split = [split_parts(v) for v in values]
            pairs.append(
                one_hot_pair(
                    [split[c][part] for part in range(PARTS) for c in range(3)],
                    entry,
                    owned_high,
                    0,
                    width,
                )
            )
    return contract(*[jnp.concatenate(x, axis=1) for x in zip(*pairs)])


def pair_owner_kernel(
    dom_count,
    own,
    link,
    mine,
    other,
    came,
    obs,
    weighted,
    out,
    total,
    index,
    table,
):
    rows = own.shape[1]
    owned_high = rows // 2
    width = 2 * LANES
    dom = lax.axis_index("dom")
    first = lax.axis_index("field") == 0

    def pick(here, there, inside):
        def line(k):
            def get(c, h):
                at = 2 * k + h
                return jnp.where(
                    inside, jnp.where(first, here(c, at), there(c, at)), 0.0
                )

            return get

        return line

    def row_of(tiles, base, shift):
        return lambda c, at: tiles[base + c, shift + at : shift + at + 1, :]

    part, fixed, his_fixed = link.at[0:3], link.at[3:6], came.at[3:6]
    low, high = dom > 0, dom < dom_count - 1
    mine_at, other_at = row_of(mine, 0, 0), row_of(other, 0, 0)
    his_mine, his_other = row_of(mine, 0, 4), row_of(other, 0, 4)
    below = pick(mine_at, other_at, low)
    above = pick(other_at, mine_at, high)
    his_below = pick(his_mine, his_other, low)
    his_above = pick(his_other, his_mine, high)
    own_middle, his_middle = row_of(part, 0, 6), row_of(came, 0, 6)
    own_lines = (
        ((0, 0), below(0)),
        ((0, 1), his_below(1)),
        ((1, 1), his_middle),
        ((2, 0), above(0)),
        ((2, 1), his_above(1)),
    )
    his_lines = (
        ((0, 0), his_below(0)),
        ((0, 1), below(1)),
        ((1, 1), own_middle),
        ((2, 0), his_above(0)),
        ((2, 1), above(1)),
    )
    total[0] = landing(fixed, own_lines, owned_high, width)
    total[1] = landing(his_fixed, his_lines, owned_high, width)
    for c in range(3):
        landed = summed(total.at[0], c * owned_high, owned_high, owned_high)
        his = summed(total.at[1], c * owned_high, owned_high, owned_high)
        for h in range(2):
            at = pl.ds(h, owned_high, stride=2)
            value = own[c, h * owned_high : (h + 1) * owned_high, :]
            value = obs[at, :] * (value + landed[:, h * LANES : (h + 1) * LANES])
            weighted[c, at, :] = value
            table[c, at, :] = value
            table[c, pl.ds(rows + h, owned_high, stride=2), :] = his[
                :, h * LANES : (h + 1) * LANES
            ]

    def node(tiles, o, k, h):
        at = (o * 2 + k) * 2 + h
        return tiles[at // SUBS, at % SUBS : at % SUBS + 1, :].astype(jnp.int32)

    index[0] = jnp.full((SUBS, LANES), -1, jnp.int32)
    index[1] = jnp.zeros((SUBS, LANES), jnp.int32)
    shift = rows * LANES
    for h in range(2):
        line = jnp.where(first, node(fixed, 2, 0, h), node(fixed, 0, 0, h))
        index[0, h : h + 1, :] = line
        for at, line in (
            (2, jnp.where(first, node(his_fixed, 2, 1, h), node(his_fixed, 0, 1, h))),
            (4, node(his_fixed, 1, 1, h)),
        ):
            index[0, at + h : at + h + 1, :] = jnp.where(line < 0, line, line + shift)
    is_open = index[0] >= 0
    index[0] = jnp.maximum(index[0], 0)
    row = lax.broadcasted_iota(jnp.int32, (SUBS, LANES), 0)

    def lined_up(tile):
        lines = []
        for h in range(2):
            lines.append(jnp.where(first, tile[4 + h : 5 + h, :], tile[h : h + 1, :]))
        lines += [tile[2:3, :], tile[3:4, :]]
        blank = jnp.zeros((2, LANES), jnp.float32)
        return jnp.concatenate([blank] + lines + [blank], axis=0)

    weight = lined_up(his_fixed[2])

    def keep(tile, c, value):
        value = jnp.where(row < 2, value, weight * (lined_up(came[c]) + value))
        out[c] = jnp.where(is_open, value, 0.0)

    lookup(table, 2 * rows, index.at[0:1], keep)


def pair_near_kernel(weighted, middle, index, coupled, near, pulled, ghosts):
    def keep(k, c, value):
        pulled[c * 10 + k] = value

    def begin(k, c):
        return pulled[c * 10 + k]

    rows = weighted.shape[1]
    lookup(weighted, rows, index, keep)
    for c in range(3):
        ghosts[c, 6:8, :] = middle[c, 4:6, :]
    lookup(ghosts, 8, index, keep, begin, rows, skip=range(6))
    image = None
    for i in range(30):
        term = coupled[i] * pulled[i]
        image = term if image is None else image + term
    near[...] = image


def write_sums(search, remain, image, sums):
    for i, product in enumerate(
        (remain * remain, search * image, remain * image, image * image)
    ):
        line = jnp.sum(product, axis=0, keepdims=True)
        for p in range(sums.shape[0]):
            sums[p, i : i + 1, :] = line


def pair_adjoint_kernel(
    dom_count,
    rows,
    near,
    mine,
    other,
    middle,
    index,
    coupled,
    marks,
    residual,
    iterate,
    reg,
    hess,
    sums,
    vectors,
    ghosts,
    pulled,
):
    pair_ghosts(dom_count, mine, other, middle, ghosts)

    def keep(k, c, value):
        pulled[c * 10 + k] = value

    lookup(ghosts, 12, index, keep, first=rows, skip=NOBODY + (6, 7))
    image = near[...]
    for i in range(30):
        image = image + coupled[i] * pulled[i]
    search, mask = marks[0], marks[1]
    remain = mask * residual[...]
    image = image + reg[...] * search
    hess[...] = image
    vectors[0] = search
    vectors[1] = remain
    vectors[2] = mask * iterate[...]
    write_sums(search, remain, image, sums)


def pair_step(background, obs, connect, live_blocks, scale, others, nodes, counts, stiff):
    f32, i32 = jnp.float32, jnp.int32
    shape = jax.ShapeDtypeStruct
    dom_count = lax.axis_size("dom")
    owned_nodes = background.shape[1]
    link_slots = nodes.shape[3]
    rows = owned_nodes // LANES
    owned_high = owned_nodes // link_slots
    tile = (SUBS, LANES)
    swap = [(0, 1), (1, 0)]
    last = dom_count - 1

    def core(d, t, f):
        return (2 * d + t) * 2 + f

    def ring(turn):
        pairs = []
        for t in range(2):
            for d in range(last):
                pairs.append((core(d, t, 0), core(d + 1, t ^ turn, 0)))
                pairs.append((core(d + 1, t, 1), core(d, t ^ turn, 1)))
            pairs.append((core(last, t, 0), core(last, t, 1)))
            pairs.append((core(0, t, 1), core(0, t, 0)))
        return pairs

    left_rows = 3 * PARTS * owned_high + up_to(3 * PARTS * SUBS, 16)

    def across(x):
        return lax.ppermute(x, "field", swap)

    def beside(x):
        return lax.ppermute(x, "sub", swap)

    def along(x, turn=0):
        return lax.ppermute(x, ("dom", "sub", "field"), ring(turn))

    def call(kernel, outs, scratch, smem, args, params=PARAMS):
        return pl.pallas_call(
            kernel,
            compiler_params=params,
            out_shape=outs,
            in_specs=[SMEM] * smem + [VMEM] * (len(args) - smem),
            out_specs=jax.tree.map(lambda x: VMEM, outs),
            scratch_shapes=scratch,
            cost_estimate=pl.CostEstimate(
                flops=2**34, bytes_accessed=2**16, transcendentals=0
            ),
        )(*args)

    packed = call(
        pair_start_kernel,
        shape((3,) + tile, f32),
        [pltpu.VMEM((1,) + tile, i32), pltpu.VMEM((3, rows, LANES), f32)],
        1,
        (counts, nodes, background),
        None,
    )
    straight, slanted = along(packed), along(packed, 1)
    middle = beside(call(pair_copy_kernel, shape((3,) + tile, f32), [], 0, (packed,)))
    direction, residual, iterate, reg = others
    index, partial, wide, vectors = call(
        functools.partial(pair_own_kernel, link_slots),
        (
            shape((10,) + tile, i32),
            shape((30,) + tile, f32),
            shape((32, 32 * len(BLOCKS)), f32),
            shape((2,) + tile, f32),
        ),
        [pltpu.VMEM((3, rows, LANES), f32)],
        0,
        (background, connect, stiff, scale, direction),
    )
    straight, partial = lax.optimization_barrier((straight, partial))
    upper = lax.broadcasted_iota(i32, (3,) + tile, 1) < 2
    mine = jnp.where(upper, straight, slanted)
    other = across(mine)
    coupled, marks, kept, sent = call(
        functools.partial(pair_forward_kernel, dom_count),
        (
            shape((30,) + tile, f32),
            shape((2,) + tile, f32),
            shape((3, rows + SUBS, LANES), f32),
            shape((3, rows + SUBS, LANES), f32),
        ),
        [
            pltpu.VMEM((3, 16, LANES), f32),
            pltpu.VMEM((2, 32 * SUBS, LANES), f32),
            pltpu.VMEM((3 * PARTS, 10) + tile, f32),
            pltpu.VMEM((left_rows, link_slots), f32),
        ],
        0,
        (
            wide,
            partial,
            index,
            mine,
            other,
            middle,
            live_blocks.reshape(1, 1),
            vectors,
        ),
    )
    came = across(sent)
    nodes, _ = lax.optimization_barrier((nodes, sent))
    fixed = call(
        pair_fixed_kernel,
        shape((4,) + tile, f32),
        [pltpu.VMEM((1,) + tile, i32), pltpu.VMEM((1, rows, LANES), f32)],
        1,
        (counts, nodes, obs),
    )
    came, fixed = lax.optimization_barrier((came, fixed))
    linked = kept[:, rows:] + came[:, rows:]
    straight, slanted = along(linked), along(linked, 1)
    own, link = call(
        pair_sum_kernel,
        (shape((3, rows, LANES), f32), shape((6,) + tile, f32)),
        [pltpu.VMEM((1,) + tile, i32), pltpu.VMEM((3, rows, LANES), f32)],
        0,
        (fixed, kept, came),
    )
    came = beside(link)
    straight, slanted, _ = lax.optimization_barrier((straight, slanted, link))
    mine = call(
        pair_join_kernel, shape((3,) + tile, f32), [], 0, (straight, slanted)
    )
    other = across(mine)
    weighted, outbound = call(
        functools.partial(pair_owner_kernel, dom_count),
        (shape((3, rows, LANES), f32), shape((3,) + tile, f32)),
        [
            pltpu.VMEM((2, 3 * PARTS * owned_high, link_slots), f32),
            pltpu.VMEM((2,) + tile, i32),
            pltpu.VMEM((3, 2 * rows, LANES), f32),
        ],
        0,
        (own, link, mine, other, came, obs),
    )
    mine = along(outbound)
    inner = call(
        pair_near_kernel,
        shape(tile, f32),
        [pltpu.VMEM((30,) + tile, f32), pltpu.VMEM((3, 16, LANES), f32)],
        0,
        (weighted, outbound, index, coupled),
    )
    mine, inner = lax.optimization_barrier((mine, inner))
    other = across(mine)
    hess, sums, vectors = call(
        functools.partial(pair_adjoint_kernel, dom_count, rows),
        (
            shape(tile, f32),
            shape((4 * dom_count, SUMS, LANES), f32),
            shape((3,) + tile, f32),
        ),
        [pltpu.VMEM((3, 16, LANES), f32), pltpu.VMEM((30,) + tile, f32)],
        0,
        (inner, mine, other, outbound, index, coupled, marks, residual, iterate, reg),
    )
    return hess, sums, vectors


def general_step(
    background, obs, connect, live_blocks, scale, others, send_nodes, counts, ref_stiff
):
    f32, i32 = jnp.float32, jnp.int32
    shape = jax.ShapeDtypeStruct
    dom_count = lax.axis_size("dom")
    sub_count = lax.axis_size("sub")
    field_count = lax.axis_size("field")
    owned_nodes = background.shape[1]
    link_slots = send_nodes.shape[3]
    halves = link_slots // LANES
    width = link_slots
    owned_high = owned_nodes // width
    owned_rows = owned_nodes // LANES
    ghost_rows = 3 * sub_count * halves
    table_rows = owned_rows + ghost_rows
    partitions = dom_count * sub_count
    devices = partitions * field_count
    chunk = up_to(3 * halves, SUBS)
    link_tiles = up_to(ghost_rows, SUBS) // SUBS
    left_rows = 3 * PARTS * owned_high + up_to(3 * PARTS * up_to(3 * sub_count, SUBS), 16)
    dims = (dom_count, sub_count, halves)
    links = ("dom", "sub")
    cores = ("dom", "sub", "field")

    outbound = pl.pallas_call(
        functools.partial(start_kernel, dims),
        out_shape=shape((partitions, chunk, LANES), f32),
        in_specs=[SMEM, VMEM, VMEM],
        out_specs=VMEM,
        scratch_shapes=[
            pltpu.VMEM((link_tiles, SUBS, LANES), i32),
            pltpu.VMEM((3, link_tiles, SUBS, LANES), f32),
            pltpu.VMEM((3, owned_rows, LANES), f32),
        ],
    )(counts, send_nodes, background)
    arrived = lax.all_to_all(outbound, links, 0, 0, tiled=True)

    coupled, vectors, owned, outbound = pl.pallas_call(
        functools.partial(forward_kernel, dims),
        compiler_params=PARAMS,
        out_shape=(
            shape((30, SUBS, LANES), f32),
            shape((5, SUBS, LANES), f32),
            shape((3, owned_high, width), f32),
            shape((devices, chunk, LANES), f32),
        ),
        in_specs=[SMEM, SMEM] + [VMEM] * 8,
        out_specs=(VMEM,) * 4,
        scratch_shapes=[
            pltpu.VMEM((3, table_rows, LANES), f32),
            pltpu.VMEM((10, SUBS, LANES), i32),
            pltpu.VMEM((30, SUBS, LANES), f32),
            pltpu.VMEM((3 * PARTS, 10, SUBS, LANES), f32),
            pltpu.VMEM((left_rows, width), f32),
        ],
    )(
        live_blocks,
        ref_stiff,
        background,
        arrived,
        connect,
        scale,
        *others,
    )
    swapped = lax.ppermute(
        owned, "field", [(i, (i + 1) % field_count) for i in range(field_count)]
    )
    arrived = lax.all_to_all(outbound, cores, 0, 0, tiled=True)

    weighted, outbound = pl.pallas_call(
        functools.partial(owner_kernel, dims),
        compiler_params=PARAMS,
        out_shape=(
            shape((3, owned_rows, LANES), f32),
            shape((partitions, chunk, LANES), f32),
        ),
        in_specs=[SMEM] + [VMEM] * 5,
        out_specs=(VMEM,) * 2,
        scratch_shapes=[
            pltpu.VMEM((link_tiles, SUBS, LANES), i32),
            pltpu.VMEM((3, link_tiles, SUBS, LANES), f32),
        ],
    )(counts, send_nodes, owned, swapped, arrived, obs)
    arrived = lax.all_to_all(outbound, links, 0, 0, tiled=True)

    hess, sums = pl.pallas_call(
        functools.partial(adjoint_kernel, dims),
        compiler_params=PARAMS,
        out_shape=(shape((SUBS, LANES), f32), shape((devices, SUMS, LANES), f32)),
        in_specs=[VMEM] * 5,
        out_specs=(VMEM,) * 2,
        scratch_shapes=[
            pltpu.VMEM((3, table_rows, LANES), f32),
            pltpu.VMEM((10, SUBS, LANES), i32),
            pltpu.VMEM((10, 3, SUBS, LANES), f32),
        ],
    )(weighted, arrived, connect, coupled, vectors)
    return hess, sums, vectors


def on_device(
    background,
    obs_weight,
    connect,
    live_blocks,
    elem_scale,
    reg_weight,
    iterate,
    residual,
    direction,
    send_nodes,
    send_count,
    ref_stiff,
):
    f32 = jnp.float32
    shape = jax.ShapeDtypeStruct
    tiled = lambda x: x.reshape(-1, LANES)
    scale, reg, guess, remain, search = map(
        tiled, (elem_scale, reg_weight, iterate, residual, direction)
    )
    obs = tiled(obs_weight)
    counts = jnp.swapaxes(send_count, 1, 2)
    two = lax.axis_size("sub") == 2 and lax.axis_size("field") == 2
    paired = two and send_nodes.shape[3] == 2 * LANES
    hess, sums, vectors = (pair_step if paired else general_step)(
        background,
        obs,
        connect,
        live_blocks,
        scale,
        (search, remain, guess, reg),
        send_nodes,
        counts,
        ref_stiff,
    )
    cores = ("dom", "sub", "field")
    sums = lax.all_to_all(sums, cores, 0, 0, tiled=True)

    results = pl.pallas_call(
        update_kernel,
        compiler_params=PARAMS,
        out_shape=(shape((SUBS, LANES), f32),) * 3,
        in_specs=[VMEM] * 3,
        out_specs=(VMEM,) * 3,
    )(sums, hess, vectors)
    return tuple(x.reshape(-1) for x in results)


def solution(mesh):
    placed = (
        P(None, ("groups", "dom", "sub")),
        P(("groups", "dom", "sub")),
        P(None, ("groups", "dom", "sub", "field")),
        P(("groups", "dom", "sub", "field")),
        P(("groups", "dom", "sub", "field")),
        P(("groups", "dom", "sub", "field")),
        P(("groups", "dom", "sub", "field")),
        P(("groups", "dom", "sub", "field")),
        P(("groups", "dom", "sub", "field")),
        P(("groups", "dom", "sub"), None, None, None),
        P(("groups", "dom", "sub"), None, None),
        P(),
    )
    return jax.shard_map(
        on_device,
        mesh=mesh,
        in_specs=placed,
        out_specs=(
            P(("groups", "dom", "sub", "field")),
            P(("groups", "dom", "sub", "field")),
            P(("groups", "dom", "sub", "field")),
        ),
        check_vma=False,
    )
```
